256 devices in a mesh: tm: 64 (over z, y, core), space: 4 (over x).
Axes of the slice: x: 4, y: 4, z: 8, core: 2. Of those that a mesh axis runs over, the one named last changes fastest.
Arguments:
- coarse_points: float32 [128, 2, 128, 1024], P('tm', None, 'space'), may hold values from -4 to 4
- coarse_decay: float32 [128, 2, 128, 1024], P('tm', None, 'space'), may hold values from 0 to 1, as said below
- diffusion: float32 [128, 1024], P('space'), may hold values from 0.2 to 0.22
- forcing: float32 [2, 128, 1024], P(None, 'space'), may hold values from -5 to 5
Outputs:
- updated: float32 [128, 2, 128, 1024], P('tm', None, 'space')
The draws below stay inside these ranges and needn't reach their ends.
Inputs may be any that keep to these rules, and one draw needn't show every extreme that they name: `coarse_decay`: 0 to 1 for every interval, cell and component.
All inputs are finite; a program needn't handle non-finite values.
Results may differ from the reference program's by a relative error of at most 0.00002.
Values sent between devices are 32-bit elements; how exact they have to be, the bound alone decides.
A program may use at most 128 MiB of HBM per device.

```python
import math
import jax
import jax.numpy as jnp
from jax import lax

NY = 1024
M = 16
NX = 128
COARSE_INTERVALS = 128


def draw_coarse_points(key, part):
    child_key_list = jax.random.split(jax.random.fold_in(key, 11), 3)
    comp_shape = (COARSE_INTERVALS, 1, NX, NY)
    heading = jnp.where(jax.random.uniform(child_key_list[0], ()) < 0.5, -1.0, 1.0)
    along_speed = jax.random.uniform(child_key_list[1], comp_shape, minval=2.0, maxval=3.8)
    cross_speed = jnp.clip(1.2 * jax.random.normal(child_key_list[2], comp_shape), -3.8, 3.8)
    return jnp.concatenate([heading * along_speed, cross_speed], axis=1).astype(jnp.float32)


def draw_coarse_decay(key, part):
    child_key_list = jax.random.split(jax.random.fold_in(key, 7), 6)
    grid_shape = (COARSE_INTERVALS, 2, NX, NY)
    slow_share = 0.5
    is_slow = jax.random.uniform(child_key_list[0], (1, 2, NX, NY)) < slow_share
    slow_rate = jnp.exp(jax.random.uniform(child_key_list[1], grid_shape, minval=math.log(0.1), maxval=math.log(1.0))) / COARSE_INTERVALS
    fast_rate = jnp.exp(jax.random.uniform(child_key_list[3], grid_shape, minval=math.log(0.05), maxval=math.log(2.0)))
    damping_speed = jnp.where(is_slow, slow_rate, fast_rate)
    spike_location = jax.random.randint(child_key_list[4], (2,), 0, COARSE_INTERVALS)
    spike_magnitude = jax.random.uniform(child_key_list[5], (COARSE_INTERVALS, 1, 1, 1), minval=0.6, maxval=0.8)
    spike_triggered = jnp.any(jnp.arange(COARSE_INTERVALS)[:, None] == spike_location[None, :], axis=1)
    spike_multiplier = jnp.where(spike_triggered[:, None, None, None], spike_magnitude, 1.0)
    return (jnp.exp(-damping_speed) * spike_multiplier).astype(jnp.float32)


def block_scale(stream_key, dims, cuts, smallest, top_value):
    loudness, own = 1.0, jax.random.fold_in(stream_key, 6)
    for dim, blocks in cuts:
        draws = jnp.exp(jax.random.uniform(jax.random.fold_in(own, dim), (blocks,), jnp.float32, smallest / len(cuts), top_value / len(cuts)))
        loudness = loudness * jnp.repeat(draws, dims[dim] // blocks).reshape([-1 if axis == dim else 1 for axis in range(len(dims))])
    return loudness


def normal_values(rng, extent, spread, limit, cuts=(), held_as=jnp.bfloat16):
    array = spread * jax.random.normal(rng, extent, jnp.float32)
    if cuts:
        array = array * block_scale(rng, extent, cuts, -0.22, 0.18)
    return jnp.clip(array, -limit, limit).astype(held_as)


def setup_inputs(seed: int = 0) -> dict:
    streams_of = jax.random.split(jax.random.key(seed), 5)
    return {
        "coarse_points": draw_coarse_points(jax.random.fold_in(streams_of[4], 71), 0),
        "coarse_decay": draw_coarse_decay(jax.random.fold_in(streams_of[4], 71), 0),
        "diffusion": jnp.clip(0.2 + 0.019999996 * jax.random.uniform(streams_of[2], (NX, NY), jnp.float32) ** block_scale(streams_of[2], (NX, NY), ((0, 4),), -0.2, 0.2), 0.2, 0.22),
        "forcing": normal_values(streams_of[3], (2, NX, NY), 1.0, 5.0, ((1, 4),), jnp.float32),
    }


def advance(field_state, diffusion, forcing):
    padded = jnp.pad(field_state, ((0, 0), (1, 1), (0, 0)))
    centre = field_state
    next_row = padded[:, 2:]
    prev_row = padded[:, :-2]
    next_col = jnp.roll(centre, -1, axis=2)
    prev_col = jnp.roll(centre, 1, axis=2)
    speed_x = centre[0:1]
    speed_y = centre[1:2]
    return centre + diffusion * (next_row + prev_row + next_col + prev_col - 4.0 * centre) - 0.05 * (speed_x * (next_row - prev_row) + speed_y * (next_col - prev_col)) + 0.05 * forcing


def reference(coarse_points, coarse_decay, diffusion, forcing):
    def one_step(counter, field_state):
        return advance(field_state, diffusion, forcing)

    def interval(current, inputs):
        start_state, decay_step = inputs
        fine_end = lax.fori_loop(0, M, one_step, start_state)
        defect = fine_end - decay_step * start_state
        advanced = decay_step * current + defect
        return advanced, advanced

    final_state, updated = lax.scan(interval, coarse_points[0], (coarse_points, coarse_decay))
    return updated
```

```python
import jax
import jax.numpy as jnp
from jax import lax
from jax.experimental import pallas as pl
from jax.experimental.pallas import tpu as pltpu
from jax.sharding import PartitionSpec as P

M = 16
HALO = M


def fine_kernel(st_ref, dif_ref, frc_ref, keep_ref, out_ref, buf):
    rows = st_ref.shape[1]
    cols = st_ref.shape[2]
    buf[...] = st_ref[...]
    dif = dif_ref[...]
    keep = keep_ref[...] > 0.5

    def one_step(counter, carry):
        for slot in range(2):
            u = buf[2 * slot]
            v = buf[2 * slot + 1]
            new = []
            for comp, c in enumerate((u, v)):
                next_row = pltpu.roll(c, rows - 1, 0)
                prev_row = pltpu.roll(c, 1, 0)
                next_col = pltpu.roll(c, cols - 1, 1)
                prev_col = pltpu.roll(c, 1, 1)
                value = (
                    c
                    + dif * (next_row + prev_row + next_col + prev_col - 4.0 * c)
                    - 0.05 * (u * (next_row - prev_row) + v * (next_col - prev_col))
                    + 0.05 * frc_ref[comp]
                )
                new.append(jnp.where(keep, value, 0.0))
            buf[2 * slot] = new[0]
            buf[2 * slot + 1] = new[1]
        return carry

    lax.fori_loop(0, M, one_step, 0)
    out_ref[...] = buf[:, HALO:rows - HALO, :]


def scan_kernel(a_ref, b_ref, x_ref):
    x = jnp.zeros(a_ref.shape[1:], jnp.float32)
    for s in range(a_ref.shape[0]):
        x_ref[s] = x
        x = a_ref[s] * x + b_ref[s]


def to_tiles(block):
    rows, cols = block.shape[-2] * block.shape[-3], block.shape[-1]
    flat = block.reshape(rows // 8, 8, cols // 128, 128)
    return flat.transpose(0, 2, 1, 3).reshape(-1, 8, 128)


def from_tiles(tiles, shape):
    rows, cols = shape[0] * shape[1], shape[2]
    grid = tiles.reshape(rows // 8, cols // 128, 8, 128)
    return grid.transpose(0, 2, 1, 3).reshape(shape)


def per_device(coarse_points, coarse_decay, diffusion, forcing):
    slots, comps, row_count, col_count = coarse_points.shape
    space_count = lax.axis_size("space")
    tm_count = lax.axis_size("tm")
    me = lax.axis_index("space")

    state = coarse_points.reshape(slots * comps, row_count, col_count)
    pack = jnp.concatenate([state, diffusion[None], forcing], axis=0)
    forward = [(i, i + 1) for i in range(space_count - 1)]
    backward = [(i + 1, i) for i in range(space_count - 1)]
    above = lax.ppermute(pack[:, row_count - HALO:], "space", forward)
    below = lax.ppermute(pack[:, :HALO], "space", backward)
    ext = jnp.concatenate([above, pack, below], axis=1)
    ext_rows = row_count + 2 * HALO
    global_row = me * row_count - HALO + lax.broadcasted_iota(jnp.int32, (ext_rows, 1), 0)
    keep = ((global_row >= 0) & (global_row < space_count * row_count)).astype(jnp.float32)

    fine_end = pl.pallas_call(
        fine_kernel,
        out_shape=jax.ShapeDtypeStruct((slots * comps, row_count, col_count), jnp.float32),
        scratch_shapes=[pltpu.VMEM((slots * comps, ext_rows, col_count), jnp.float32)],
    )(ext[: slots * comps], ext[slots * comps], ext[slots * comps + 1:], keep)
    fine_end = fine_end.reshape(coarse_points.shape)

    shift = fine_end - coarse_decay * coarse_points
    scale = coarse_decay
    at_anchor = lax.axis_index("tm") == 0
    shift0 = jnp.where(at_anchor, coarse_decay[0] * coarse_points[0] + shift[0], shift[0])
    scale0 = jnp.where(at_anchor, 0.0, scale[0])
    comp_scale = scale[1] * scale0
    comp_shift = scale[1] * shift0 + shift[1]

    both = jnp.stack([to_tiles(comp_scale), to_tiles(comp_shift)])
    got = lax.all_to_all(both, "tm", split_axis=1, concat_axis=1, tiled=True)
    per_src = got.shape[1] // tm_count
    got = got.reshape(2, tm_count, per_src, 8, 128)
    prefix = pl.pallas_call(
        scan_kernel,
        out_shape=jax.ShapeDtypeStruct((tm_count, per_src, 8, 128), jnp.float32),
    )(got[0], got[1])
    back = lax.all_to_all(
        prefix.reshape(tm_count * per_src, 8, 128), "tm", split_axis=0, concat_axis=0, tiled=True
    )
    entering = from_tiles(back, (comps, row_count, col_count))

    first = scale0 * entering + shift0
    second = scale[1] * first + shift[1]
    return jnp.stack([first, second], axis=0)


def solution(mesh):
    placed = (
        P("tm", None, "space", None),
        P("tm", None, "space", None),
        P("space", None),
        P(None, "space", None),
    )
    return jax.shard_map(
        per_device,
        mesh=mesh,
        in_specs=placed,
        out_specs=P("tm", None, "space", None),
        check_vma=False,
    )
```

```python
import jax
import jax.numpy as jnp
from jax import lax
from jax.experimental import pallas as pl
from jax.experimental.pallas import tpu as pltpu
from jax.sharding import PartitionSpec as P

M = 16
HALO = M


def fine_kernel(st_ref, dif_ref, frc_ref, up_ref, dn_ref, keep_ref, order_ref, out_ref, buf, dbuf, fbuf):
    n_state = st_ref.shape[0]
    own = st_ref.shape[1]
    cols = st_ref.shape[2]
    rows = own + 2 * HALO
    buf[:, :HALO] = up_ref[:n_state]
    buf[:, HALO:HALO + own] = st_ref[...]
    buf[:, HALO + own:] = dn_ref[:n_state]
    dbuf[:HALO] = up_ref[n_state]
    dbuf[HALO:HALO + own] = dif_ref[...]
    dbuf[HALO + own:] = dn_ref[n_state]
    fbuf[:, :HALO] = up_ref[n_state + 1:]
    fbuf[:, HALO:HALO + own] = frc_ref[...]
    fbuf[:, HALO + own:] = dn_ref[n_state + 1:]

    def make_step(lo, hi):
        span = hi - lo

        def one_step(counter, carry):
            dif = dbuf[lo:hi]
            keep = keep_ref[lo:hi] > 0.5
            for slot in range(2):
                u = buf[2 * slot, lo:hi]
                v = buf[2 * slot + 1, lo:hi]
                new = []
                for comp, c in enumerate((u, v)):
                    next_row = pltpu.roll(c, span - 1, 0)
                    prev_row = pltpu.roll(c, 1, 0)
                    next_col = pltpu.roll(c, cols - 1, 1)
                    prev_col = pltpu.roll(c, 1, 1)
                    value = (
                        c
                        + dif * (next_row + prev_row + next_col + prev_col - 4.0 * c)
                        - 0.05 * (u * (next_row - prev_row) + v * (next_col - prev_col))
                        + 0.05 * fbuf[comp, lo:hi]
                    )
                    new.append(jnp.where(keep, value, 0.0))
                buf[2 * slot, lo:hi] = new[0]
                buf[2 * slot + 1, lo:hi] = new[1]
            return carry

        return one_step

    half = M // 2
    lax.fori_loop(0, half, make_step(0, rows), 0)
    lax.fori_loop(0, M - half, make_step(half, rows - half), 0)
    out_ref[...] = buf[:, HALO:HALO + own, :]


def scan_kernel(a_ref, b_ref, x_ref):
    x = jnp.zeros(a_ref.shape[1:], jnp.float32)
    for s in range(a_ref.shape[0]):
        x_ref[s] = x
        x = a_ref[s] * x + b_ref[s]


def to_tiles(block):
    rows, cols = block.shape[-2] * block.shape[-3], block.shape[-1]
    flat = block.reshape(rows // 8, 8, cols // 128, 128)
    return flat.transpose(0, 2, 1, 3).reshape(-1, 8, 128)


def from_tiles(tiles, shape):
    rows, cols = shape[0] * shape[1], shape[2]
    grid = tiles.reshape(rows // 8, cols // 128, 8, 128)
    return grid.transpose(0, 2, 1, 3).reshape(shape)


def per_device_body(coarse_points, coarse_decay, diffusion, forcing):
    slots, comps, row_count, col_count = coarse_points.shape
    space_count = lax.axis_size("space")
    tm_count = lax.axis_size("tm")
    me = lax.axis_index("space")

    at_anchor = lax.axis_index("tm") == 0
    scale0 = jnp.where(at_anchor, 0.0, coarse_decay[0])
    comp_scale = coarse_decay[1] * scale0
    scale_tiles = to_tiles(comp_scale)
    got_scale = lax.all_to_all(scale_tiles, "tm", split_axis=0, concat_axis=0, tiled=True)

    state = coarse_points.reshape(slots * comps, row_count, col_count)
    forward = [(i, i + 1) for i in range(space_count - 1)]
    backward = [(i + 1, i) for i in range(space_count - 1)]

    def rim(lo, hi):
        return jnp.concatenate([state[:, lo:hi], diffusion[None, lo:hi], forcing[:, lo:hi]], axis=0)

    up_rim = rim(row_count - HALO, row_count)
    dn_rim = rim(0, HALO)
    above = lax.ppermute(up_rim, "space", forward)
    below = lax.ppermute(dn_rim, "space", backward)
    ext_rows = row_count + 2 * HALO
    global_row = me * row_count - HALO + lax.broadcasted_iota(jnp.int32, (ext_rows, 1), 0)
    keep = ((global_row >= 0) & (global_row < space_count * row_count)).astype(jnp.float32)

    vmem = pl.BlockSpec(memory_space=pltpu.VMEM)
    fine_end = pl.pallas_call(
        fine_kernel,
        out_shape=jax.ShapeDtypeStruct((slots * comps, row_count, col_count), jnp.float32),
        in_specs=[vmem] * 6 + [pl.BlockSpec(memory_space=pl.ANY)],
        out_specs=vmem,
        scratch_shapes=[
            pltpu.VMEM((slots * comps, ext_rows, col_count), jnp.float32),
            pltpu.VMEM((ext_rows, col_count), jnp.float32),
            pltpu.VMEM((comps, ext_rows, col_count), jnp.float32),
        ],
    )(state, diffusion, forcing, above, below, keep, got_scale)
    fine_end = fine_end.reshape(coarse_points.shape)

    shift = fine_end - coarse_decay * coarse_points
    scale = coarse_decay
    shift0 = jnp.where(at_anchor, coarse_decay[0] * coarse_points[0] + shift[0], shift[0])
    comp_shift = scale[1] * shift0 + shift[1]

    got_shift = lax.all_to_all(to_tiles(comp_shift), "tm", split_axis=0, concat_axis=0, tiled=True)
    per_src = got_shift.shape[0] // tm_count
    tile_shape = (tm_count, per_src, 8, 128)
    prefix = pl.pallas_call(
        scan_kernel,
        out_shape=jax.ShapeDtypeStruct(tile_shape, jnp.float32),
    )(got_scale.reshape(tile_shape), got_shift.reshape(tile_shape))
    back = lax.all_to_all(
        prefix.reshape(tm_count * per_src, 8, 128), "tm", split_axis=0, concat_axis=0, tiled=True
    )
    entering = from_tiles(back, (comps, row_count, col_count))

    first = scale0 * entering + shift0
    second = scale[1] * first + shift[1]
    return jnp.stack([first, second], axis=0)


def solution(mesh):
    placed = (
        P("tm", None, "space", None),
        P("tm", None, "space", None),
        P("space", None),
        P(None, "space", None),
    )
    return jax.shard_map(
        per_device_body,
        mesh=mesh,
        in_specs=placed,
        out_specs=P("tm", None, "space", None),
        check_vma=False,
    )
```

```python
import jax
import jax.numpy as jnp
from jax import lax
from jax.experimental import pallas as pl
from jax.experimental.pallas import tpu as pltpu
from jax.sharding import PartitionSpec as P

M = 16
HALO = M


def fine_kernel(st_ref, dif_ref, frc_ref, up_ref, dn_ref, keep_ref, out_ref, buf, dbuf, fbuf):
    n_state = st_ref.shape[0]
    own = st_ref.shape[1]
    cols = st_ref.shape[2]
    rows = own + 2 * HALO
    buf[:, :HALO] = up_ref[:n_state]
    buf[:, HALO:HALO + own] = st_ref[...]
    buf[:, HALO + own:] = dn_ref[:n_state]
    dbuf[:HALO] = up_ref[n_state]
    dbuf[HALO:HALO + own] = dif_ref[...]
    dbuf[HALO + own:] = dn_ref[n_state]
    fbuf[:, :HALO] = up_ref[n_state + 1:]
    fbuf[:, HALO:HALO + own] = frc_ref[...]
    fbuf[:, HALO + own:] = dn_ref[n_state + 1:]

    def make_step(lo, hi):
        span = hi - lo

        def one_step(counter, carry):
            dif = dbuf[lo:hi]
            keep = keep_ref[lo:hi] > 0.5
            for slot in range(2):
                u = buf[2 * slot, lo:hi]
                v = buf[2 * slot + 1, lo:hi]
                new = []
                for comp, c in enumerate((u, v)):
                    next_row = pltpu.roll(c, span - 1, 0)
                    prev_row = pltpu.roll(c, 1, 0)
                    next_col = pltpu.roll(c, cols - 1, 1)
                    prev_col = pltpu.roll(c, 1, 1)
                    value = (
                        c
                        + dif * (next_row + prev_row + next_col + prev_col - 4.0 * c)
                        - 0.05 * (u * (next_row - prev_row) + v * (next_col - prev_col))
                        + 0.05 * fbuf[comp, lo:hi]
                    )
                    new.append(jnp.where(keep, value, 0.0))
                buf[2 * slot, lo:hi] = new[0]
                buf[2 * slot + 1, lo:hi] = new[1]
            return carry

        return one_step

    half = M // 2
    lax.fori_loop(0, half, make_step(0, rows), 0)
    lax.fori_loop(0, M - half, make_step(half, rows - half), 0)
    out_ref[...] = buf[:, HALO:HALO + own, :]


def scan_kernel(a_ref, b_ref, x_ref):
    x = jnp.zeros(a_ref.shape[1:], jnp.float32)
    for s in range(a_ref.shape[0]):
        x_ref[s] = x
        x = a_ref[s] * x + b_ref[s]


def to_tiles(block):
    rows, cols = block.shape[-2] * block.shape[-3], block.shape[-1]
    flat = block.reshape(rows // 8, 8, cols // 128, 128)
    return flat.transpose(0, 2, 1, 3).reshape(-1, 8, 128)


def from_tiles(tiles, shape):
    rows, cols = shape[0] * shape[1], shape[2]
    grid = tiles.reshape(rows // 8, cols // 128, 8, 128)
    return grid.transpose(0, 2, 1, 3).reshape(shape)


def per_device_body(coarse_points, coarse_decay, diffusion, forcing):
    slots, comps, row_count, col_count = coarse_points.shape
    space_count = lax.axis_size("space")
    tm_count = lax.axis_size("tm")
    me = lax.axis_index("space")

    at_anchor = lax.axis_index("tm") == 0
    scale0 = jnp.where(at_anchor, 0.0, coarse_decay[0])
    comp_scale = coarse_decay[1] * scale0

    state = coarse_points.reshape(slots * comps, row_count, col_count)
    forward = [(i, i + 1) for i in range(space_count - 1)]
    backward = [(i + 1, i) for i in range(space_count - 1)]

    def rim(lo, hi):
        return jnp.concatenate([state[:, lo:hi], diffusion[None, lo:hi], forcing[:, lo:hi]], axis=0)

    up_rim = rim(row_count - HALO, row_count)
    dn_rim = rim(0, HALO)
    above = lax.ppermute(up_rim, "space", forward)
    below = lax.ppermute(dn_rim, "space", backward)
    ext_rows = row_count + 2 * HALO
    global_row = me * row_count - HALO + lax.broadcasted_iota(jnp.int32, (ext_rows, 1), 0)
    keep = ((global_row >= 0) & (global_row < space_count * row_count)).astype(jnp.float32)

    vmem = pl.BlockSpec(memory_space=pltpu.VMEM)
    fine_end = pl.pallas_call(
        fine_kernel,
        out_shape=jax.ShapeDtypeStruct((slots * comps, row_count, col_count), jnp.float32),
        in_specs=[vmem] * 6,
        out_specs=vmem,
        scratch_shapes=[
            pltpu.VMEM((slots * comps, ext_rows, col_count), jnp.float32),
            pltpu.VMEM((ext_rows, col_count), jnp.float32),
            pltpu.VMEM((comps, ext_rows, col_count), jnp.float32),
        ],
    )(state, diffusion, forcing, above, below, keep)
    fine_end = fine_end.reshape(coarse_points.shape)

    shift = fine_end - coarse_decay * coarse_points
    scale = coarse_decay
    shift0 = jnp.where(at_anchor, coarse_decay[0] * coarse_points[0] + shift[0], shift[0])
    comp_shift = scale[1] * shift0 + shift[1]

    both = jnp.stack([to_tiles(comp_scale), to_tiles(comp_shift)])
    got = lax.all_to_all(both, "tm", split_axis=1, concat_axis=1, tiled=True)
    got_scale, got_shift = got[0], got[1]
    per_src = got_shift.shape[0] // tm_count
    tile_shape = (tm_count, per_src, 8, 128)
    prefix = pl.pallas_call(
        scan_kernel,
        out_shape=jax.ShapeDtypeStruct(tile_shape, jnp.float32),
    )(got_scale.reshape(tile_shape), got_shift.reshape(tile_shape))
    back = lax.all_to_all(
        prefix.reshape(tm_count * per_src, 8, 128), "tm", split_axis=0, concat_axis=0, tiled=True
    )
    entering = from_tiles(back, (comps, row_count, col_count))

    first = scale0 * entering + shift0
    second = scale[1] * first + shift[1]
    return jnp.stack([first, second], axis=0)


def solution(mesh):
    placed = (
        P("tm", None, "space", None),
        P("tm", None, "space", None),
        P("space", None),
        P(None, "space", None),
    )
    return jax.shard_map(
        per_device_body,
        mesh=mesh,
        in_specs=placed,
        out_specs=P("tm", None, "space", None),
        check_vma=False,
    )
```

```python
import jax
import jax.numpy as jnp
from jax import lax
from jax.experimental import pallas as pl
from jax.experimental.pallas import tpu as pltpu
from jax.sharding import PartitionSpec as P

M = 16
HALO = M


def fine_kernel(st_ref, dif_ref, frc_ref, up_ref, dn_ref, keep_ref, out_ref, buf, dbuf, fbuf):
    n_state = st_ref.shape[0]
    own = st_ref.shape[1]
    cols = st_ref.shape[2]
    rows = own + 2 * HALO
    buf[:, :HALO] = up_ref[:n_state]
    buf[:, HALO:HALO + own] = st_ref[...]
    buf[:, HALO + own:] = dn_ref[:n_state]
    dbuf[:HALO] = up_ref[n_state]
    dbuf[HALO:HALO + own] = dif_ref[...]
    dbuf[HALO + own:] = dn_ref[n_state]
    fbuf[:, :HALO] = up_ref[n_state + 1:]
    fbuf[:, HALO:HALO + own] = frc_ref[...]
    fbuf[:, HALO + own:] = dn_ref[n_state + 1:]

    def make_step(lo, hi):
        span = hi - lo

        def one_step(counter, carry):
            dif = dbuf[lo:hi]
            keep = keep_ref[lo:hi] > 0.5
            for slot in range(2):
                u = buf[2 * slot, lo:hi]
                v = buf[2 * slot + 1, lo:hi]
                new = []
                for comp, c in enumerate((u, v)):
                    next_row = pltpu.roll(c, span - 1, 0)
                    prev_row = pltpu.roll(c, 1, 0)
                    next_col = pltpu.roll(c, cols - 1, 1)
                    prev_col = pltpu.roll(c, 1, 1)
                    value = (
                        c
                        + dif * (next_row + prev_row + next_col + prev_col - 4.0 * c)
                        - 0.05 * (u * (next_row - prev_row) + v * (next_col - prev_col))
                        + 0.05 * fbuf[comp, lo:hi]
                    )
                    new.append(jnp.where(keep, value, 0.0))
                buf[2 * slot, lo:hi] = new[0]
                buf[2 * slot + 1, lo:hi] = new[1]
            return carry

        return one_step

    half = M // 2
    lax.fori_loop(0, half, make_step(0, rows), 0)
    lax.fori_loop(0, M - half, make_step(half, rows - half), 0)
    out_ref[...] = buf[:, HALO:HALO + own, :]


def scan_kernel(a_ref, b_ref, x_ref):
    x = jnp.zeros(a_ref.shape[1:], jnp.float32)
    for s in range(a_ref.shape[0]):
        x_ref[s] = x
        x = a_ref[s] * x + b_ref[s]


def group_kernel(a_ref, b_ref, pa_ref, pb_ref, ga_ref, gb_ref):
    pa = jnp.ones(a_ref.shape[1:], jnp.float32)
    pb = jnp.zeros(a_ref.shape[1:], jnp.float32)
    for s in range(a_ref.shape[0]):
        pa_ref[s] = pa
        pb_ref[s] = pb
        a = a_ref[s]
        pa = a * pa
        pb = a * pb + b_ref[s]
    ga_ref[...] = pa
    gb_ref[...] = pb


def to_tiles(block):
    rows, cols = block.shape[-2] * block.shape[-3], block.shape[-1]
    flat = block.reshape(rows // 8, 8, cols // 128, 128)
    return flat.transpose(0, 2, 1, 3).reshape(-1, 8, 128)


def from_tiles(tiles, shape):
    rows, cols = shape[0] * shape[1], shape[2]
    grid = tiles.reshape(rows // 8, cols // 128, 8, 128)
    return grid.transpose(0, 2, 1, 3).reshape(shape)


def per_device_body(coarse_points, coarse_decay, diffusion, forcing):
    slots, comps, row_count, col_count = coarse_points.shape
    space_count = lax.axis_size("space")
    me = lax.axis_index("space")

    at_anchor = (lax.axis_index("tz") == 0) & (lax.axis_index("tq") == 0)
    scale0 = jnp.where(at_anchor, 0.0, coarse_decay[0])
    comp_scale = coarse_decay[1] * scale0

    state = coarse_points.reshape(slots * comps, row_count, col_count)
    forward = [(i, i + 1) for i in range(space_count - 1)]
    backward = [(i + 1, i) for i in range(space_count - 1)]

    def rim(lo, hi):
        return jnp.concatenate([state[:, lo:hi], diffusion[None, lo:hi], forcing[:, lo:hi]], axis=0)

    up_rim = rim(row_count - HALO, row_count)
    dn_rim = rim(0, HALO)
    above = lax.ppermute(up_rim, "space", forward)
    below = lax.ppermute(dn_rim, "space", backward)
    ext_rows = row_count + 2 * HALO
    global_row = me * row_count - HALO + lax.broadcasted_iota(jnp.int32, (ext_rows, 1), 0)
    keep = ((global_row >= 0) & (global_row < space_count * row_count)).astype(jnp.float32)

    vmem = pl.BlockSpec(memory_space=pltpu.VMEM)
    fine_end = pl.pallas_call(
        fine_kernel,
        out_shape=jax.ShapeDtypeStruct((slots * comps, row_count, col_count), jnp.float32),
        in_specs=[vmem] * 6,
        out_specs=vmem,
        scratch_shapes=[
            pltpu.VMEM((slots * comps, ext_rows, col_count), jnp.float32),
            pltpu.VMEM((ext_rows, col_count), jnp.float32),
            pltpu.VMEM((comps, ext_rows, col_count), jnp.float32),
        ],
    )(state, diffusion, forcing, above, below, keep)
    fine_end = fine_end.reshape(coarse_points.shape)

    shift = fine_end - coarse_decay * coarse_points
    scale = coarse_decay
    shift0 = jnp.where(at_anchor, coarse_decay[0] * coarse_points[0] + shift[0], shift[0])
    comp_shift = scale[1] * shift0 + shift[1]

    q_count = lax.axis_size("tq")
    z_count = lax.axis_size("tz")
    both = jnp.stack([to_tiles(comp_scale), to_tiles(comp_shift)])
    tiles = both.shape[1]
    c1 = tiles // q_count
    c2 = c1 // z_count
    got = lax.all_to_all(both, "tq", split_axis=1, concat_axis=1, tiled=True)
    got = got.reshape(2, q_count, c1, 8, 128)
    shape1 = jax.ShapeDtypeStruct((q_count, c1, 8, 128), jnp.float32)
    shape_g = jax.ShapeDtypeStruct((c1, 8, 128), jnp.float32)
    pa, pb, ga, gb = pl.pallas_call(group_kernel, out_shape=(shape1, shape1, shape_g, shape_g))(
        got[0], got[1]
    )
    groups = lax.all_to_all(jnp.stack([ga, gb]), "tz", split_axis=1, concat_axis=1, tiled=True)
    groups = groups.reshape(2, z_count, c2, 8, 128)
    group_in = pl.pallas_call(
        scan_kernel,
        out_shape=jax.ShapeDtypeStruct((z_count, c2, 8, 128), jnp.float32),
    )(groups[0], groups[1])
    group_in = lax.all_to_all(
        group_in.reshape(c1, 8, 128), "tz", split_axis=0, concat_axis=0, tiled=True
    )
    prefix = pa * group_in[None] + pb
    back = lax.all_to_all(
        prefix.reshape(tiles, 8, 128), "tq", split_axis=0, concat_axis=0, tiled=True
    )
    entering = from_tiles(back, (comps, row_count, col_count))

    first = scale0 * entering + shift0
    second = scale[1] * first + shift[1]
    return jnp.stack([first, second], axis=0)


def solution(mesh):
    tm_count = mesh.shape["tm"]
    q_count = 8 if tm_count >= 16 and tm_count % 8 == 0 else 2
    grid = mesh.devices.reshape(tm_count // q_count, q_count, mesh.shape["space"])
    mesh = jax.sharding.Mesh(grid, ("tz", "tq", "space"))
    time_axes = ("tz", "tq")
    placed = (
        P(time_axes, None, "space", None),
        P(time_axes, None, "space", None),
        P("space", None),
        P(None, "space", None),
    )
    return jax.shard_map(
        per_device_body,
        mesh=mesh,
        in_specs=placed,
        out_specs=P(time_axes, None, "space", None),
        check_vma=False,
    )
```

```python
import jax
import jax.numpy as jnp
from jax import lax
from jax.experimental import pallas as pl
from jax.experimental.pallas import tpu as pltpu
from jax.sharding import PartitionSpec as P

M = 16
HALO = M


def fine_kernel(st_ref, dif_ref, frc_ref, up_ref, dn_ref, keep_ref, out_ref, buf, dbuf, fbuf):
    n_state = st_ref.shape[0]
    own = st_ref.shape[1]
    cols = st_ref.shape[2]
    rows = own + 2 * HALO
    buf[:, :HALO] = up_ref[:n_state]
    buf[:, HALO:HALO + own] = st_ref[...]
    buf[:, HALO + own:] = dn_ref[:n_state]
    dbuf[:HALO] = up_ref[n_state]
    dbuf[HALO:HALO + own] = dif_ref[...]
    dbuf[HALO + own:] = dn_ref[n_state]
    fbuf[:, :HALO] = up_ref[n_state + 1:]
    fbuf[:, HALO:HALO + own] = frc_ref[...]
    fbuf[:, HALO + own:] = dn_ref[n_state + 1:]

    def make_step(lo, hi):
        span = hi - lo

        def one_step(counter, carry):
            dif = dbuf[lo:hi]
            keep = keep_ref[lo:hi] > 0.5
            for slot in range(2):
                u = buf[2 * slot, lo:hi]
                v = buf[2 * slot + 1, lo:hi]
                new = []
                for comp, c in enumerate((u, v)):
                    next_row = pltpu.roll(c, span - 1, 0)
                    prev_row = pltpu.roll(c, 1, 0)
                    next_col = pltpu.roll(c, cols - 1, 1)
                    prev_col = pltpu.roll(c, 1, 1)
                    value = (
                        c
                        + dif * (next_row + prev_row + next_col + prev_col - 4.0 * c)
                        - 0.05 * (u * (next_row - prev_row) + v * (next_col - prev_col))
                        + 0.05 * fbuf[comp, lo:hi]
                    )
                    new.append(jnp.where(keep, value, 0.0))
                buf[2 * slot, lo:hi] = new[0]
                buf[2 * slot + 1, lo:hi] = new[1]
            return carry

        return one_step

    half = M // 2
    lax.fori_loop(0, half, make_step(0, rows), 0)
    lax.fori_loop(0, M - half, make_step(half, rows - half), 0)
    out_ref[...] = buf[:, HALO:HALO + own, :]


def exchange_kernel(send_ref, out_ref, recv, xbuf, back, s1, r1, s2, r2):
    n = send_ref.shape[0]
    me = lax.axis_index("tm")
    sp = lax.axis_index("space")
    mesh_id = pl.DeviceIdType.MESH

    def outgoing(d, src, dst, ssem, rsem):
        return pltpu.make_async_remote_copy(
            src_ref=src.at[d], dst_ref=dst.at[me], send_sem=ssem.at[d], recv_sem=rsem.at[me],
            device_id=(d, sp), device_id_type=mesh_id,
        )

    def incoming(e, src, dst, ssem, rsem):
        return pltpu.make_async_remote_copy(
            src_ref=src.at[e], dst_ref=dst.at[e], send_sem=ssem.at[e], recv_sem=rsem.at[e],
            device_id=(e, sp), device_id_type=mesh_id,
        )

    def peer(k):
        return lax.rem(me + k, n)

    def start1(k, carry):
        outgoing(peer(k), send_ref, recv, s1, r1).start()
        return carry

    lax.fori_loop(1, n, start1, 0)
    recv[me] = send_ref[me]

    def wait1(k, carry):
        outgoing(peer(k), send_ref, recv, s1, r1).wait_send()
        incoming(peer(k), send_ref, recv, s1, r1).wait_recv()
        return carry

    lax.fori_loop(1, n, wait1, 0)

    def scan_step(s, x):
        xbuf[s] = x
        return recv[s, :, 0] * x + recv[s, :, 1]

    lax.fori_loop(0, n, scan_step, jnp.zeros(xbuf.shape[1:], jnp.float32))

    def start2(k, carry):
        outgoing(peer(k), xbuf, back, s2, r2).start()
        return carry

    lax.fori_loop(1, n, start2, 0)
    back[me] = xbuf[me]

    def wait2(k, carry):
        outgoing(peer(k), xbuf, back, s2, r2).wait_send()
        incoming(peer(k), xbuf, back, s2, r2).wait_recv()
        return carry

    lax.fori_loop(1, n, wait2, 0)
    out_ref[...] = back[...]


def to_tiles(block):
    rows, cols = block.shape[-2] * block.shape[-3], block.shape[-1]
    flat = block.reshape(rows // 8, 8, cols // 128, 128)
    return flat.transpose(0, 2, 1, 3).reshape(-1, 8, 128)


def from_tiles(tiles, shape):
    rows, cols = shape[0] * shape[1], shape[2]
    grid = tiles.reshape(rows // 8, cols // 128, 8, 128)
    return grid.transpose(0, 2, 1, 3).reshape(shape)


def per_device_body(coarse_points, coarse_decay, diffusion, forcing):
    slots, comps, row_count, col_count = coarse_points.shape
    space_count = lax.axis_size("space")
    tm_count = lax.axis_size("tm")
    me = lax.axis_index("space")

    at_anchor = lax.axis_index("tm") == 0
    scale0 = jnp.where(at_anchor, 0.0, coarse_decay[0])
    comp_scale = coarse_decay[1] * scale0

    state = coarse_points.reshape(slots * comps, row_count, col_count)
    forward = [(i, i + 1) for i in range(space_count - 1)]
    backward = [(i + 1, i) for i in range(space_count - 1)]

    def rim(lo, hi):
        return jnp.concatenate([state[:, lo:hi], diffusion[None, lo:hi], forcing[:, lo:hi]], axis=0)

    up_rim = rim(row_count - HALO, row_count)
    dn_rim = rim(0, HALO)
    above = lax.ppermute(up_rim, "space", forward)
    below = lax.ppermute(dn_rim, "space", backward)
    ext_rows = row_count + 2 * HALO
    global_row = me * row_count - HALO + lax.broadcasted_iota(jnp.int32, (ext_rows, 1), 0)
    keep = ((global_row >= 0) & (global_row < space_count * row_count)).astype(jnp.float32)

    vmem = pl.BlockSpec(memory_space=pltpu.VMEM)
    fine_end = pl.pallas_call(
        fine_kernel,
        out_shape=jax.ShapeDtypeStruct((slots * comps, row_count, col_count), jnp.float32),
        in_specs=[vmem] * 6,
        out_specs=vmem,
        scratch_shapes=[
            pltpu.VMEM((slots * comps, ext_rows, col_count), jnp.float32),
            pltpu.VMEM((ext_rows, col_count), jnp.float32),
            pltpu.VMEM((comps, ext_rows, col_count), jnp.float32),
        ],
    )(state, diffusion, forcing, above, below, keep)
    fine_end = fine_end.reshape(coarse_points.shape)

    shift = fine_end - coarse_decay * coarse_points
    scale = coarse_decay
    shift0 = jnp.where(at_anchor, coarse_decay[0] * coarse_points[0] + shift[0], shift[0])
    comp_shift = scale[1] * shift0 + shift[1]

    both = jnp.stack([to_tiles(comp_scale), to_tiles(comp_shift)], axis=1)
    tiles = both.shape[0]
    chunk = tiles // tm_count
    both = both.reshape(tm_count, chunk, 2, 8, 128)
    x_shape = (tm_count, chunk, 8, 128)
    vmem = pl.BlockSpec(memory_space=pltpu.VMEM)
    back = pl.pallas_call(
        exchange_kernel,
        out_shape=jax.ShapeDtypeStruct(x_shape, jnp.float32),
        in_specs=[vmem],
        out_specs=vmem,
        scratch_shapes=[
            pltpu.VMEM(both.shape, jnp.float32),
            pltpu.VMEM(x_shape, jnp.float32),
            pltpu.VMEM(x_shape, jnp.float32),
            pltpu.SemaphoreType.DMA((tm_count,)),
            pltpu.SemaphoreType.DMA((tm_count,)),
            pltpu.SemaphoreType.DMA((tm_count,)),
            pltpu.SemaphoreType.DMA((tm_count,)),
        ],
        compiler_params=pltpu.CompilerParams(has_side_effects=True),
    )(both)
    back = back.reshape(tiles, 8, 128)
    entering = from_tiles(back, (comps, row_count, col_count))

    first = scale0 * entering + shift0
    second = scale[1] * first + shift[1]
    return jnp.stack([first, second], axis=0)


def solution(mesh):
    placed = (
        P("tm", None, "space", None),
        P("tm", None, "space", None),
        P("space", None),
        P(None, "space", None),
    )
    return jax.shard_map(
        per_device_body,
        mesh=mesh,
        in_specs=placed,
        out_specs=P("tm", None, "space", None),
        check_vma=False,
    )
```

```python
import jax
import jax.numpy as jnp
from jax import lax
from jax.experimental import pallas as pl
from jax.experimental.pallas import tpu as pltpu
from jax.sharding import PartitionSpec as P

M = 16
HALO = M


def fine_kernel(st_ref, dif_ref, frc_ref, up_ref, dn_ref, keep_ref, out_ref, buf, dbuf, fbuf):
    n_state = st_ref.shape[0]
    own = st_ref.shape[1]
    cols = st_ref.shape[2]
    rows = own + 2 * HALO
    buf[:, :HALO] = up_ref[:n_state]
    buf[:, HALO:HALO + own] = st_ref[...]
    buf[:, HALO + own:] = dn_ref[:n_state]
    dbuf[:HALO] = up_ref[n_state]
    dbuf[HALO:HALO + own] = dif_ref[...]
    dbuf[HALO + own:] = dn_ref[n_state]
    fbuf[:, :HALO] = up_ref[n_state + 1:]
    fbuf[:, HALO:HALO + own] = frc_ref[...]
    fbuf[:, HALO + own:] = dn_ref[n_state + 1:]

    def make_step(lo, hi):
        span = hi - lo

        def one_step(counter, carry):
            dif = dbuf[lo:hi]
            keep = keep_ref[lo:hi] > 0.5
            for slot in range(2):
                u = buf[2 * slot, lo:hi]
                v = buf[2 * slot + 1, lo:hi]
                new = []
                for comp, c in enumerate((u, v)):
                    next_row = pltpu.roll(c, span - 1, 0)
                    prev_row = pltpu.roll(c, 1, 0)
                    next_col = pltpu.roll(c, cols - 1, 1)
                    prev_col = pltpu.roll(c, 1, 1)
                    value = (
                        c
                        + dif * (next_row + prev_row + next_col + prev_col - 4.0 * c)
                        - 0.05 * (u * (next_row - prev_row) + v * (next_col - prev_col))
                        + 0.05 * fbuf[comp, lo:hi]
                    )
                    new.append(jnp.where(keep, value, 0.0))
                buf[2 * slot, lo:hi] = new[0]
                buf[2 * slot + 1, lo:hi] = new[1]
            return carry

        return one_step

    half = M // 2
    lax.fori_loop(0, half, make_step(0, rows), 0)
    lax.fori_loop(0, M - half, make_step(half, rows - half), 0)
    out_ref[...] = buf[:, HALO:HALO + own, :]


def exchange_kernel(send_ref, out_ref, recv1, pa, pb, gsend, recv2, xg, back2, xs, back1, sems):
    nq = send_ref.shape[0]
    nz = gsend.shape[0]
    mz = lax.axis_index("tz")
    mq = lax.axis_index("tq")
    sp = lax.axis_index("space")
    mesh_id = pl.DeviceIdType.MESH

    def exchange(phase, src, dst, n, me, where):
        ssem, rsem = sems.at[2 * phase], sems.at[2 * phase + 1]

        def outgoing(d):
            return pltpu.make_async_remote_copy(
                src_ref=src.at[d], dst_ref=dst.at[me], send_sem=ssem.at[d], recv_sem=rsem.at[me],
                device_id=where(d), device_id_type=mesh_id,
            )

        def incoming(e):
            return pltpu.make_async_remote_copy(
                src_ref=src.at[e], dst_ref=dst.at[e], send_sem=ssem.at[e], recv_sem=rsem.at[e],
                device_id=where(e), device_id_type=mesh_id,
            )

        def start(k, carry):
            outgoing(lax.rem(me + k, n)).start()
            return carry

        lax.fori_loop(1, n, start, 0)
        dst[me] = src[me]

        def wait(k, carry):
            d = lax.rem(me + k, n)
            outgoing(d).wait_send()
            incoming(d).wait_recv()
            return carry

        lax.fori_loop(1, n, wait, 0)

    in_plane = lambda d: (mz, d, sp)
    across = lambda d: (d, mq, sp)
    exchange(0, send_ref, recv1, nq, mq, in_plane)

    def group_step(s, carry):
        ga, gb = carry
        pa[s] = ga
        pb[s] = gb
        a = recv1[s, :, 0]
        return a * ga, a * gb + recv1[s, :, 1]

    ones = jnp.ones(pa.shape[1:], jnp.float32)
    ga, gb = lax.fori_loop(0, nq, group_step, (ones, jnp.zeros_like(ones)))
    c2 = gsend.shape[1]
    for z in range(nz):
        gsend[z, :, 0] = ga[z * c2:(z + 1) * c2]
        gsend[z, :, 1] = gb[z * c2:(z + 1) * c2]
    exchange(1, gsend, recv2, nz, mz, across)

    def entry_step(s, x):
        xg[s] = x
        return recv2[s, :, 0] * x + recv2[s, :, 1]

    lax.fori_loop(0, nz, entry_step, jnp.zeros(xg.shape[1:], jnp.float32))
    exchange(2, xg, back2, nz, mz, across)
    group_in = back2[...].reshape(pa.shape[1:])

    def spread_step(s, carry):
        xs[s] = pa[s] * group_in + pb[s]
        return carry

    lax.fori_loop(0, nq, spread_step, 0)
    exchange(3, xs, back1, nq, mq, in_plane)
    out_ref[...] = back1[...]


def to_tiles(block):
    rows, cols = block.shape[-2] * block.shape[-3], block.shape[-1]
    flat = block.reshape(rows // 8, 8, cols // 128, 128)
    return flat.transpose(0, 2, 1, 3).reshape(-1, 8, 128)


def from_tiles(tiles, shape):
    rows, cols = shape[0] * shape[1], shape[2]
    grid = tiles.reshape(rows // 8, cols // 128, 8, 128)
    return grid.transpose(0, 2, 1, 3).reshape(shape)


def per_device_body(coarse_points, coarse_decay, diffusion, forcing):
    slots, comps, row_count, col_count = coarse_points.shape
    space_count = lax.axis_size("space")
    me = lax.axis_index("space")

    at_anchor = (lax.axis_index("tz") == 0) & (lax.axis_index("tq") == 0)
    scale0 = jnp.where(at_anchor, 0.0, coarse_decay[0])
    comp_scale = coarse_decay[1] * scale0

    state = coarse_points.reshape(slots * comps, row_count, col_count)
    forward = [(i, i + 1) for i in range(space_count - 1)]
    backward = [(i + 1, i) for i in range(space_count - 1)]

    def rim(lo, hi):
        return jnp.concatenate([state[:, lo:hi], diffusion[None, lo:hi], forcing[:, lo:hi]], axis=0)

    up_rim = rim(row_count - HALO, row_count)
    dn_rim = rim(0, HALO)
    above = lax.ppermute(up_rim, "space", forward)
    below = lax.ppermute(dn_rim, "space", backward)
    ext_rows = row_count + 2 * HALO
    global_row = me * row_count - HALO + lax.broadcasted_iota(jnp.int32, (ext_rows, 1), 0)
    keep = ((global_row >= 0) & (global_row < space_count * row_count)).astype(jnp.float32)

    vmem = pl.BlockSpec(memory_space=pltpu.VMEM)
    fine_end = pl.pallas_call(
        fine_kernel,
        out_shape=jax.ShapeDtypeStruct((slots * comps, row_count, col_count), jnp.float32),
        in_specs=[vmem] * 6,
        out_specs=vmem,
        scratch_shapes=[
            pltpu.VMEM((slots * comps, ext_rows, col_count), jnp.float32),
            pltpu.VMEM((ext_rows, col_count), jnp.float32),
            pltpu.VMEM((comps, ext_rows, col_count), jnp.float32),
        ],
    )(state, diffusion, forcing, above, below, keep)
    fine_end = fine_end.reshape(coarse_points.shape)

    shift = fine_end - coarse_decay * coarse_points
    scale = coarse_decay
    shift0 = jnp.where(at_anchor, coarse_decay[0] * coarse_points[0] + shift[0], shift[0])
    comp_shift = scale[1] * shift0 + shift[1]

    both = jnp.stack([to_tiles(comp_scale), to_tiles(comp_shift)], axis=1)
    tiles = both.shape[0]
    q_count = lax.axis_size("tq")
    z_count = lax.axis_size("tz")
    c1 = tiles // q_count
    c2 = c1 // z_count
    both = both.reshape(q_count, c1, 2, 8, 128)
    x1 = (q_count, c1, 8, 128)
    x2 = (z_count, c2, 8, 128)
    vmem = pl.BlockSpec(memory_space=pltpu.VMEM)
    back = pl.pallas_call(
        exchange_kernel,
        out_shape=jax.ShapeDtypeStruct(x1, jnp.float32),
        in_specs=[vmem],
        out_specs=vmem,
        scratch_shapes=[
            pltpu.VMEM(both.shape, jnp.float32),
            pltpu.VMEM(x1, jnp.float32),
            pltpu.VMEM(x1, jnp.float32),
            pltpu.VMEM((z_count, c2, 2, 8, 128), jnp.float32),
            pltpu.VMEM((z_count, c2, 2, 8, 128), jnp.float32),
            pltpu.VMEM(x2, jnp.float32),
            pltpu.VMEM(x2, jnp.float32),
            pltpu.VMEM(x1, jnp.float32),
            pltpu.VMEM(x1, jnp.float32),
            pltpu.SemaphoreType.DMA((8, max(q_count, z_count))),
        ],
        compiler_params=pltpu.CompilerParams(has_side_effects=True),
    )(both)
    back = back.reshape(tiles, 8, 128)
    entering = from_tiles(back, (comps, row_count, col_count))

    first = scale0 * entering + shift0
    second = scale[1] * first + shift[1]
    return jnp.stack([first, second], axis=0)


def solution(mesh):
    tm_count = mesh.shape["tm"]
    q_count = 8 if tm_count >= 16 and tm_count % 8 == 0 else 2
    grid = mesh.devices.reshape(tm_count // q_count, q_count, mesh.shape["space"])
    mesh = jax.sharding.Mesh(grid, ("tz", "tq", "space"))
    time_axes = ("tz", "tq")
    placed = (
        P(time_axes, None, "space", None),
        P(time_axes, None, "space", None),
        P("space", None),
        P(None, "space", None),
    )
    return jax.shard_map(
        per_device_body,
        mesh=mesh,
        in_specs=placed,
        out_specs=P(time_axes, None, "space", None),
        check_vma=False,
    )
```

```python
import jax
import jax.numpy as jnp
from jax import lax
from jax.experimental import pallas as pl
from jax.experimental.pallas import tpu as pltpu
from jax.sharding import PartitionSpec as P

M = 16
HALO = M


def fine_kernel(st_ref, dif_ref, frc_ref, keep_ref, out_ref, buf, dbuf, fbuf, sems):
    n_state = st_ref.shape[0]
    own = st_ref.shape[1]
    cols = st_ref.shape[2]
    rows = own + 2 * HALO
    n = lax.axis_size("space")
    me = lax.axis_index("space")
    place = (lax.axis_index("tz"), lax.axis_index("tq"))
    mesh_id = pl.DeviceIdType.MESH
    pairs = ((st_ref, buf), (dif_ref, dbuf), (frc_ref, fbuf))

    def rim_copy(k, src, dst, down, target):
        if down:
            s_rows, d_rows = pl.ds(own - HALO, HALO), pl.ds(0, HALO)
        else:
            s_rows, d_rows = pl.ds(0, HALO), pl.ds(HALO + own, HALO)
        if src.ndim == 3:
            src_v, dst_v = src.at[:, s_rows], dst.at[:, d_rows]
        else:
            src_v, dst_v = src.at[s_rows], dst.at[d_rows]
        slot = k + (0 if down else 3)
        return pltpu.make_async_remote_copy(
            src_ref=src_v, dst_ref=dst_v, send_sem=sems.at[slot], recv_sem=sems.at[6 + slot],
            device_id=place + (target,), device_id_type=mesh_id,
        )

    @pl.when(me < n - 1)
    def _():
        for k, (src, dst) in enumerate(pairs):
            rim_copy(k, src, dst, True, me + 1).start()

    @pl.when(me > 0)
    def _():
        for k, (src, dst) in enumerate(pairs):
            rim_copy(k, src, dst, False, me - 1).start()

    buf[:, HALO:HALO + own] = st_ref[...]
    dbuf[HALO:HALO + own] = dif_ref[...]
    fbuf[:, HALO:HALO + own] = frc_ref[...]

    @pl.when(me == 0)
    def _():
        buf[:, :HALO] = jnp.zeros((n_state, HALO, cols), jnp.float32)
        dbuf[:HALO] = jnp.zeros((HALO, cols), jnp.float32)
        fbuf[:, :HALO] = jnp.zeros((fbuf.shape[0], HALO, cols), jnp.float32)

    @pl.when(me == n - 1)
    def _():
        buf[:, HALO + own:] = jnp.zeros((n_state, HALO, cols), jnp.float32)
        dbuf[HALO + own:] = jnp.zeros((HALO, cols), jnp.float32)
        fbuf[:, HALO + own:] = jnp.zeros((fbuf.shape[0], HALO, cols), jnp.float32)

    @pl.when(me < n - 1)
    def _():
        for k, (src, dst) in enumerate(pairs):
            rim_copy(k, src, dst, True, me + 1).wait_send()
            rim_copy(k, src, dst, False, me + 1).wait_recv()

    @pl.when(me > 0)
    def _():
        for k, (src, dst) in enumerate(pairs):
            rim_copy(k, src, dst, False, me - 1).wait_send()
            rim_copy(k, src, dst, True, me - 1).wait_recv()

    def make_step(lo, hi):
        span = hi - lo

        def one_step(counter, carry):
            dif = dbuf[lo:hi]
            keep = keep_ref[lo:hi] > 0.5
            for slot in range(2):
                u = buf[2 * slot, lo:hi]
                v = buf[2 * slot + 1, lo:hi]
                new = []
                for comp, c in enumerate((u, v)):
                    next_row = pltpu.roll(c, span - 1, 0)
                    prev_row = pltpu.roll(c, 1, 0)
                    next_col = pltpu.roll(c, cols - 1, 1)
                    prev_col = pltpu.roll(c, 1, 1)
                    value = (
                        c
                        + dif * (next_row + prev_row + next_col + prev_col - 4.0 * c)
                        - 0.05 * (u * (next_row - prev_row) + v * (next_col - prev_col))
                        + 0.05 * fbuf[comp, lo:hi]
                    )
                    new.append(jnp.where(keep, value, 0.0))
                buf[2 * slot, lo:hi] = new[0]
                buf[2 * slot + 1, lo:hi] = new[1]
            return carry

        return one_step

    half = M // 2
    lax.fori_loop(0, half, make_step(0, rows), 0)
    lax.fori_loop(0, M - half, make_step(half, rows - half), 0)
    out_ref[...] = buf[:, HALO:HALO + own, :]


def exchange_kernel(send_ref, out_ref, recv1, pa, pb, gsend, recv2, xg, back2, xs, back1, sems):
    nq = send_ref.shape[0]
    nz = gsend.shape[0]
    mz = lax.axis_index("tz")
    mq = lax.axis_index("tq")
    sp = lax.axis_index("space")
    mesh_id = pl.DeviceIdType.MESH

    def exchange(phase, src, dst, n, me, where):
        ssem, rsem = sems.at[2 * phase], sems.at[2 * phase + 1]

        def outgoing(d):
            return pltpu.make_async_remote_copy(
                src_ref=src.at[d], dst_ref=dst.at[me], send_sem=ssem.at[d], recv_sem=rsem.at[me],
                device_id=where(d), device_id_type=mesh_id,
            )

        def incoming(e):
            return pltpu.make_async_remote_copy(
                src_ref=src.at[e], dst_ref=dst.at[e], send_sem=ssem.at[e], recv_sem=rsem.at[e],
                device_id=where(e), device_id_type=mesh_id,
            )

        def start(k, carry):
            outgoing(lax.rem(me + k, n)).start()
            return carry

        lax.fori_loop(1, n, start, 0)
        dst[me] = src[me]

        def wait(k, carry):
            d = lax.rem(me + k, n)
            outgoing(d).wait_send()
            incoming(d).wait_recv()
            return carry

        lax.fori_loop(1, n, wait, 0)

    in_plane = lambda d: (mz, d, sp)
    across = lambda d: (d, mq, sp)
    exchange(0, send_ref, recv1, nq, mq, in_plane)

    def group_step(s, carry):
        ga, gb = carry
        pa[s] = ga
        pb[s] = gb
        a = recv1[s, :, 0]
        return a * ga, a * gb + recv1[s, :, 1]

    ones = jnp.ones(pa.shape[1:], jnp.float32)
    ga, gb = lax.fori_loop(0, nq, group_step, (ones, jnp.zeros_like(ones)))
    c2 = gsend.shape[1]
    for z in range(nz):
        gsend[z, :, 0] = ga[z * c2:(z + 1) * c2]
        gsend[z, :, 1] = gb[z * c2:(z + 1) * c2]
    exchange(1, gsend, recv2, nz, mz, across)

    def entry_step(s, x):
        xg[s] = x
        return recv2[s, :, 0] * x + recv2[s, :, 1]

    lax.fori_loop(0, nz, entry_step, jnp.zeros(xg.shape[1:], jnp.float32))
    exchange(2, xg, back2, nz, mz, across)
    group_in = back2[...].reshape(pa.shape[1:])

    def spread_step(s, carry):
        xs[s] = pa[s] * group_in + pb[s]
        return carry

    lax.fori_loop(0, nq, spread_step, 0)
    exchange(3, xs, back1, nq, mq, in_plane)
    out_ref[...] = back1[...]


def to_tiles(block):
    rows, cols = block.shape[-2] * block.shape[-3], block.shape[-1]
    flat = block.reshape(rows // 8, 8, cols // 128, 128)
    return flat.transpose(0, 2, 1, 3).reshape(-1, 8, 128)


def from_tiles(tiles, shape):
    rows, cols = shape[0] * shape[1], shape[2]
    grid = tiles.reshape(rows // 8, cols // 128, 8, 128)
    return grid.transpose(0, 2, 1, 3).reshape(shape)


def per_device_body(coarse_points, coarse_decay, diffusion, forcing):
    slots, comps, row_count, col_count = coarse_points.shape
    space_count = lax.axis_size("space")
    me = lax.axis_index("space")

    at_anchor = (lax.axis_index("tz") == 0) & (lax.axis_index("tq") == 0)
    scale0 = jnp.where(at_anchor, 0.0, coarse_decay[0])
    comp_scale = coarse_decay[1] * scale0

    state = coarse_points.reshape(slots * comps, row_count, col_count)
    ext_rows = row_count + 2 * HALO
    global_row = me * row_count - HALO + lax.broadcasted_iota(jnp.int32, (ext_rows, 1), 0)
    keep = ((global_row >= 0) & (global_row < space_count * row_count)).astype(jnp.float32)

    vmem = pl.BlockSpec(memory_space=pltpu.VMEM)
    fine_end = pl.pallas_call(
        fine_kernel,
        out_shape=jax.ShapeDtypeStruct((slots * comps, row_count, col_count), jnp.float32),
        in_specs=[vmem] * 4,
        out_specs=vmem,
        scratch_shapes=[
            pltpu.VMEM((slots * comps, ext_rows, col_count), jnp.float32),
            pltpu.VMEM((ext_rows, col_count), jnp.float32),
            pltpu.VMEM((comps, ext_rows, col_count), jnp.float32),
            pltpu.SemaphoreType.DMA((12,)),
        ],
        compiler_params=pltpu.CompilerParams(has_side_effects=True),
    )(state, diffusion, forcing, keep)
    fine_end = fine_end.reshape(coarse_points.shape)

    shift = fine_end - coarse_decay * coarse_points
    scale = coarse_decay
    shift0 = jnp.where(at_anchor, coarse_decay[0] * coarse_points[0] + shift[0], shift[0])
    comp_shift = scale[1] * shift0 + shift[1]

    both = jnp.stack([to_tiles(comp_scale), to_tiles(comp_shift)], axis=1)
    tiles = both.shape[0]
    q_count = lax.axis_size("tq")
    z_count = lax.axis_size("tz")
    c1 = tiles // q_count
    c2 = c1 // z_count
    both = both.reshape(q_count, c1, 2, 8, 128)
    x1 = (q_count, c1, 8, 128)
    x2 = (z_count, c2, 8, 128)
    vmem = pl.BlockSpec(memory_space=pltpu.VMEM)
    back = pl.pallas_call(
        exchange_kernel,
        out_shape=jax.ShapeDtypeStruct(x1, jnp.float32),
        in_specs=[vmem],
        out_specs=vmem,
        scratch_shapes=[
            pltpu.VMEM(both.shape, jnp.float32),
            pltpu.VMEM(x1, jnp.float32),
            pltpu.VMEM(x1, jnp.float32),
            pltpu.VMEM((z_count, c2, 2, 8, 128), jnp.float32),
            pltpu.VMEM((z_count, c2, 2, 8, 128), jnp.float32),
            pltpu.VMEM(x2, jnp.float32),
            pltpu.VMEM(x2, jnp.float32),
            pltpu.VMEM(x1, jnp.float32),
            pltpu.VMEM(x1, jnp.float32),
            pltpu.SemaphoreType.DMA((8, max(q_count, z_count))),
        ],
        compiler_params=pltpu.CompilerParams(has_side_effects=True),
    )(both)
    back = back.reshape(tiles, 8, 128)
    entering = from_tiles(back, (comps, row_count, col_count))

    first = scale0 * entering + shift0
    second = scale[1] * first + shift[1]
    return jnp.stack([first, second], axis=0)


def solution(mesh):
    tm_count = mesh.shape["tm"]
    q_count = 8 if tm_count >= 16 and tm_count % 8 == 0 else 2
    grid = mesh.devices.reshape(tm_count // q_count, q_count, mesh.shape["space"])
    mesh = jax.sharding.Mesh(grid, ("tz", "tq", "space"))
    time_axes = ("tz", "tq")
    placed = (
        P(time_axes, None, "space", None),
        P(time_axes, None, "space", None),
        P("space", None),
        P(None, "space", None),
    )
    return jax.shard_map(
        per_device_body,
        mesh=mesh,
        in_specs=placed,
        out_specs=P(time_axes, None, "space", None),
        check_vma=False,
    )
```

```python
import jax
import jax.numpy as jnp
from jax import lax
from jax.experimental import pallas as pl
from jax.experimental.pallas import tpu as pltpu
from jax.sharding import PartitionSpec as P

M = 16
HALO = M


def fine_kernel(st_ref, dif_ref, frc_ref, up_ref, dn_ref, keep_ref, out_ref, buf, dbuf, fbuf):
    n_state = st_ref.shape[0]
    own = st_ref.shape[1]
    cols = st_ref.shape[2]
    rows = own + 2 * HALO
    buf[:, :HALO] = up_ref[:n_state]
    buf[:, HALO:HALO + own] = st_ref[...]
    buf[:, HALO + own:] = dn_ref[:n_state]
    dbuf[:HALO] = up_ref[n_state]
    dbuf[HALO:HALO + own] = dif_ref[...]
    dbuf[HALO + own:] = dn_ref[n_state]
    fbuf[:, :HALO] = up_ref[n_state + 1:]
    fbuf[:, HALO:HALO + own] = frc_ref[...]
    fbuf[:, HALO + own:] = dn_ref[n_state + 1:]

    def make_step(lo, hi):
        span = hi - lo

        def one_step(counter, carry):
            dif = dbuf[lo:hi]
            keep = keep_ref[lo:hi] > 0.5
            for slot in range(2):
                u = buf[2 * slot, lo:hi]
                v = buf[2 * slot + 1, lo:hi]
                new = []
                for comp, c in enumerate((u, v)):
                    next_row = pltpu.roll(c, span - 1, 0)
                    prev_row = pltpu.roll(c, 1, 0)
                    next_col = pltpu.roll(c, cols - 1, 1)
                    prev_col = pltpu.roll(c, 1, 1)
                    value = (
                        c
                        + dif * (next_row + prev_row + next_col + prev_col - 4.0 * c)
                        - 0.05 * (u * (next_row - prev_row) + v * (next_col - prev_col))
                        + 0.05 * fbuf[comp, lo:hi]
                    )
                    new.append(jnp.where(keep, value, 0.0))
                buf[2 * slot, lo:hi] = new[0]
                buf[2 * slot + 1, lo:hi] = new[1]
            return carry

        return one_step

    half = M // 2
    lax.fori_loop(0, half, make_step(0, rows), 0)
    lax.fori_loop(0, M - half, make_step(half, rows - half), 0)
    out_ref[...] = buf[:, HALO:HALO + own, :]


def exchange_kernel(send_ref, out_ref, recv1, pa, pb, gsend, recv2, xg, back2, xs, back1, sems):
    nq = send_ref.shape[0]
    nz = gsend.shape[0]
    mz = lax.axis_index("tz")
    mq = lax.axis_index("tq")
    sp = lax.axis_index("space")
    mesh_id = pl.DeviceIdType.MESH

    def exchange(phase, src, dst, n, me, where):
        ssem, rsem = sems.at[2 * phase], sems.at[2 * phase + 1]

        def outgoing(d):
            return pltpu.make_async_remote_copy(
                src_ref=src.at[d], dst_ref=dst.at[me], send_sem=ssem.at[d], recv_sem=rsem.at[me],
                device_id=where(d), device_id_type=mesh_id,
            )

        def incoming(e):
            return pltpu.make_async_remote_copy(
                src_ref=src.at[e], dst_ref=dst.at[e], send_sem=ssem.at[e], recv_sem=rsem.at[e],
                device_id=where(e), device_id_type=mesh_id,
            )

        def start(k, carry):
            outgoing(lax.rem(me + k, n)).start()
            return carry

        lax.fori_loop(1, n, start, 0)
        dst[me] = src[me]

        def wait(k, carry):
            d = lax.rem(me + k, n)
            outgoing(d).wait_send()
            incoming(d).wait_recv()
            return carry

        lax.fori_loop(1, n, wait, 0)

    in_plane = lambda d: (mz, d, sp)
    across = lambda d: (d, mq, sp)
    barrier = pltpu.get_barrier_semaphore()
    for k in range(1, nq):
        pl.semaphore_signal(
            barrier, 1, device_id=in_plane(lax.rem(mq + k, nq)), device_id_type=mesh_id
        )
    for k in range(1, nz):
        pl.semaphore_signal(
            barrier, 1, device_id=across(lax.rem(mz + k, nz)), device_id_type=mesh_id
        )
    pl.semaphore_wait(barrier, nq + nz - 2)
    exchange(0, send_ref, recv1, nq, mq, in_plane)

    def group_step(s, carry):
        ga, gb = carry
        pa[s] = ga
        pb[s] = gb
        a = recv1[s, :, 0]
        return a * ga, a * gb + recv1[s, :, 1]

    ones = jnp.ones(pa.shape[1:], jnp.float32)
    ga, gb = lax.fori_loop(0, nq, group_step, (ones, jnp.zeros_like(ones)))
    c2 = gsend.shape[1]
    for z in range(nz):
        gsend[z, :, 0] = ga[z * c2:(z + 1) * c2]
        gsend[z, :, 1] = gb[z * c2:(z + 1) * c2]
    exchange(1, gsend, recv2, nz, mz, across)

    def entry_step(s, x):
        xg[s] = x
        return recv2[s, :, 0] * x + recv2[s, :, 1]

    lax.fori_loop(0, nz, entry_step, jnp.zeros(xg.shape[1:], jnp.float32))
    exchange(2, xg, back2, nz, mz, across)
    group_in = back2[...].reshape(pa.shape[1:])

    def spread_step(s, carry):
        xs[s] = pa[s] * group_in + pb[s]
        return carry

    lax.fori_loop(0, nq, spread_step, 0)
    exchange(3, xs, back1, nq, mq, in_plane)
    out_ref[...] = back1[...]


def to_tiles(block):
    rows, cols = block.shape[-2] * block.shape[-3], block.shape[-1]
    flat = block.reshape(rows // 8, 8, cols // 128, 128)
    return flat.transpose(0, 2, 1, 3).reshape(-1, 8, 128)


def from_tiles(tiles, shape):
    rows, cols = shape[0] * shape[1], shape[2]
    grid = tiles.reshape(rows // 8, cols // 128, 8, 128)
    return grid.transpose(0, 2, 1, 3).reshape(shape)


def per_device_body(coarse_points, coarse_decay, diffusion, forcing):
    slots, comps, row_count, col_count = coarse_points.shape
    space_count = lax.axis_size("space")
    me = lax.axis_index("space")

    at_anchor = (lax.axis_index("tz") == 0) & (lax.axis_index("tq") == 0)
    scale0 = jnp.where(at_anchor, 0.0, coarse_decay[0])
    comp_scale = coarse_decay[1] * scale0

    state = coarse_points.reshape(slots * comps, row_count, col_count)
    forward = [(i, i + 1) for i in range(space_count - 1)]
    backward = [(i + 1, i) for i in range(space_count - 1)]

    def rim(lo, hi):
        return jnp.concatenate([state[:, lo:hi], diffusion[None, lo:hi], forcing[:, lo:hi]], axis=0)

    up_rim = rim(row_count - HALO, row_count)
    dn_rim = rim(0, HALO)
    above = lax.ppermute(up_rim, "space", forward)
    below = lax.ppermute(dn_rim, "space", backward)
    ext_rows = row_count + 2 * HALO
    global_row = me * row_count - HALO + lax.broadcasted_iota(jnp.int32, (ext_rows, 1), 0)
    keep = ((global_row >= 0) & (global_row < space_count * row_count)).astype(jnp.float32)

    vmem = pl.BlockSpec(memory_space=pltpu.VMEM)
    fine_end = pl.pallas_call(
        fine_kernel,
        out_shape=jax.ShapeDtypeStruct((slots * comps, row_count, col_count), jnp.float32),
        in_specs=[vmem] * 6,
        out_specs=vmem,
        scratch_shapes=[
            pltpu.VMEM((slots * comps, ext_rows, col_count), jnp.float32),
            pltpu.VMEM((ext_rows, col_count), jnp.float32),
            pltpu.VMEM((comps, ext_rows, col_count), jnp.float32),
        ],
    )(state, diffusion, forcing, above, below, keep)
    fine_end = fine_end.reshape(coarse_points.shape)

    shift = fine_end - coarse_decay * coarse_points
    scale = coarse_decay
    shift0 = jnp.where(at_anchor, coarse_decay[0] * coarse_points[0] + shift[0], shift[0])
    comp_shift = scale[1] * shift0 + shift[1]

    both = jnp.stack([to_tiles(comp_scale), to_tiles(comp_shift)], axis=1)
    tiles = both.shape[0]
    q_count = lax.axis_size("tq")
    z_count = lax.axis_size("tz")
    c1 = tiles // q_count
    c2 = c1 // z_count
    both = both.reshape(q_count, c1, 2, 8, 128)
    x1 = (q_count, c1, 8, 128)
    x2 = (z_count, c2, 8, 128)
    vmem = pl.BlockSpec(memory_space=pltpu.VMEM)
    back = pl.pallas_call(
        exchange_kernel,
        out_shape=jax.ShapeDtypeStruct(x1, jnp.float32),
        in_specs=[vmem],
        out_specs=vmem,
        scratch_shapes=[
            pltpu.VMEM(both.shape, jnp.float32),
            pltpu.VMEM(x1, jnp.float32),
            pltpu.VMEM(x1, jnp.float32),
            pltpu.VMEM((z_count, c2, 2, 8, 128), jnp.float32),
            pltpu.VMEM((z_count, c2, 2, 8, 128), jnp.float32),
            pltpu.VMEM(x2, jnp.float32),
            pltpu.VMEM(x2, jnp.float32),
            pltpu.VMEM(x1, jnp.float32),
            pltpu.VMEM(x1, jnp.float32),
            pltpu.SemaphoreType.DMA((8, max(q_count, z_count))),
        ],
        compiler_params=pltpu.CompilerParams(collective_id=0, has_side_effects=True),
    )(both)
    back = back.reshape(tiles, 8, 128)
    entering = from_tiles(back, (comps, row_count, col_count))

    first = scale0 * entering + shift0
    second = scale[1] * first + shift[1]
    return jnp.stack([first, second], axis=0)


def solution(mesh):
    tm_count = mesh.shape["tm"]
    q_count = 8 if tm_count >= 16 and tm_count % 8 == 0 else 2
    grid = mesh.devices.reshape(tm_count // q_count, q_count, mesh.shape["space"])
    mesh = jax.sharding.Mesh(grid, ("tz", "tq", "space"))
    time_axes = ("tz", "tq")
    placed = (
        P(time_axes, None, "space", None),
        P(time_axes, None, "space", None),
        P("space", None),
        P(None, "space", None),
    )
    return jax.shard_map(
        per_device_body,
        mesh=mesh,
        in_specs=placed,
        out_specs=P(time_axes, None, "space", None),
        check_vma=False,
    )
```

```python
import jax
import jax.numpy as jnp
from jax import lax
from jax.experimental import pallas as pl
from jax.experimental.pallas import tpu as pltpu
from jax.sharding import PartitionSpec as P

M = 16
HALO = M


def fine_kernel(st_ref, dif_ref, frc_ref, keep_ref, out_ref, buf, dbuf, fbuf, sems):
    n_state = st_ref.shape[0]
    own = st_ref.shape[1]
    cols = st_ref.shape[2]
    rows = own + 2 * HALO
    n = lax.axis_size("space")
    me = lax.axis_index("space")
    place = (lax.axis_index("tz"), lax.axis_index("tq"))
    mesh_id = pl.DeviceIdType.MESH
    pairs = ((st_ref, buf), (dif_ref, dbuf), (frc_ref, fbuf))
    barrier = pltpu.get_barrier_semaphore()

    @pl.when(me > 0)
    def _():
        pl.semaphore_signal(barrier, 1, device_id=place + (me - 1,), device_id_type=mesh_id)

    @pl.when(me < n - 1)
    def _():
        pl.semaphore_signal(barrier, 1, device_id=place + (me + 1,), device_id_type=mesh_id)

    @pl.when((me > 0) & (me < n - 1))
    def _():
        pl.semaphore_wait(barrier, 2)

    @pl.when((me == 0) | (me == n - 1))
    def _():
        pl.semaphore_wait(barrier, 1)

    def rim_copy(k, src, dst, down, target):
        if down:
            s_rows, d_rows = pl.ds(own - HALO, HALO), pl.ds(0, HALO)
        else:
            s_rows, d_rows = pl.ds(0, HALO), pl.ds(HALO + own, HALO)
        if src.ndim == 3:
            src_v, dst_v = src.at[:, s_rows], dst.at[:, d_rows]
        else:
            src_v, dst_v = src.at[s_rows], dst.at[d_rows]
        slot = k + (0 if down else 3)
        return pltpu.make_async_remote_copy(
            src_ref=src_v, dst_ref=dst_v, send_sem=sems.at[slot], recv_sem=sems.at[6 + slot],
            device_id=place + (target,), device_id_type=mesh_id,
        )

    @pl.when(me < n - 1)
    def _():
        for k, (src, dst) in enumerate(pairs):
            rim_copy(k, src, dst, True, me + 1).start()

    @pl.when(me > 0)
    def _():
        for k, (src, dst) in enumerate(pairs):
            rim_copy(k, src, dst, False, me - 1).start()

    buf[:, HALO:HALO + own] = st_ref[...]
    dbuf[HALO:HALO + own] = dif_ref[...]
    fbuf[:, HALO:HALO + own] = frc_ref[...]

    @pl.when(me == 0)
    def _():
        buf[:, :HALO] = jnp.zeros((n_state, HALO, cols), jnp.float32)
        dbuf[:HALO] = jnp.zeros((HALO, cols), jnp.float32)
        fbuf[:, :HALO] = jnp.zeros((fbuf.shape[0], HALO, cols), jnp.float32)

    @pl.when(me == n - 1)
    def _():
        buf[:, HALO + own:] = jnp.zeros((n_state, HALO, cols), jnp.float32)
        dbuf[HALO + own:] = jnp.zeros((HALO, cols), jnp.float32)
        fbuf[:, HALO + own:] = jnp.zeros((fbuf.shape[0], HALO, cols), jnp.float32)

    @pl.when(me < n - 1)
    def _():
        for k, (src, dst) in enumerate(pairs):
            rim_copy(k, src, dst, True, me + 1).wait_send()
            rim_copy(k, src, dst, False, me + 1).wait_recv()

    @pl.when(me > 0)
    def _():
        for k, (src, dst) in enumerate(pairs):
            rim_copy(k, src, dst, False, me - 1).wait_send()
            rim_copy(k, src, dst, True, me - 1).wait_recv()

    def make_step(lo, hi):
        span = hi - lo

        def one_step(counter, carry):
            dif = dbuf[lo:hi]
            keep = keep_ref[lo:hi] > 0.5
            for slot in range(2):
                u = buf[2 * slot, lo:hi]
                v = buf[2 * slot + 1, lo:hi]
                new = []
                for comp, c in enumerate((u, v)):
                    next_row = pltpu.roll(c, span - 1, 0)
                    prev_row = pltpu.roll(c, 1, 0)
                    next_col = pltpu.roll(c, cols - 1, 1)
                    prev_col = pltpu.roll(c, 1, 1)
                    value = (
                        c
                        + dif * (next_row + prev_row + next_col + prev_col - 4.0 * c)
                        - 0.05 * (u * (next_row - prev_row) + v * (next_col - prev_col))
                        + 0.05 * fbuf[comp, lo:hi]
                    )
                    new.append(jnp.where(keep, value, 0.0))
                buf[2 * slot, lo:hi] = new[0]
                buf[2 * slot + 1, lo:hi] = new[1]
            return carry

        return one_step

    half = M // 2
    lax.fori_loop(0, half, make_step(0, rows), 0)
    lax.fori_loop(0, M - half, make_step(half, rows - half), 0)
    out_ref[...] = buf[:, HALO:HALO + own, :]


def exchange_kernel(send_ref, out_ref, recv1, pa, pb, gsend, recv2, xg, back2, xs, back1, sems):
    nq = send_ref.shape[0]
    nz = gsend.shape[0]
    mz = lax.axis_index("tz")
    mq = lax.axis_index("tq")
    sp = lax.axis_index("space")
    mesh_id = pl.DeviceIdType.MESH

    def exchange(phase, src, dst, n, me, where):
        ssem, rsem = sems.at[2 * phase], sems.at[2 * phase + 1]

        def outgoing(d):
            return pltpu.make_async_remote_copy(
                src_ref=src.at[d], dst_ref=dst.at[me], send_sem=ssem.at[d], recv_sem=rsem.at[me],
                device_id=where(d), device_id_type=mesh_id,
            )

        def incoming(e):
            return pltpu.make_async_remote_copy(
                src_ref=src.at[e], dst_ref=dst.at[e], send_sem=ssem.at[e], recv_sem=rsem.at[e],
                device_id=where(e), device_id_type=mesh_id,
            )

        def start(k, carry):
            outgoing(lax.rem(me + k, n)).start()
            return carry

        lax.fori_loop(1, n, start, 0)
        dst[me] = src[me]

        def wait(k, carry):
            d = lax.rem(me + k, n)
            outgoing(d).wait_send()
            incoming(d).wait_recv()
            return carry

        lax.fori_loop(1, n, wait, 0)

    in_plane = lambda d: (mz, d, sp)
    across = lambda d: (d, mq, sp)
    barrier = pltpu.get_barrier_semaphore()
    for k in range(1, nq):
        pl.semaphore_signal(
            barrier, 1, device_id=in_plane(lax.rem(mq + k, nq)), device_id_type=mesh_id
        )
    for k in range(1, nz):
        pl.semaphore_signal(
            barrier, 1, device_id=across(lax.rem(mz + k, nz)), device_id_type=mesh_id
        )
    pl.semaphore_wait(barrier, nq + nz - 2)
    exchange(0, send_ref, recv1, nq, mq, in_plane)

    def group_step(s, carry):
        ga, gb = carry
        pa[s] = ga
        pb[s] = gb
        a = recv1[s, :, 0]
        return a * ga, a * gb + recv1[s, :, 1]

    ones = jnp.ones(pa.shape[1:], jnp.float32)
    ga, gb = lax.fori_loop(0, nq, group_step, (ones, jnp.zeros_like(ones)))
    c2 = gsend.shape[1]
    for z in range(nz):
        gsend[z, :, 0] = ga[z * c2:(z + 1) * c2]
        gsend[z, :, 1] = gb[z * c2:(z + 1) * c2]
    exchange(1, gsend, recv2, nz, mz, across)

    def entry_step(s, x):
        xg[s] = x
        return recv2[s, :, 0] * x + recv2[s, :, 1]

    lax.fori_loop(0, nz, entry_step, jnp.zeros(xg.shape[1:], jnp.float32))
    exchange(2, xg, back2, nz, mz, across)
    group_in = back2[...].reshape(pa.shape[1:])

    def spread_step(s, carry):
        xs[s] = pa[s] * group_in + pb[s]
        return carry

    lax.fori_loop(0, nq, spread_step, 0)
    exchange(3, xs, back1, nq, mq, in_plane)
    out_ref[...] = back1[...]


def to_tiles(block):
    rows, cols = block.shape[-2] * block.shape[-3], block.shape[-1]
    flat = block.reshape(rows // 8, 8, cols // 128, 128)
    return flat.transpose(0, 2, 1, 3).reshape(-1, 8, 128)


def from_tiles(tiles, shape):
    rows, cols = shape[0] * shape[1], shape[2]
    grid = tiles.reshape(rows // 8, cols // 128, 8, 128)
    return grid.transpose(0, 2, 1, 3).reshape(shape)


def per_device_body(coarse_points, coarse_decay, diffusion, forcing):
    slots, comps, row_count, col_count = coarse_points.shape
    space_count = lax.axis_size("space")
    me = lax.axis_index("space")

    at_anchor = (lax.axis_index("tz") == 0) & (lax.axis_index("tq") == 0)
    scale0 = jnp.where(at_anchor, 0.0, coarse_decay[0])
    comp_scale = coarse_decay[1] * scale0

    state = coarse_points.reshape(slots * comps, row_count, col_count)
    ext_rows = row_count + 2 * HALO
    global_row = me * row_count - HALO + lax.broadcasted_iota(jnp.int32, (ext_rows, 1), 0)
    keep = ((global_row >= 0) & (global_row < space_count * row_count)).astype(jnp.float32)

    vmem = pl.BlockSpec(memory_space=pltpu.VMEM)
    fine_end = pl.pallas_call(
        fine_kernel,
        out_shape=jax.ShapeDtypeStruct((slots * comps, row_count, col_count), jnp.float32),
        in_specs=[vmem] * 4,
        out_specs=vmem,
        scratch_shapes=[
            pltpu.VMEM((slots * comps, ext_rows, col_count), jnp.float32),
            pltpu.VMEM((ext_rows, col_count), jnp.float32),
            pltpu.VMEM((comps, ext_rows, col_count), jnp.float32),
            pltpu.SemaphoreType.DMA((12,)),
        ],
        compiler_params=pltpu.CompilerParams(collective_id=1, has_side_effects=True),
    )(state, diffusion, forcing, keep)
    fine_end = fine_end.reshape(coarse_points.shape)

    shift = fine_end - coarse_decay * coarse_points
    scale = coarse_decay
    shift0 = jnp.where(at_anchor, coarse_decay[0] * coarse_points[0] + shift[0], shift[0])
    comp_shift = scale[1] * shift0 + shift[1]

    both = jnp.stack([to_tiles(comp_scale), to_tiles(comp_shift)], axis=1)
    tiles = both.shape[0]
    q_count = lax.axis_size("tq")
    z_count = lax.axis_size("tz")
    c1 = tiles // q_count
    c2 = c1 // z_count
    both = both.reshape(q_count, c1, 2, 8, 128)
    x1 = (q_count, c1, 8, 128)
    x2 = (z_count, c2, 8, 128)
    vmem = pl.BlockSpec(memory_space=pltpu.VMEM)
    back = pl.pallas_call(
        exchange_kernel,
        out_shape=jax.ShapeDtypeStruct(x1, jnp.float32),
        in_specs=[vmem],
        out_specs=vmem,
        scratch_shapes=[
            pltpu.VMEM(both.shape, jnp.float32),
            pltpu.VMEM(x1, jnp.float32),
            pltpu.VMEM(x1, jnp.float32),
            pltpu.VMEM((z_count, c2, 2, 8, 128), jnp.float32),
            pltpu.VMEM((z_count, c2, 2, 8, 128), jnp.float32),
            pltpu.VMEM(x2, jnp.float32),
            pltpu.VMEM(x2, jnp.float32),
            pltpu.VMEM(x1, jnp.float32),
            pltpu.VMEM(x1, jnp.float32),
            pltpu.SemaphoreType.DMA((8, max(q_count, z_count))),
        ],
        compiler_params=pltpu.CompilerParams(collective_id=0, has_side_effects=True),
    )(both)
    back = back.reshape(tiles, 8, 128)
    entering = from_tiles(back, (comps, row_count, col_count))

    first = scale0 * entering + shift0
    second = scale[1] * first + shift[1]
    return jnp.stack([first, second], axis=0)


def solution(mesh):
    tm_count = mesh.shape["tm"]
    q_count = 8 if tm_count >= 16 and tm_count % 8 == 0 else 2
    grid = mesh.devices.reshape(tm_count // q_count, q_count, mesh.shape["space"])
    mesh = jax.sharding.Mesh(grid, ("tz", "tq", "space"))
    time_axes = ("tz", "tq")
    placed = (
        P(time_axes, None, "space", None),
        P(time_axes, None, "space", None),
        P("space", None),
        P(None, "space", None),
    )
    return jax.shard_map(
        per_device_body,
        mesh=mesh,
        in_specs=placed,
        out_specs=P(time_axes, None, "space", None),
        check_vma=False,
    )
```

```python
import jax
import jax.numpy as jnp
from jax import lax
from jax.experimental import pallas as pl
from jax.experimental.pallas import tpu as pltpu
from jax.sharding import PartitionSpec as P

M = 16
HALO = M


def fine_kernel(st_ref, dif_ref, frc_ref, keep_ref, cd_ref, tiles_ref, shift_ref, buf, dbuf, fbuf, sems):
    n_state = st_ref.shape[0]
    own = st_ref.shape[1]
    cols = st_ref.shape[2]
    rows = own + 2 * HALO
    n = lax.axis_size("space")
    me = lax.axis_index("space")
    place = (lax.axis_index("tz"), lax.axis_index("tq"))
    mesh_id = pl.DeviceIdType.MESH
    pairs = ((st_ref, buf), (dif_ref, dbuf), (frc_ref, fbuf))
    barrier = pltpu.get_barrier_semaphore()

    @pl.when(me > 0)
    def _():
        pl.semaphore_signal(barrier, 1, device_id=place + (me - 1,), device_id_type=mesh_id)

    @pl.when(me < n - 1)
    def _():
        pl.semaphore_signal(barrier, 1, device_id=place + (me + 1,), device_id_type=mesh_id)

    @pl.when((me > 0) & (me < n - 1))
    def _():
        pl.semaphore_wait(barrier, 2)

    @pl.when((me == 0) | (me == n - 1))
    def _():
        pl.semaphore_wait(barrier, 1)

    def rim_copy(k, src, dst, down, target):
        if down:
            s_rows, d_rows = pl.ds(own - HALO, HALO), pl.ds(0, HALO)
        else:
            s_rows, d_rows = pl.ds(0, HALO), pl.ds(HALO + own, HALO)
        if src.ndim == 3:
            src_v, dst_v = src.at[:, s_rows], dst.at[:, d_rows]
        else:
            src_v, dst_v = src.at[s_rows], dst.at[d_rows]
        slot = k + (0 if down else 3)
        return pltpu.make_async_remote_copy(
            src_ref=src_v, dst_ref=dst_v, send_sem=sems.at[slot], recv_sem=sems.at[6 + slot],
            device_id=place + (target,), device_id_type=mesh_id,
        )

    @pl.when(me < n - 1)
    def _():
        for k, (src, dst) in enumerate(pairs):
            rim_copy(k, src, dst, True, me + 1).start()

    @pl.when(me > 0)
    def _():
        for k, (src, dst) in enumerate(pairs):
            rim_copy(k, src, dst, False, me - 1).start()

    buf[:, HALO:HALO + own] = st_ref[...]
    dbuf[HALO:HALO + own] = dif_ref[...]
    fbuf[:, HALO:HALO + own] = frc_ref[...]

    @pl.when(me == 0)
    def _():
        buf[:, :HALO] = jnp.zeros((n_state, HALO, cols), jnp.float32)
        dbuf[:HALO] = jnp.zeros((HALO, cols), jnp.float32)
        fbuf[:, :HALO] = jnp.zeros((fbuf.shape[0], HALO, cols), jnp.float32)

    @pl.when(me == n - 1)
    def _():
        buf[:, HALO + own:] = jnp.zeros((n_state, HALO, cols), jnp.float32)
        dbuf[HALO + own:] = jnp.zeros((HALO, cols), jnp.float32)
        fbuf[:, HALO + own:] = jnp.zeros((fbuf.shape[0], HALO, cols), jnp.float32)

    @pl.when(me < n - 1)
    def _():
        for k, (src, dst) in enumerate(pairs):
            rim_copy(k, src, dst, True, me + 1).wait_send()
            rim_copy(k, src, dst, False, me + 1).wait_recv()

    @pl.when(me > 0)
    def _():
        for k, (src, dst) in enumerate(pairs):
            rim_copy(k, src, dst, False, me - 1).wait_send()
            rim_copy(k, src, dst, True, me - 1).wait_recv()

    def make_step(lo, hi):
        span = hi - lo

        def one_step(counter, carry):
            dif = dbuf[lo:hi]
            keep = keep_ref[lo:hi] > 0.5
            for slot in range(2):
                u = buf[2 * slot, lo:hi]
                v = buf[2 * slot + 1, lo:hi]
                new = []
                for comp, c in enumerate((u, v)):
                    next_row = pltpu.roll(c, span - 1, 0)
                    prev_row = pltpu.roll(c, 1, 0)
                    next_col = pltpu.roll(c, cols - 1, 1)
                    prev_col = pltpu.roll(c, 1, 1)
                    value = (
                        c
                        + dif * (next_row + prev_row + next_col + prev_col - 4.0 * c)
                        - 0.05 * (u * (next_row - prev_row) + v * (next_col - prev_col))
                        + 0.05 * fbuf[comp, lo:hi]
                    )
                    new.append(jnp.where(keep, value, 0.0))
                buf[2 * slot, lo:hi] = new[0]
                buf[2 * slot + 1, lo:hi] = new[1]
            return carry

        return one_step

    half = M // 2
    lax.fori_loop(0, half, make_step(0, rows), 0)
    lax.fori_loop(0, M - half, make_step(half, rows - half), 0)
    anchor = (lax.axis_index("tz") == 0) & (lax.axis_index("tq") == 0)
    comps = n_state // 2
    blocks = own // 8
    for comp in range(comps):
        d0, d1 = cd_ref[comp], cd_ref[comps + comp]
        c0, c1 = st_ref[comp], st_ref[comps + comp]
        plain0 = buf[comp, HALO:HALO + own] - d0 * c0
        sh1 = buf[comps + comp, HALO:HALO + own] - d1 * c1
        sh0 = jnp.where(anchor, d0 * c0 + plain0, plain0)
        s0 = jnp.where(anchor, 0.0, d0)
        shift_ref[comp] = sh0
        shift_ref[comps + comp] = sh1
        comp_scale = d1 * s0
        comp_shift = d1 * sh0 + sh1
        for rb in range(blocks):
            for cb in range(cols // 128):
                p = (comp * blocks + rb) * (cols // 128) + cb
                rs, cs = slice(rb * 8, rb * 8 + 8), slice(cb * 128, cb * 128 + 128)
                tiles_ref[p, 0] = comp_scale[rs, cs]
                tiles_ref[p, 1] = comp_shift[rs, cs]


def exchange_kernel(send_ref, out_ref, recv1, pa, pb, gsend, recv2, xg, back2, xs, back1, sems):
    nq = send_ref.shape[0]
    nz = gsend.shape[0]
    mz = lax.axis_index("tz")
    mq = lax.axis_index("tq")
    sp = lax.axis_index("space")
    mesh_id = pl.DeviceIdType.MESH

    def exchange(phase, src, dst, n, me, where):
        ssem, rsem = sems.at[2 * phase], sems.at[2 * phase + 1]

        def outgoing(d):
            return pltpu.make_async_remote_copy(
                src_ref=src.at[d], dst_ref=dst.at[me], send_sem=ssem.at[d], recv_sem=rsem.at[me],
                device_id=where(d), device_id_type=mesh_id,
            )

        def incoming(e):
            return pltpu.make_async_remote_copy(
                src_ref=src.at[e], dst_ref=dst.at[e], send_sem=ssem.at[e], recv_sem=rsem.at[e],
                device_id=where(e), device_id_type=mesh_id,
            )

        def start(k, carry):
            outgoing(lax.rem(me + k, n)).start()
            return carry

        lax.fori_loop(1, n, start, 0)
        dst[me] = src[me]

        def wait(k, carry):
            d = lax.rem(me + k, n)
            outgoing(d).wait_send()
            incoming(d).wait_recv()
            return carry

        lax.fori_loop(1, n, wait, 0)

    in_plane = lambda d: (mz, d, sp)
    across = lambda d: (d, mq, sp)
    barrier = pltpu.get_barrier_semaphore()
    for k in range(1, nq):
        pl.semaphore_signal(
            barrier, 1, device_id=in_plane(lax.rem(mq + k, nq)), device_id_type=mesh_id
        )
    for k in range(1, nz):
        pl.semaphore_signal(
            barrier, 1, device_id=across(lax.rem(mz + k, nz)), device_id_type=mesh_id
        )
    pl.semaphore_wait(barrier, nq + nz - 2)
    exchange(0, send_ref, recv1, nq, mq, in_plane)

    def group_step(s, carry):
        ga, gb = carry
        pa[s] = ga
        pb[s] = gb
        a = recv1[s, :, 0]
        return a * ga, a * gb + recv1[s, :, 1]

    ones = jnp.ones(pa.shape[1:], jnp.float32)
    ga, gb = lax.fori_loop(0, nq, group_step, (ones, jnp.zeros_like(ones)))
    c2 = gsend.shape[1]
    for z in range(nz):
        gsend[z, :, 0] = ga[z * c2:(z + 1) * c2]
        gsend[z, :, 1] = gb[z * c2:(z + 1) * c2]
    exchange(1, gsend, recv2, nz, mz, across)

    def entry_step(s, x):
        xg[s] = x
        return recv2[s, :, 0] * x + recv2[s, :, 1]

    lax.fori_loop(0, nz, entry_step, jnp.zeros(xg.shape[1:], jnp.float32))
    exchange(2, xg, back2, nz, mz, across)
    group_in = back2[...].reshape(pa.shape[1:])

    def spread_step(s, carry):
        xs[s] = pa[s] * group_in + pb[s]
        return carry

    lax.fori_loop(0, nq, spread_step, 0)
    exchange(3, xs, back1, nq, mq, in_plane)
    out_ref[...] = back1[...]


def from_tiles(tiles, shape):
    rows, cols = shape[0] * shape[1], shape[2]
    grid = tiles.reshape(rows // 8, cols // 128, 8, 128)
    return grid.transpose(0, 2, 1, 3).reshape(shape)


def per_device_body(coarse_points, coarse_decay, diffusion, forcing):
    slots, comps, row_count, col_count = coarse_points.shape
    space_count = lax.axis_size("space")
    me = lax.axis_index("space")


    state = coarse_points.reshape(slots * comps, row_count, col_count)
    ext_rows = row_count + 2 * HALO
    global_row = me * row_count - HALO + lax.broadcasted_iota(jnp.int32, (ext_rows, 1), 0)
    keep = ((global_row >= 0) & (global_row < space_count * row_count)).astype(jnp.float32)

    vmem = pl.BlockSpec(memory_space=pltpu.VMEM)
    tile_count = slots * comps * row_count * col_count // (2 * 8 * 128)
    both, shifts = pl.pallas_call(
        fine_kernel,
        out_shape=(
            jax.ShapeDtypeStruct((tile_count, 2, 8, 128), jnp.float32),
            jax.ShapeDtypeStruct((slots * comps, row_count, col_count), jnp.float32),
        ),
        in_specs=[vmem] * 5,
        out_specs=(vmem, vmem),
        scratch_shapes=[
            pltpu.VMEM((slots * comps, ext_rows, col_count), jnp.float32),
            pltpu.VMEM((ext_rows, col_count), jnp.float32),
            pltpu.VMEM((comps, ext_rows, col_count), jnp.float32),
            pltpu.SemaphoreType.DMA((12,)),
        ],
        compiler_params=pltpu.CompilerParams(collective_id=1, has_side_effects=True),
    )(state, diffusion, forcing, keep, coarse_decay.reshape(state.shape))
    scale = coarse_decay
    at_anchor = (lax.axis_index("tz") == 0) & (lax.axis_index("tq") == 0)
    scale0 = jnp.where(at_anchor, 0.0, coarse_decay[0])
    shifts = shifts.reshape(coarse_points.shape)
    shift0 = shifts[0]
    shift = shifts
    tiles = both.shape[0]
    q_count = lax.axis_size("tq")
    z_count = lax.axis_size("tz")
    c1 = tiles // q_count
    c2 = c1 // z_count
    both = both.reshape(q_count, c1, 2, 8, 128)
    x1 = (q_count, c1, 8, 128)
    x2 = (z_count, c2, 8, 128)
    vmem = pl.BlockSpec(memory_space=pltpu.VMEM)
    back = pl.pallas_call(
        exchange_kernel,
        out_shape=jax.ShapeDtypeStruct(x1, jnp.float32),
        in_specs=[vmem],
        out_specs=vmem,
        scratch_shapes=[
            pltpu.VMEM(both.shape, jnp.float32),
            pltpu.VMEM(x1, jnp.float32),
            pltpu.VMEM(x1, jnp.float32),
            pltpu.VMEM((z_count, c2, 2, 8, 128), jnp.float32),
            pltpu.VMEM((z_count, c2, 2, 8, 128), jnp.float32),
            pltpu.VMEM(x2, jnp.float32),
            pltpu.VMEM(x2, jnp.float32),
            pltpu.VMEM(x1, jnp.float32),
            pltpu.VMEM(x1, jnp.float32),
            pltpu.SemaphoreType.DMA((8, max(q_count, z_count))),
        ],
        compiler_params=pltpu.CompilerParams(collective_id=0, has_side_effects=True),
    )(both)
    back = back.reshape(tiles, 8, 128)
    entering = from_tiles(back, (comps, row_count, col_count))

    first = scale0 * entering + shift0
    second = scale[1] * first + shift[1]
    return jnp.stack([first, second], axis=0)


def solution(mesh):
    tm_count = mesh.shape["tm"]
    q_count = 8 if tm_count >= 16 and tm_count % 8 == 0 else 2
    grid = mesh.devices.reshape(tm_count // q_count, q_count, mesh.shape["space"])
    mesh = jax.sharding.Mesh(grid, ("tz", "tq", "space"))
    time_axes = ("tz", "tq")
    placed = (
        P(time_axes, None, "space", None),
        P(time_axes, None, "space", None),
        P("space", None),
        P(None, "space", None),
    )
    return jax.shard_map(
        per_device_body,
        mesh=mesh,
        in_specs=placed,
        out_specs=P(time_axes, None, "space", None),
        check_vma=False,
    )
```

```python
import jax
import jax.numpy as jnp
from jax import lax
from jax.experimental import pallas as pl
from jax.experimental.pallas import tpu as pltpu
from jax.sharding import PartitionSpec as P

M = 16
HALO = M


def fine_kernel(st_ref, dif_ref, frc_ref, keep_ref, cd_ref, tiles_ref, shift_ref, buf, dbuf, fbuf, sems):
    n_state = st_ref.shape[0]
    own = st_ref.shape[1]
    cols = st_ref.shape[2]
    rows = own + 2 * HALO
    n = lax.axis_size("space")
    me = lax.axis_index("space")
    place = (lax.axis_index("tz"), lax.axis_index("tq"))
    mesh_id = pl.DeviceIdType.MESH
    pairs = ((st_ref, buf), (dif_ref, dbuf), (frc_ref, fbuf))
    barrier = pltpu.get_barrier_semaphore()

    @pl.when(me > 0)
    def _():
        pl.semaphore_signal(barrier, 1, device_id=place + (me - 1,), device_id_type=mesh_id)

    @pl.when(me < n - 1)
    def _():
        pl.semaphore_signal(barrier, 1, device_id=place + (me + 1,), device_id_type=mesh_id)

    @pl.when((me > 0) & (me < n - 1))
    def _():
        pl.semaphore_wait(barrier, 2)

    @pl.when((me == 0) | (me == n - 1))
    def _():
        pl.semaphore_wait(barrier, 1)

    def rim_copy(k, src, dst, down, target):
        if down:
            s_rows, d_rows = pl.ds(own - HALO, HALO), pl.ds(0, HALO)
        else:
            s_rows, d_rows = pl.ds(0, HALO), pl.ds(HALO + own, HALO)
        if src.ndim == 3:
            src_v, dst_v = src.at[:, s_rows], dst.at[:, d_rows]
        else:
            src_v, dst_v = src.at[s_rows], dst.at[d_rows]
        slot = k + (0 if down else 3)
        return pltpu.make_async_remote_copy(
            src_ref=src_v, dst_ref=dst_v, send_sem=sems.at[slot], recv_sem=sems.at[6 + slot],
            device_id=place + (target,), device_id_type=mesh_id,
        )

    @pl.when(me < n - 1)
    def _():
        for k, (src, dst) in enumerate(pairs):
            rim_copy(k, src, dst, True, me + 1).start()

    @pl.when(me > 0)
    def _():
        for k, (src, dst) in enumerate(pairs):
            rim_copy(k, src, dst, False, me - 1).start()

    buf[:, HALO:HALO + own] = st_ref[...]
    dbuf[HALO:HALO + own] = dif_ref[...]
    fbuf[:, HALO:HALO + own] = frc_ref[...]

    @pl.when(me == 0)
    def _():
        buf[:, :HALO] = jnp.zeros((n_state, HALO, cols), jnp.float32)
        dbuf[:HALO] = jnp.zeros((HALO, cols), jnp.float32)
        fbuf[:, :HALO] = jnp.zeros((fbuf.shape[0], HALO, cols), jnp.float32)

    @pl.when(me == n - 1)
    def _():
        buf[:, HALO + own:] = jnp.zeros((n_state, HALO, cols), jnp.float32)
        dbuf[HALO + own:] = jnp.zeros((HALO, cols), jnp.float32)
        fbuf[:, HALO + own:] = jnp.zeros((fbuf.shape[0], HALO, cols), jnp.float32)

    @pl.when(me < n - 1)
    def _():
        for k, (src, dst) in enumerate(pairs):
            rim_copy(k, src, dst, True, me + 1).wait_send()
            rim_copy(k, src, dst, False, me + 1).wait_recv()

    @pl.when(me > 0)
    def _():
        for k, (src, dst) in enumerate(pairs):
            rim_copy(k, src, dst, False, me - 1).wait_send()
            rim_copy(k, src, dst, True, me - 1).wait_recv()

    def make_step(lo, hi):
        span = hi - lo

        def one_step(counter, carry):
            dif = dbuf[lo:hi]
            keep = keep_ref[lo:hi] > 0.5
            for slot in range(2):
                u = buf[2 * slot, lo:hi]
                v = buf[2 * slot + 1, lo:hi]
                new = []
                for comp, c in enumerate((u, v)):
                    next_row = pltpu.roll(c, span - 1, 0)
                    prev_row = pltpu.roll(c, 1, 0)
                    next_col = pltpu.roll(c, cols - 1, 1)
                    prev_col = pltpu.roll(c, 1, 1)
                    value = (
                        c
                        + dif * (next_row + prev_row + next_col + prev_col - 4.0 * c)
                        - 0.05 * (u * (next_row - prev_row) + v * (next_col - prev_col))
                        + 0.05 * fbuf[comp, lo:hi]
                    )
                    new.append(jnp.where(keep, value, 0.0))
                buf[2 * slot, lo:hi] = new[0]
                buf[2 * slot + 1, lo:hi] = new[1]
            return carry

        return one_step

    half = M // 2
    lax.fori_loop(0, half, make_step(0, rows), 0)
    lax.fori_loop(0, M - half, make_step(half, rows - half), 0)
    anchor = (lax.axis_index("tz") == 0) & (lax.axis_index("tq") == 0)
    comps = n_state // 2
    blocks = own // 8
    for comp in range(comps):
        d0, d1 = cd_ref[comp], cd_ref[comps + comp]
        c0, c1 = st_ref[comp], st_ref[comps + comp]
        plain0 = buf[comp, HALO:HALO + own] - d0 * c0
        sh1 = buf[comps + comp, HALO:HALO + own] - d1 * c1
        sh0 = jnp.where(anchor, d0 * c0 + plain0, plain0)
        s0 = jnp.where(anchor, 0.0, d0)
        shift_ref[comp] = sh0
        shift_ref[comps + comp] = sh1
        comp_scale = d1 * s0
        comp_shift = d1 * sh0 + sh1
        for rb in range(blocks):
            for cb in range(cols // 128):
                p = (comp * blocks + rb) * (cols // 128) + cb
                rs, cs = slice(rb * 8, rb * 8 + 8), slice(cb * 128, cb * 128 + 128)
                tiles_ref[p, 0] = comp_scale[rs, cs]
                tiles_ref[p, 1] = comp_shift[rs, cs]


def exchange_kernel(send_ref, cd_ref, sh_ref, out_ref, recv1, pa, pb, gsend, recv2, xg, back2, xs, back1, sems):
    nq = send_ref.shape[0]
    nz = gsend.shape[0]
    mz = lax.axis_index("tz")
    mq = lax.axis_index("tq")
    sp = lax.axis_index("space")
    mesh_id = pl.DeviceIdType.MESH

    def exchange(phase, src, dst, n, me, where):
        ssem, rsem = sems.at[2 * phase], sems.at[2 * phase + 1]

        def outgoing(d):
            return pltpu.make_async_remote_copy(
                src_ref=src.at[d], dst_ref=dst.at[me], send_sem=ssem.at[d], recv_sem=rsem.at[me],
                device_id=where(d), device_id_type=mesh_id,
            )

        def incoming(e):
            return pltpu.make_async_remote_copy(
                src_ref=src.at[e], dst_ref=dst.at[e], send_sem=ssem.at[e], recv_sem=rsem.at[e],
                device_id=where(e), device_id_type=mesh_id,
            )

        def start(k, carry):
            outgoing(lax.rem(me + k, n)).start()
            return carry

        lax.fori_loop(1, n, start, 0)
        dst[me] = src[me]

        def wait(k, carry):
            d = lax.rem(me + k, n)
            outgoing(d).wait_send()
            incoming(d).wait_recv()
            return carry

        lax.fori_loop(1, n, wait, 0)

    in_plane = lambda d: (mz, d, sp)
    across = lambda d: (d, mq, sp)
    barrier = pltpu.get_barrier_semaphore()
    for k in range(1, nq):
        pl.semaphore_signal(
            barrier, 1, device_id=in_plane(lax.rem(mq + k, nq)), device_id_type=mesh_id
        )
    for k in range(1, nz):
        pl.semaphore_signal(
            barrier, 1, device_id=across(lax.rem(mz + k, nz)), device_id_type=mesh_id
        )
    pl.semaphore_wait(barrier, nq + nz - 2)
    exchange(0, send_ref, recv1, nq, mq, in_plane)

    def group_step(s, carry):
        ga, gb = carry
        pa[s] = ga
        pb[s] = gb
        a = recv1[s, :, 0]
        return a * ga, a * gb + recv1[s, :, 1]

    ones = jnp.ones(pa.shape[1:], jnp.float32)
    ga, gb = lax.fori_loop(0, nq, group_step, (ones, jnp.zeros_like(ones)))
    c2 = gsend.shape[1]
    for z in range(nz):
        gsend[z, :, 0] = ga[z * c2:(z + 1) * c2]
        gsend[z, :, 1] = gb[z * c2:(z + 1) * c2]
    exchange(1, gsend, recv2, nz, mz, across)

    def entry_step(s, x):
        xg[s] = x
        return recv2[s, :, 0] * x + recv2[s, :, 1]

    lax.fori_loop(0, nz, entry_step, jnp.zeros(xg.shape[1:], jnp.float32))
    exchange(2, xg, back2, nz, mz, across)
    group_in = back2[...].reshape(pa.shape[1:])

    def spread_step(s, carry):
        xs[s] = pa[s] * group_in + pb[s]
        return carry

    lax.fori_loop(0, nq, spread_step, 0)
    exchange(3, xs, back1, nq, mq, in_plane)
    anchor = (mz == 0) & (mq == 0)
    n_state, own, cols = cd_ref.shape
    comps = n_state // 2
    blocks = own // 8
    c1 = back1.shape[1]
    for comp in range(comps):
        for rb in range(blocks):
            for cb in range(cols // 128):
                p = (comp * blocks + rb) * (cols // 128) + cb
                rs, cs = pl.ds(rb * 8, 8), pl.ds(cb * 128, 128)
                entering = back1[p // c1, p % c1]
                s0 = jnp.where(anchor, 0.0, cd_ref[comp, rs, cs])
                first = s0 * entering + sh_ref[comp, rs, cs]
                out_ref[comp, rs, cs] = first
                out_ref[comps + comp, rs, cs] = (
                    cd_ref[comps + comp, rs, cs] * first + sh_ref[comps + comp, rs, cs]
                )


def per_device_body(coarse_points, coarse_decay, diffusion, forcing):
    slots, comps, row_count, col_count = coarse_points.shape
    space_count = lax.axis_size("space")
    me = lax.axis_index("space")


    state = coarse_points.reshape(slots * comps, row_count, col_count)
    ext_rows = row_count + 2 * HALO
    global_row = me * row_count - HALO + lax.broadcasted_iota(jnp.int32, (ext_rows, 1), 0)
    keep = ((global_row >= 0) & (global_row < space_count * row_count)).astype(jnp.float32)

    vmem = pl.BlockSpec(memory_space=pltpu.VMEM)
    tile_count = slots * comps * row_count * col_count // (2 * 8 * 128)
    both, shifts = pl.pallas_call(
        fine_kernel,
        out_shape=(
            jax.ShapeDtypeStruct((tile_count, 2, 8, 128), jnp.float32),
            jax.ShapeDtypeStruct((slots * comps, row_count, col_count), jnp.float32),
        ),
        in_specs=[vmem] * 5,
        out_specs=(vmem, vmem),
        scratch_shapes=[
            pltpu.VMEM((slots * comps, ext_rows, col_count), jnp.float32),
            pltpu.VMEM((ext_rows, col_count), jnp.float32),
            pltpu.VMEM((comps, ext_rows, col_count), jnp.float32),
            pltpu.SemaphoreType.DMA((12,)),
        ],
        compiler_params=pltpu.CompilerParams(collective_id=1, has_side_effects=True),
    )(state, diffusion, forcing, keep, coarse_decay.reshape(state.shape))
    at_anchor = (lax.axis_index("tz") == 0) & (lax.axis_index("tq") == 0)
    scale0 = jnp.where(at_anchor, 0.0, coarse_decay[0])
    shifts = shifts.reshape(coarse_points.shape)
    tiles = both.shape[0]
    q_count = lax.axis_size("tq")
    z_count = lax.axis_size("tz")
    c1 = tiles // q_count
    c2 = c1 // z_count
    both = both.reshape(q_count, c1, 2, 8, 128)
    x1 = (q_count, c1, 8, 128)
    x2 = (z_count, c2, 8, 128)
    vmem = pl.BlockSpec(memory_space=pltpu.VMEM)
    updated = pl.pallas_call(
        exchange_kernel,
        out_shape=jax.ShapeDtypeStruct(state.shape, jnp.float32),
        in_specs=[vmem] * 3,
        out_specs=vmem,
        scratch_shapes=[
            pltpu.VMEM(both.shape, jnp.float32),
            pltpu.VMEM(x1, jnp.float32),
            pltpu.VMEM(x1, jnp.float32),
            pltpu.VMEM((z_count, c2, 2, 8, 128), jnp.float32),
            pltpu.VMEM((z_count, c2, 2, 8, 128), jnp.float32),
            pltpu.VMEM(x2, jnp.float32),
            pltpu.VMEM(x2, jnp.float32),
            pltpu.VMEM(x1, jnp.float32),
            pltpu.VMEM(x1, jnp.float32),
            pltpu.SemaphoreType.DMA((8, max(q_count, z_count))),
        ],
        compiler_params=pltpu.CompilerParams(collective_id=0, has_side_effects=True),
    )(both, coarse_decay.reshape(state.shape), shifts.reshape(state.shape))
    return updated.reshape(coarse_points.shape)


def solution(mesh):
    tm_count = mesh.shape["tm"]
    q_count = 8 if tm_count >= 16 and tm_count % 8 == 0 else 2
    grid = mesh.devices.reshape(tm_count // q_count, q_count, mesh.shape["space"])
    mesh = jax.sharding.Mesh(grid, ("tz", "tq", "space"))
    time_axes = ("tz", "tq")
    placed = (
        P(time_axes, None, "space", None),
        P(time_axes, None, "space", None),
        P("space", None),
        P(None, "space", None),
    )
    return jax.shard_map(
        per_device_body,
        mesh=mesh,
        in_specs=placed,
        out_specs=P(time_axes, None, "space", None),
        check_vma=False,
    )
```

```python
import jax
import jax.numpy as jnp
from jax import lax
from jax.experimental import pallas as pl
from jax.experimental.pallas import tpu as pltpu
from jax.sharding import PartitionSpec as P

M = 16
HALO = M


def fine_kernel(st_ref, dif_ref, frc_ref, keep_ref, cd_ref, tiles_ref, shift_ref, buf, dbuf, fbuf, sems):
    n_state = st_ref.shape[0]
    own = st_ref.shape[1]
    cols = st_ref.shape[2]
    rows = own + 2 * HALO
    n = lax.axis_size("space")
    me = lax.axis_index("space")
    place = (lax.axis_index("tz"), lax.axis_index("tq"))
    mesh_id = pl.DeviceIdType.MESH
    pairs = ((st_ref, buf), (dif_ref, dbuf), (frc_ref, fbuf))
    barrier = pltpu.get_barrier_semaphore()

    @pl.when(me > 0)
    def _():
        pl.semaphore_signal(barrier, 1, device_id=place + (me - 1,), device_id_type=mesh_id)

    @pl.when(me < n - 1)
    def _():
        pl.semaphore_signal(barrier, 1, device_id=place + (me + 1,), device_id_type=mesh_id)

    @pl.when((me > 0) & (me < n - 1))
    def _():
        pl.semaphore_wait(barrier, 2)

    @pl.when((me == 0) | (me == n - 1))
    def _():
        pl.semaphore_wait(barrier, 1)

    def rim_copy(k, src, dst, down, target):
        if down:
            s_rows, d_rows = pl.ds(own - HALO, HALO), pl.ds(0, HALO)
        else:
            s_rows, d_rows = pl.ds(0, HALO), pl.ds(HALO + own, HALO)
        if src.ndim == 3:
            src_v, dst_v = src.at[:, s_rows], dst.at[:, d_rows]
        else:
            src_v, dst_v = src.at[s_rows], dst.at[d_rows]
        slot = k + (0 if down else 3)
        return pltpu.make_async_remote_copy(
            src_ref=src_v, dst_ref=dst_v, send_sem=sems.at[slot], recv_sem=sems.at[6 + slot],
            device_id=place + (target,), device_id_type=mesh_id,
        )

    @pl.when(me < n - 1)
    def _():
        for k, (src, dst) in enumerate(pairs):
            rim_copy(k, src, dst, True, me + 1).start()

    @pl.when(me > 0)
    def _():
        for k, (src, dst) in enumerate(pairs):
            rim_copy(k, src, dst, False, me - 1).start()

    buf[:, HALO:HALO + own] = st_ref[...]
    dbuf[HALO:HALO + own] = dif_ref[...]
    fbuf[:, HALO:HALO + own] = frc_ref[...]

    @pl.when(me == 0)
    def _():
        buf[:, :HALO] = jnp.zeros((n_state, HALO, cols), jnp.float32)
        dbuf[:HALO] = jnp.zeros((HALO, cols), jnp.float32)
        fbuf[:, :HALO] = jnp.zeros((fbuf.shape[0], HALO, cols), jnp.float32)

    @pl.when(me == n - 1)
    def _():
        buf[:, HALO + own:] = jnp.zeros((n_state, HALO, cols), jnp.float32)
        dbuf[HALO + own:] = jnp.zeros((HALO, cols), jnp.float32)
        fbuf[:, HALO + own:] = jnp.zeros((fbuf.shape[0], HALO, cols), jnp.float32)

    @pl.when(me < n - 1)
    def _():
        for k, (src, dst) in enumerate(pairs):
            rim_copy(k, src, dst, True, me + 1).wait_send()
            rim_copy(k, src, dst, False, me + 1).wait_recv()

    @pl.when(me > 0)
    def _():
        for k, (src, dst) in enumerate(pairs):
            rim_copy(k, src, dst, False, me - 1).wait_send()
            rim_copy(k, src, dst, True, me - 1).wait_recv()

    def make_step(lo, hi):
        span = hi - lo

        def one_step(counter, carry):
            dif = dbuf[lo:hi]
            keep = keep_ref[lo:hi] > 0.5
            for slot in range(2):
                u = buf[2 * slot, lo:hi]
                v = buf[2 * slot + 1, lo:hi]
                new = []
                for comp, c in enumerate((u, v)):
                    next_row = pltpu.roll(c, span - 1, 0)
                    prev_row = pltpu.roll(c, 1, 0)
                    next_col = pltpu.roll(c, cols - 1, 1)
                    prev_col = pltpu.roll(c, 1, 1)
                    value = (
                        c
                        + dif * (next_row + prev_row + next_col + prev_col - 4.0 * c)
                        - 0.05 * (u * (next_row - prev_row) + v * (next_col - prev_col))
                        + 0.05 * fbuf[comp, lo:hi]
                    )
                    new.append(jnp.where(keep, value, 0.0))
                buf[2 * slot, lo:hi] = new[0]
                buf[2 * slot + 1, lo:hi] = new[1]
            return carry

        return one_step

    half = M // 2
    lax.fori_loop(0, half, make_step(0, rows), 0)
    lax.fori_loop(0, M - half, make_step(half, rows - half), 0)
    anchor = (lax.axis_index("tz") == 0) & (lax.axis_index("tq") == 0)
    comps = n_state // 2
    blocks = own // 8
    for comp in range(comps):
        d0, d1 = cd_ref[comp], cd_ref[comps + comp]
        c0, c1 = st_ref[comp], st_ref[comps + comp]
        plain0 = buf[comp, HALO:HALO + own] - d0 * c0
        sh1 = buf[comps + comp, HALO:HALO + own] - d1 * c1
        sh0 = jnp.where(anchor, d0 * c0 + plain0, plain0)
        s0 = jnp.where(anchor, 0.0, d0)
        shift_ref[comp] = sh0
        shift_ref[comps + comp] = sh1
        comp_scale = d1 * s0
        comp_shift = d1 * sh0 + sh1
        for rb in range(blocks):
            for cb in range(cols // 128):
                p = (comp * blocks + rb) * (cols // 128) + cb
                rs, cs = slice(rb * 8, rb * 8 + 8), slice(cb * 128, cb * 128 + 128)
                tiles_ref[p, 0] = comp_scale[rs, cs]
                tiles_ref[p, 1] = comp_shift[rs, cs]


def exchange_kernel(send_ref, out_ref, recv1, pa, pb, gsend, recv2, xg, back2, xs, back1, sems):
    nq = send_ref.shape[0]
    nz = gsend.shape[0]
    mz = lax.axis_index("tz")
    mq = lax.axis_index("tq")
    sp = lax.axis_index("space")
    mesh_id = pl.DeviceIdType.MESH

    def exchange(phase, src, dst, n, me, where):
        ssem, rsem = sems.at[2 * phase], sems.at[2 * phase + 1]

        def outgoing(d):
            return pltpu.make_async_remote_copy(
                src_ref=src.at[d], dst_ref=dst.at[me], send_sem=ssem.at[d], recv_sem=rsem.at[me],
                device_id=where(d), device_id_type=mesh_id,
            )

        def incoming(e):
            return pltpu.make_async_remote_copy(
                src_ref=src.at[e], dst_ref=dst.at[e], send_sem=ssem.at[e], recv_sem=rsem.at[e],
                device_id=where(e), device_id_type=mesh_id,
            )

        def start(k, carry):
            outgoing(lax.rem(me + k, n)).start()
            return carry

        lax.fori_loop(1, n, start, 0)
        dst[me] = src[me]

        def wait(k, carry):
            d = lax.rem(me + k, n)
            outgoing(d).wait_send()
            incoming(d).wait_recv()
            return carry

        lax.fori_loop(1, n, wait, 0)

    in_plane = lambda d: (mz, d, sp)
    across = lambda d: (d, mq, sp)
    barrier = pltpu.get_barrier_semaphore()
    for k in range(1, nq):
        pl.semaphore_signal(
            barrier, 1, device_id=in_plane(lax.rem(mq + k, nq)), device_id_type=mesh_id
        )
    for k in range(1, nz):
        pl.semaphore_signal(
            barrier, 1, device_id=across(lax.rem(mz + k, nz)), device_id_type=mesh_id
        )
    pl.semaphore_wait(barrier, nq + nz - 2)
    exchange(0, send_ref, recv1, nq, mq, in_plane)

    def group_step(s, carry):
        ga, gb = carry
        pa[s] = ga
        pb[s] = gb
        a = recv1[s, :, 0]
        return a * ga, a * gb + recv1[s, :, 1]

    ones = jnp.ones(pa.shape[1:], jnp.float32)
    ga, gb = lax.fori_loop(0, nq, group_step, (ones, jnp.zeros_like(ones)))
    for z in range(nz):
        gsend[z, :, 0] = ga
        gsend[z, :, 1] = gb
    exchange(1, gsend, recv2, nz, mz, across)

    def entry_step(s, x):
        return jnp.where(s < mz, recv2[s, :, 0] * x + recv2[s, :, 1], x)

    group_in = lax.fori_loop(0, nz, entry_step, jnp.zeros(pa.shape[1:], jnp.float32))

    def spread_step(s, carry):
        xs[s] = pa[s] * group_in + pb[s]
        return carry

    lax.fori_loop(0, nq, spread_step, 0)
    exchange(3, xs, back1, nq, mq, in_plane)
    out_ref[...] = back1[...]


def from_tiles(tiles, shape):
    rows, cols = shape[0] * shape[1], shape[2]
    grid = tiles.reshape(rows // 8, cols // 128, 8, 128)
    return grid.transpose(0, 2, 1, 3).reshape(shape)


def per_device_body(coarse_points, coarse_decay, diffusion, forcing):
    slots, comps, row_count, col_count = coarse_points.shape
    space_count = lax.axis_size("space")
    me = lax.axis_index("space")


    state = coarse_points.reshape(slots * comps, row_count, col_count)
    ext_rows = row_count + 2 * HALO
    global_row = me * row_count - HALO + lax.broadcasted_iota(jnp.int32, (ext_rows, 1), 0)
    keep = ((global_row >= 0) & (global_row < space_count * row_count)).astype(jnp.float32)

    vmem = pl.BlockSpec(memory_space=pltpu.VMEM)
    tile_count = slots * comps * row_count * col_count // (2 * 8 * 128)
    both, shifts = pl.pallas_call(
        fine_kernel,
        out_shape=(
            jax.ShapeDtypeStruct((tile_count, 2, 8, 128), jnp.float32),
            jax.ShapeDtypeStruct((slots * comps, row_count, col_count), jnp.float32),
        ),
        in_specs=[vmem] * 5,
        out_specs=(vmem, vmem),
        scratch_shapes=[
            pltpu.VMEM((slots * comps, ext_rows, col_count), jnp.float32),
            pltpu.VMEM((ext_rows, col_count), jnp.float32),
            pltpu.VMEM((comps, ext_rows, col_count), jnp.float32),
            pltpu.SemaphoreType.DMA((12,)),
        ],
        compiler_params=pltpu.CompilerParams(collective_id=1, has_side_effects=True),
    )(state, diffusion, forcing, keep, coarse_decay.reshape(state.shape))
    scale = coarse_decay
    at_anchor = (lax.axis_index("tz") == 0) & (lax.axis_index("tq") == 0)
    scale0 = jnp.where(at_anchor, 0.0, coarse_decay[0])
    shifts = shifts.reshape(coarse_points.shape)
    shift0 = shifts[0]
    shift = shifts
    tiles = both.shape[0]
    q_count = lax.axis_size("tq")
    z_count = lax.axis_size("tz")
    c1 = tiles // q_count
    c2 = c1 // z_count
    both = both.reshape(q_count, c1, 2, 8, 128)
    x1 = (q_count, c1, 8, 128)
    x2 = (z_count, c2, 8, 128)
    vmem = pl.BlockSpec(memory_space=pltpu.VMEM)
    back = pl.pallas_call(
        exchange_kernel,
        out_shape=jax.ShapeDtypeStruct(x1, jnp.float32),
        in_specs=[vmem],
        out_specs=vmem,
        scratch_shapes=[
            pltpu.VMEM(both.shape, jnp.float32),
            pltpu.VMEM(x1, jnp.float32),
            pltpu.VMEM(x1, jnp.float32),
            pltpu.VMEM((z_count, c1, 2, 8, 128), jnp.float32),
            pltpu.VMEM((z_count, c1, 2, 8, 128), jnp.float32),
            pltpu.VMEM(x2, jnp.float32),
            pltpu.VMEM(x2, jnp.float32),
            pltpu.VMEM(x1, jnp.float32),
            pltpu.VMEM(x1, jnp.float32),
            pltpu.SemaphoreType.DMA((8, max(q_count, z_count))),
        ],
        compiler_params=pltpu.CompilerParams(collective_id=0, has_side_effects=True),
    )(both)
    back = back.reshape(tiles, 8, 128)
    entering = from_tiles(back, (comps, row_count, col_count))

    first = scale0 * entering + shift0
    second = scale[1] * first + shift[1]
    return jnp.stack([first, second], axis=0)


def solution(mesh):
    tm_count = mesh.shape["tm"]
    q_count = 8 if tm_count >= 16 and tm_count % 8 == 0 else 2
    grid = mesh.devices.reshape(tm_count // q_count, q_count, mesh.shape["space"])
    mesh = jax.sharding.Mesh(grid, ("tz", "tq", "space"))
    time_axes = ("tz", "tq")
    placed = (
        P(time_axes, None, "space", None),
        P(time_axes, None, "space", None),
        P("space", None),
        P(None, "space", None),
    )
    return jax.shard_map(
        per_device_body,
        mesh=mesh,
        in_specs=placed,
        out_specs=P(time_axes, None, "space", None),
        check_vma=False,
    )
```

```python
import jax
import jax.numpy as jnp
from jax import lax
from jax.experimental import pallas as pl
from jax.experimental.pallas import tpu as pltpu
from jax.sharding import PartitionSpec as P

M = 16
HALO = M


def fine_body(st_ref, dif_ref, frc_ref, keep_ref, cd_ref, tiles_ref, shift_ref, buf, dbuf, fbuf, sems):
    n_state = st_ref.shape[0]
    own = st_ref.shape[1]
    cols = st_ref.shape[2]
    rows = own + 2 * HALO
    n = lax.axis_size("space")
    me = lax.axis_index("space")
    place = (lax.axis_index("tz"), lax.axis_index("tq"))
    mesh_id = pl.DeviceIdType.MESH
    pairs = ((st_ref, buf), (dif_ref, dbuf), (frc_ref, fbuf))

    def rim_copy(k, src, dst, down, target):
        if down:
            s_rows, d_rows = pl.ds(own - HALO, HALO), pl.ds(0, HALO)
        else:
            s_rows, d_rows = pl.ds(0, HALO), pl.ds(HALO + own, HALO)
        if src.ndim == 3:
            src_v, dst_v = src.at[:, s_rows], dst.at[:, d_rows]
        else:
            src_v, dst_v = src.at[s_rows], dst.at[d_rows]
        slot = k + (0 if down else 3)
        return pltpu.make_async_remote_copy(
            src_ref=src_v, dst_ref=dst_v, send_sem=sems.at[slot], recv_sem=sems.at[6 + slot],
            device_id=place + (target,), device_id_type=mesh_id,
        )

    @pl.when(me < n - 1)
    def _():
        for k, (src, dst) in enumerate(pairs):
            rim_copy(k, src, dst, True, me + 1).start()

    @pl.when(me > 0)
    def _():
        for k, (src, dst) in enumerate(pairs):
            rim_copy(k, src, dst, False, me - 1).start()

    buf[:, HALO:HALO + own] = st_ref[...]
    dbuf[HALO:HALO + own] = dif_ref[...]
    fbuf[:, HALO:HALO + own] = frc_ref[...]

    @pl.when(me == 0)
    def _():
        buf[:, :HALO] = jnp.zeros((n_state, HALO, cols), jnp.float32)
        dbuf[:HALO] = jnp.zeros((HALO, cols), jnp.float32)
        fbuf[:, :HALO] = jnp.zeros((fbuf.shape[0], HALO, cols), jnp.float32)

    @pl.when(me == n - 1)
    def _():
        buf[:, HALO + own:] = jnp.zeros((n_state, HALO, cols), jnp.float32)
        dbuf[HALO + own:] = jnp.zeros((HALO, cols), jnp.float32)
        fbuf[:, HALO + own:] = jnp.zeros((fbuf.shape[0], HALO, cols), jnp.float32)

    @pl.when(me < n - 1)
    def _():
        for k, (src, dst) in enumerate(pairs):
            rim_copy(k, src, dst, True, me + 1).wait_send()
            rim_copy(k, src, dst, False, me + 1).wait_recv()

    @pl.when(me > 0)
    def _():
        for k, (src, dst) in enumerate(pairs):
            rim_copy(k, src, dst, False, me - 1).wait_send()
            rim_copy(k, src, dst, True, me - 1).wait_recv()

    def make_step(lo, hi):
        span = hi - lo

        def one_step(counter, carry):
            dif = dbuf[lo:hi]
            keep = keep_ref[lo:hi] > 0.5
            for slot in range(2):
                u = buf[2 * slot, lo:hi]
                v = buf[2 * slot + 1, lo:hi]
                new = []
                for comp, c in enumerate((u, v)):
                    next_row = pltpu.roll(c, span - 1, 0)
                    prev_row = pltpu.roll(c, 1, 0)
                    next_col = pltpu.roll(c, cols - 1, 1)
                    prev_col = pltpu.roll(c, 1, 1)
                    value = (
                        c
                        + dif * (next_row + prev_row + next_col + prev_col - 4.0 * c)
                        - 0.05 * (u * (next_row - prev_row) + v * (next_col - prev_col))
                        + 0.05 * fbuf[comp, lo:hi]
                    )
                    new.append(jnp.where(keep, value, 0.0))
                buf[2 * slot, lo:hi] = new[0]
                buf[2 * slot + 1, lo:hi] = new[1]
            return carry

        return one_step

    half = M // 2
    lax.fori_loop(0, half, make_step(0, rows), 0)
    lax.fori_loop(0, M - half, make_step(half, rows - half), 0)
    anchor = (lax.axis_index("tz") == 0) & (lax.axis_index("tq") == 0)
    comps = n_state // 2
    blocks = own // 8
    for comp in range(comps):
        d0, d1 = cd_ref[comp], cd_ref[comps + comp]
        c0, c1 = st_ref[comp], st_ref[comps + comp]
        plain0 = buf[comp, HALO:HALO + own] - d0 * c0
        sh1 = buf[comps + comp, HALO:HALO + own] - d1 * c1
        sh0 = jnp.where(anchor, d0 * c0 + plain0, plain0)
        s0 = jnp.where(anchor, 0.0, d0)
        shift_ref[comp] = sh0
        shift_ref[comps + comp] = sh1
        comp_scale = d1 * s0
        comp_shift = d1 * sh0 + sh1
        for rb in range(blocks):
            for cb in range(cols // 128):
                p = (comp * blocks + rb) * (cols // 128) + cb
                rs, cs = slice(rb * 8, rb * 8 + 8), slice(cb * 128, cb * 128 + 128)
                c1 = tiles_ref.shape[1]
                tiles_ref[p // c1, p % c1, 0] = comp_scale[rs, cs]
                tiles_ref[p // c1, p % c1, 1] = comp_shift[rs, cs]


def exchange_body(send_ref, out_ref, recv1, pa, pb, gsend, recv2, xg, back2, xs, back1, sems):
    nq = send_ref.shape[0]
    nz = gsend.shape[0]
    mz = lax.axis_index("tz")
    mq = lax.axis_index("tq")
    sp = lax.axis_index("space")
    mesh_id = pl.DeviceIdType.MESH

    def exchange(phase, src, dst, n, me, where):
        ssem, rsem = sems.at[2 * phase], sems.at[2 * phase + 1]

        def outgoing(d):
            return pltpu.make_async_remote_copy(
                src_ref=src.at[d], dst_ref=dst.at[me], send_sem=ssem.at[d], recv_sem=rsem.at[me],
                device_id=where(d), device_id_type=mesh_id,
            )

        def incoming(e):
            return pltpu.make_async_remote_copy(
                src_ref=src.at[e], dst_ref=dst.at[e], send_sem=ssem.at[e], recv_sem=rsem.at[e],
                device_id=where(e), device_id_type=mesh_id,
            )

        def start(k, carry):
            outgoing(lax.rem(me + k, n)).start()
            return carry

        lax.fori_loop(1, n, start, 0)
        dst[me] = src[me]

        def wait(k, carry):
            d = lax.rem(me + k, n)
            outgoing(d).wait_send()
            incoming(d).wait_recv()
            return carry

        lax.fori_loop(1, n, wait, 0)

    in_plane = lambda d: (mz, d, sp)
    across = lambda d: (d, mq, sp)
    exchange(0, send_ref, recv1, nq, mq, in_plane)

    def group_step(s, carry):
        ga, gb = carry
        pa[s] = ga
        pb[s] = gb
        a = recv1[s, :, 0]
        return a * ga, a * gb + recv1[s, :, 1]

    ones = jnp.ones(pa.shape[1:], jnp.float32)
    ga, gb = lax.fori_loop(0, nq, group_step, (ones, jnp.zeros_like(ones)))
    c2 = gsend.shape[1]
    for z in range(nz):
        gsend[z, :, 0] = ga[z * c2:(z + 1) * c2]
        gsend[z, :, 1] = gb[z * c2:(z + 1) * c2]
    exchange(1, gsend, recv2, nz, mz, across)

    def entry_step(s, x):
        xg[s] = x
        return recv2[s, :, 0] * x + recv2[s, :, 1]

    lax.fori_loop(0, nz, entry_step, jnp.zeros(xg.shape[1:], jnp.float32))
    exchange(2, xg, back2, nz, mz, across)
    group_in = back2[...].reshape(pa.shape[1:])

    def spread_step(s, carry):
        xs[s] = pa[s] * group_in + pb[s]
        return carry

    lax.fori_loop(0, nq, spread_step, 0)
    exchange(3, xs, back1, nq, mq, in_plane)
    out_ref[...] = back1[...]


def whole_kernel(st_ref, dif_ref, frc_ref, keep_ref, cd_ref, shift_ref, x_ref,
                 buf, dbuf, fbuf, fsems, send, recv1, pa, pb, gsend, recv2, xg, back2, xs, back1, xsems):
    n = lax.axis_size("space")
    me = lax.axis_index("space")
    mz = lax.axis_index("tz")
    mq = lax.axis_index("tq")
    nq = lax.axis_size("tq")
    nz = lax.axis_size("tz")
    mesh_id = pl.DeviceIdType.MESH
    barrier = pltpu.get_barrier_semaphore()

    @pl.when(me > 0)
    def _():
        pl.semaphore_signal(barrier, 1, device_id=(mz, mq, me - 1), device_id_type=mesh_id)

    @pl.when(me < n - 1)
    def _():
        pl.semaphore_signal(barrier, 1, device_id=(mz, mq, me + 1), device_id_type=mesh_id)

    for k in range(1, nq):
        pl.semaphore_signal(
            barrier, 1, device_id=(mz, lax.rem(mq + k, nq), me), device_id_type=mesh_id
        )
    for k in range(1, nz):
        pl.semaphore_signal(
            barrier, 1, device_id=(lax.rem(mz + k, nz), mq, me), device_id_type=mesh_id
        )
    peers = nq + nz - 2

    @pl.when((me > 0) & (me < n - 1))
    def _():
        pl.semaphore_wait(barrier, peers + 2)

    @pl.when((me == 0) | (me == n - 1))
    def _():
        pl.semaphore_wait(barrier, peers + 1)

    fine_body(st_ref, dif_ref, frc_ref, keep_ref, cd_ref, send, shift_ref, buf, dbuf, fbuf, fsems)
    exchange_body(send, x_ref, recv1, pa, pb, gsend, recv2, xg, back2, xs, back1, xsems)


def from_tiles(tiles, shape):
    rows, cols = shape[0] * shape[1], shape[2]
    grid = tiles.reshape(rows // 8, cols // 128, 8, 128)
    return grid.transpose(0, 2, 1, 3).reshape(shape)


def per_device_body(coarse_points, coarse_decay, diffusion, forcing):
    slots, comps, row_count, col_count = coarse_points.shape
    space_count = lax.axis_size("space")
    me = lax.axis_index("space")


    state = coarse_points.reshape(slots * comps, row_count, col_count)
    ext_rows = row_count + 2 * HALO
    global_row = me * row_count - HALO + lax.broadcasted_iota(jnp.int32, (ext_rows, 1), 0)
    keep = ((global_row >= 0) & (global_row < space_count * row_count)).astype(jnp.float32)

    vmem = pl.BlockSpec(memory_space=pltpu.VMEM)
    tiles = slots * comps * row_count * col_count // (2 * 8 * 128)
    q_count = lax.axis_size("tq")
    z_count = lax.axis_size("tz")
    c1 = tiles // q_count
    c2 = c1 // z_count
    x1 = (q_count, c1, 8, 128)
    x2 = (z_count, c2, 8, 128)
    send_shape = (q_count, c1, 2, 8, 128)
    shifts, back = pl.pallas_call(
        whole_kernel,
        out_shape=(
            jax.ShapeDtypeStruct((slots * comps, row_count, col_count), jnp.float32),
            jax.ShapeDtypeStruct(x1, jnp.float32),
        ),
        in_specs=[vmem] * 5,
        out_specs=(vmem, vmem),
        scratch_shapes=[
            pltpu.VMEM((slots * comps, ext_rows, col_count), jnp.float32),
            pltpu.VMEM((ext_rows, col_count), jnp.float32),
            pltpu.VMEM((comps, ext_rows, col_count), jnp.float32),
            pltpu.SemaphoreType.DMA((12,)),
            pltpu.VMEM(send_shape, jnp.float32),
            pltpu.VMEM(send_shape, jnp.float32),
            pltpu.VMEM(x1, jnp.float32),
            pltpu.VMEM(x1, jnp.float32),
            pltpu.VMEM((z_count, c2, 2, 8, 128), jnp.float32),
            pltpu.VMEM((z_count, c2, 2, 8, 128), jnp.float32),
            pltpu.VMEM(x2, jnp.float32),
            pltpu.VMEM(x2, jnp.float32),
            pltpu.VMEM(x1, jnp.float32),
            pltpu.VMEM(x1, jnp.float32),
            pltpu.SemaphoreType.DMA((8, max(q_count, z_count))),
        ],
        compiler_params=pltpu.CompilerParams(collective_id=0, has_side_effects=True),
    )(state, diffusion, forcing, keep, coarse_decay.reshape(state.shape))
    scale = coarse_decay
    at_anchor = (lax.axis_index("tz") == 0) & (lax.axis_index("tq") == 0)
    scale0 = jnp.where(at_anchor, 0.0, coarse_decay[0])
    shifts = shifts.reshape(coarse_points.shape)
    shift0 = shifts[0]
    shift = shifts
    back = back.reshape(tiles, 8, 128)
    entering = from_tiles(back, (comps, row_count, col_count))

    first = scale0 * entering + shift0
    second = scale[1] * first + shift[1]
    return jnp.stack([first, second], axis=0)


def solution(mesh):
    tm_count = mesh.shape["tm"]
    q_count = 8 if tm_count >= 16 and tm_count % 8 == 0 else 2
    grid = mesh.devices.reshape(tm_count // q_count, q_count, mesh.shape["space"])
    mesh = jax.sharding.Mesh(grid, ("tz", "tq", "space"))
    time_axes = ("tz", "tq")
    placed = (
        P(time_axes, None, "space", None),
        P(time_axes, None, "space", None),
        P("space", None),
        P(None, "space", None),
    )
    return jax.shard_map(
        per_device_body,
        mesh=mesh,
        in_specs=placed,
        out_specs=P(time_axes, None, "space", None),
        check_vma=False,
    )
```

```python
import jax
import jax.numpy as jnp
from jax import lax
from jax.experimental import pallas as pl
from jax.experimental.pallas import tpu as pltpu
from jax.sharding import PartitionSpec as P

M = 16
HALO = M


def fine_body(st_ref, dif_ref, frc_ref, keep_ref, cd_ref, tiles_ref, shift_ref, buf, dbuf, fbuf, sems):
    n_state = st_ref.shape[0]
    own = st_ref.shape[1]
    cols = st_ref.shape[2]
    rows = own + 2 * HALO
    n = lax.axis_size("space")
    me = lax.axis_index("space")
    place = (lax.axis_index("tz"), lax.axis_index("tq"))
    mesh_id = pl.DeviceIdType.MESH
    pairs = ((st_ref, buf), (dif_ref, dbuf), (frc_ref, fbuf))

    def rim_copy(k, src, dst, down, target):
        if down:
            s_rows, d_rows = pl.ds(own - HALO, HALO), pl.ds(0, HALO)
        else:
            s_rows, d_rows = pl.ds(0, HALO), pl.ds(HALO + own, HALO)
        if src.ndim == 3:
            src_v, dst_v = src.at[:, s_rows], dst.at[:, d_rows]
        else:
            src_v, dst_v = src.at[s_rows], dst.at[d_rows]
        slot = k + (0 if down else 3)
        return pltpu.make_async_remote_copy(
            src_ref=src_v, dst_ref=dst_v, send_sem=sems.at[slot], recv_sem=sems.at[6 + slot],
            device_id=place + (target,), device_id_type=mesh_id,
        )

    @pl.when(me < n - 1)
    def _():
        for k, (src, dst) in enumerate(pairs):
            rim_copy(k, src, dst, True, me + 1).start()

    @pl.when(me > 0)
    def _():
        for k, (src, dst) in enumerate(pairs):
            rim_copy(k, src, dst, False, me - 1).start()

    buf[:, HALO:HALO + own] = st_ref[...]
    dbuf[HALO:HALO + own] = dif_ref[...]
    fbuf[:, HALO:HALO + own] = frc_ref[...]

    @pl.when(me == 0)
    def _():
        buf[:, :HALO] = jnp.zeros((n_state, HALO, cols), jnp.float32)
        dbuf[:HALO] = jnp.zeros((HALO, cols), jnp.float32)
        fbuf[:, :HALO] = jnp.zeros((fbuf.shape[0], HALO, cols), jnp.float32)

    @pl.when(me == n - 1)
    def _():
        buf[:, HALO + own:] = jnp.zeros((n_state, HALO, cols), jnp.float32)
        dbuf[HALO + own:] = jnp.zeros((HALO, cols), jnp.float32)
        fbuf[:, HALO + own:] = jnp.zeros((fbuf.shape[0], HALO, cols), jnp.float32)

    @pl.when(me < n - 1)
    def _():
        for k, (src, dst) in enumerate(pairs):
            rim_copy(k, src, dst, True, me + 1).wait_send()
            rim_copy(k, src, dst, False, me + 1).wait_recv()

    @pl.when(me > 0)
    def _():
        for k, (src, dst) in enumerate(pairs):
            rim_copy(k, src, dst, False, me - 1).wait_send()
            rim_copy(k, src, dst, True, me - 1).wait_recv()

    def make_step(lo, hi):
        span = hi - lo

        def one_step(counter, carry):
            dif = dbuf[lo:hi]
            keep = keep_ref[lo:hi] > 0.5
            for slot in range(2):
                u = buf[2 * slot, lo:hi]
                v = buf[2 * slot + 1, lo:hi]
                new = []
                for comp, c in enumerate((u, v)):
                    next_row = pltpu.roll(c, span - 1, 0)
                    prev_row = pltpu.roll(c, 1, 0)
                    next_col = pltpu.roll(c, cols - 1, 1)
                    prev_col = pltpu.roll(c, 1, 1)
                    value = (
                        c
                        + dif * (next_row + prev_row + next_col + prev_col - 4.0 * c)
                        - 0.05 * (u * (next_row - prev_row) + v * (next_col - prev_col))
                        + 0.05 * fbuf[comp, lo:hi]
                    )
                    new.append(jnp.where(keep, value, 0.0))
                buf[2 * slot, lo:hi] = new[0]
                buf[2 * slot + 1, lo:hi] = new[1]
            return carry

        return one_step

    half = M // 2
    lax.fori_loop(0, half, make_step(0, rows), 0)
    lax.fori_loop(0, M - half, make_step(half, rows - half), 0)
    anchor = (lax.axis_index("tz") == 0) & (lax.axis_index("tq") == 0)
    comps = n_state // 2
    blocks = own // 8
    for comp in range(comps):
        d0, d1 = cd_ref[comp], cd_ref[comps + comp]
        c0, c1 = st_ref[comp], st_ref[comps + comp]
        plain0 = buf[comp, HALO:HALO + own] - d0 * c0
        sh1 = buf[comps + comp, HALO:HALO + own] - d1 * c1
        sh0 = jnp.where(anchor, d0 * c0 + plain0, plain0)
        shift_ref[comp] = sh0
        shift_ref[comps + comp] = sh1
        comp_shift = d1 * sh0 + sh1
        for rb in range(blocks):
            for cb in range(cols // 128):
                p = (comp * blocks + rb) * (cols // 128) + cb
                rs, cs = slice(rb * 8, rb * 8 + 8), slice(cb * 128, cb * 128 + 128)
                c1 = tiles_ref.shape[1]
                tiles_ref[p // c1, p % c1, 1] = comp_shift[rs, cs]


def exchange_body(send_ref, out_ref, recv1, pa, pb, gsend, recv2, xg, back2, xs, back1, sems, first=True):
    nq = send_ref.shape[0]
    nz = gsend.shape[0]
    mz = lax.axis_index("tz")
    mq = lax.axis_index("tq")
    sp = lax.axis_index("space")
    mesh_id = pl.DeviceIdType.MESH

    def exchange(phase, src, dst, n, me, where):
        ssem, rsem = sems.at[2 * phase], sems.at[2 * phase + 1]

        def outgoing(d):
            return pltpu.make_async_remote_copy(
                src_ref=src.at[d], dst_ref=dst.at[me], send_sem=ssem.at[d], recv_sem=rsem.at[me],
                device_id=where(d), device_id_type=mesh_id,
            )

        def incoming(e):
            return pltpu.make_async_remote_copy(
                src_ref=src.at[e], dst_ref=dst.at[e], send_sem=ssem.at[e], recv_sem=rsem.at[e],
                device_id=where(e), device_id_type=mesh_id,
            )

        def start(k, carry):
            outgoing(lax.rem(me + k, n)).start()
            return carry

        lax.fori_loop(1, n, start, 0)
        dst[me] = src[me]

        def wait(k, carry):
            d = lax.rem(me + k, n)
            outgoing(d).wait_send()
            incoming(d).wait_recv()
            return carry

        lax.fori_loop(1, n, wait, 0)

    in_plane = lambda d: (mz, d, sp)
    across = lambda d: (d, mq, sp)
    if first:
        exchange(0, send_ref, recv1, nq, mq, in_plane)

    def group_step(s, carry):
        ga, gb = carry
        pa[s] = ga
        pb[s] = gb
        a = recv1[s, :, 0]
        return a * ga, a * gb + recv1[s, :, 1]

    ones = jnp.ones(pa.shape[1:], jnp.float32)
    ga, gb = lax.fori_loop(0, nq, group_step, (ones, jnp.zeros_like(ones)))
    c2 = gsend.shape[1]
    for z in range(nz):
        gsend[z, :, 0] = ga[z * c2:(z + 1) * c2]
        gsend[z, :, 1] = gb[z * c2:(z + 1) * c2]
    exchange(1, gsend, recv2, nz, mz, across)

    def entry_step(s, x):
        xg[s] = x
        return recv2[s, :, 0] * x + recv2[s, :, 1]

    lax.fori_loop(0, nz, entry_step, jnp.zeros(xg.shape[1:], jnp.float32))
    exchange(2, xg, back2, nz, mz, across)
    group_in = back2[...].reshape(pa.shape[1:])

    def spread_step(s, carry):
        xs[s] = pa[s] * group_in + pb[s]
        return carry

    lax.fori_loop(0, nq, spread_step, 0)
    exchange(3, xs, back1, nq, mq, in_plane)
    out_ref[...] = back1[...]


def whole_kernel(st_ref, dif_ref, frc_ref, keep_ref, cd_ref, shift_ref, x_ref,
                 buf, dbuf, fbuf, fsems, send, recv1, pa, pb, gsend, recv2, xg, back2, xs, back1, xsems):
    n = lax.axis_size("space")
    me = lax.axis_index("space")
    mz = lax.axis_index("tz")
    mq = lax.axis_index("tq")
    nq = lax.axis_size("tq")
    nz = lax.axis_size("tz")
    mesh_id = pl.DeviceIdType.MESH
    barrier = pltpu.get_barrier_semaphore()

    @pl.when(me > 0)
    def _():
        pl.semaphore_signal(barrier, 1, device_id=(mz, mq, me - 1), device_id_type=mesh_id)

    @pl.when(me < n - 1)
    def _():
        pl.semaphore_signal(barrier, 1, device_id=(mz, mq, me + 1), device_id_type=mesh_id)

    for k in range(1, nq):
        pl.semaphore_signal(
            barrier, 1, device_id=(mz, lax.rem(mq + k, nq), me), device_id_type=mesh_id
        )
    for k in range(1, nz):
        pl.semaphore_signal(
            barrier, 1, device_id=(lax.rem(mz + k, nz), mq, me), device_id_type=mesh_id
        )
    peers = nq + nz - 2

    @pl.when((me > 0) & (me < n - 1))
    def _():
        pl.semaphore_wait(barrier, peers + 2)

    @pl.when((me == 0) | (me == n - 1))
    def _():
        pl.semaphore_wait(barrier, peers + 1)

    def half_copy(h, d_src, d_dst, peer):
        return pltpu.make_async_remote_copy(
            src_ref=send.at[d_src, :, h], dst_ref=recv1.at[d_dst, :, h],
            send_sem=xsems.at[8 + 2 * h, d_src], recv_sem=xsems.at[9 + 2 * h, d_dst],
            device_id=(mz, peer, me), device_id_type=mesh_id,
        )

    def start_half(h):
        def start(k, carry):
            d = lax.rem(mq + k, nq)
            half_copy(h, d, mq, d).start()
            return carry

        lax.fori_loop(1, nq, start, 0)
        recv1[mq, :, h] = send[mq, :, h]

    def wait_half(h):
        def wait(k, carry):
            d = lax.rem(mq + k, nq)
            half_copy(h, d, mq, d).wait_send()
            half_copy(h, d, d, d).wait_recv()
            return carry

        lax.fori_loop(1, nq, wait, 0)

    anchor = (mz == 0) & (mq == 0)
    n_state, own, cols = cd_ref.shape
    comps = n_state // 2
    blocks = own // 8
    c1 = send.shape[1]
    for comp in range(comps):
        s0 = jnp.where(anchor, 0.0, cd_ref[comp])
        comp_scale = cd_ref[comps + comp] * s0
        for rb in range(blocks):
            for cb in range(cols // 128):
                p = (comp * blocks + rb) * (cols // 128) + cb
                rs, cs = slice(rb * 8, rb * 8 + 8), slice(cb * 128, cb * 128 + 128)
                send[p // c1, p % c1, 0] = comp_scale[rs, cs]
    start_half(0)
    fine_body(st_ref, dif_ref, frc_ref, keep_ref, cd_ref, send, shift_ref, buf, dbuf, fbuf, fsems)
    start_half(1)
    wait_half(0)
    wait_half(1)
    exchange_body(send, x_ref, recv1, pa, pb, gsend, recv2, xg, back2, xs, back1, xsems, first=False)


def from_tiles(tiles, shape):
    rows, cols = shape[0] * shape[1], shape[2]
    grid = tiles.reshape(rows // 8, cols // 128, 8, 128)
    return grid.transpose(0, 2, 1, 3).reshape(shape)


def per_device_body(coarse_points, coarse_decay, diffusion, forcing):
    slots, comps, row_count, col_count = coarse_points.shape
    space_count = lax.axis_size("space")
    me = lax.axis_index("space")


    state = coarse_points.reshape(slots * comps, row_count, col_count)
    ext_rows = row_count + 2 * HALO
    global_row = me * row_count - HALO + lax.broadcasted_iota(jnp.int32, (ext_rows, 1), 0)
    keep = ((global_row >= 0) & (global_row < space_count * row_count)).astype(jnp.float32)

    vmem = pl.BlockSpec(memory_space=pltpu.VMEM)
    tiles = slots * comps * row_count * col_count // (2 * 8 * 128)
    q_count = lax.axis_size("tq")
    z_count = lax.axis_size("tz")
    c1 = tiles // q_count
    c2 = c1 // z_count
    x1 = (q_count, c1, 8, 128)
    x2 = (z_count, c2, 8, 128)
    send_shape = (q_count, c1, 2, 8, 128)
    shifts, back = pl.pallas_call(
        whole_kernel,
        out_shape=(
            jax.ShapeDtypeStruct((slots * comps, row_count, col_count), jnp.float32),
            jax.ShapeDtypeStruct(x1, jnp.float32),
        ),
        in_specs=[vmem] * 5,
        out_specs=(vmem, vmem),
        scratch_shapes=[
            pltpu.VMEM((slots * comps, ext_rows, col_count), jnp.float32),
            pltpu.VMEM((ext_rows, col_count), jnp.float32),
            pltpu.VMEM((comps, ext_rows, col_count), jnp.float32),
            pltpu.SemaphoreType.DMA((12,)),
            pltpu.VMEM(send_shape, jnp.float32),
            pltpu.VMEM(send_shape, jnp.float32),
            pltpu.VMEM(x1, jnp.float32),
            pltpu.VMEM(x1, jnp.float32),
            pltpu.VMEM((z_count, c2, 2, 8, 128), jnp.float32),
            pltpu.VMEM((z_count, c2, 2, 8, 128), jnp.float32),
            pltpu.VMEM(x2, jnp.float32),
            pltpu.VMEM(x2, jnp.float32),
            pltpu.VMEM(x1, jnp.float32),
            pltpu.VMEM(x1, jnp.float32),
            pltpu.SemaphoreType.DMA((12, max(q_count, z_count))),
        ],
        compiler_params=pltpu.CompilerParams(collective_id=0, has_side_effects=True),
    )(state, diffusion, forcing, keep, coarse_decay.reshape(state.shape))
    scale = coarse_decay
    at_anchor = (lax.axis_index("tz") == 0) & (lax.axis_index("tq") == 0)
    scale0 = jnp.where(at_anchor, 0.0, coarse_decay[0])
    shifts = shifts.reshape(coarse_points.shape)
    shift0 = shifts[0]
    shift = shifts
    back = back.reshape(tiles, 8, 128)
    entering = from_tiles(back, (comps, row_count, col_count))

    first = scale0 * entering + shift0
    second = scale[1] * first + shift[1]
    return jnp.stack([first, second], axis=0)


def solution(mesh):
    tm_count = mesh.shape["tm"]
    q_count = 8 if tm_count >= 16 and tm_count % 8 == 0 else 2
    grid = mesh.devices.reshape(tm_count // q_count, q_count, mesh.shape["space"])
    mesh = jax.sharding.Mesh(grid, ("tz", "tq", "space"))
    time_axes = ("tz", "tq")
    placed = (
        P(time_axes, None, "space", None),
        P(time_axes, None, "space", None),
        P("space", None),
        P(None, "space", None),
    )
    return jax.shard_map(
        per_device_body,
        mesh=mesh,
        in_specs=placed,
        out_specs=P(time_axes, None, "space", None),
        check_vma=False,
    )
```

```python
import jax
import jax.numpy as jnp
from jax import lax
from jax.experimental import pallas as pl
from jax.experimental.pallas import tpu as pltpu
from jax.sharding import PartitionSpec as P

M = 16
HALO = M


def fine_body(st_ref, dif_ref, frc_ref, keep_ref, cd_ref, tiles_ref, shift_ref, buf, dbuf, fbuf, sems, early=None):
    n_state = st_ref.shape[0]
    own = st_ref.shape[1]
    cols = st_ref.shape[2]
    rows = own + 2 * HALO
    n = lax.axis_size("space")
    me = lax.axis_index("space")
    place = (lax.axis_index("tz"), lax.axis_index("tq"))
    mesh_id = pl.DeviceIdType.MESH
    pairs = ((st_ref, buf), (dif_ref, dbuf), (frc_ref, fbuf))

    def rim_copy(k, src, dst, down, target):
        if down:
            s_rows, d_rows = pl.ds(own - HALO, HALO), pl.ds(0, HALO)
        else:
            s_rows, d_rows = pl.ds(0, HALO), pl.ds(HALO + own, HALO)
        if src.ndim == 3:
            src_v, dst_v = src.at[:, s_rows], dst.at[:, d_rows]
        else:
            src_v, dst_v = src.at[s_rows], dst.at[d_rows]
        slot = k + (0 if down else 3)
        return pltpu.make_async_remote_copy(
            src_ref=src_v, dst_ref=dst_v, send_sem=sems.at[slot], recv_sem=sems.at[6 + slot],
            device_id=place + (target,), device_id_type=mesh_id,
        )

    @pl.when(me < n - 1)
    def _():
        for k, (src, dst) in enumerate(pairs):
            rim_copy(k, src, dst, True, me + 1).start()

    @pl.when(me > 0)
    def _():
        for k, (src, dst) in enumerate(pairs):
            rim_copy(k, src, dst, False, me - 1).start()

    if early is not None:
        early()
    buf[:, HALO:HALO + own] = st_ref[...]
    dbuf[HALO:HALO + own] = dif_ref[...]
    fbuf[:, HALO:HALO + own] = frc_ref[...]

    @pl.when(me == 0)
    def _():
        buf[:, :HALO] = jnp.zeros((n_state, HALO, cols), jnp.float32)
        dbuf[:HALO] = jnp.zeros((HALO, cols), jnp.float32)
        fbuf[:, :HALO] = jnp.zeros((fbuf.shape[0], HALO, cols), jnp.float32)

    @pl.when(me == n - 1)
    def _():
        buf[:, HALO + own:] = jnp.zeros((n_state, HALO, cols), jnp.float32)
        dbuf[HALO + own:] = jnp.zeros((HALO, cols), jnp.float32)
        fbuf[:, HALO + own:] = jnp.zeros((fbuf.shape[0], HALO, cols), jnp.float32)

    @pl.when(me < n - 1)
    def _():
        for k, (src, dst) in enumerate(pairs):
            rim_copy(k, src, dst, True, me + 1).wait_send()
            rim_copy(k, src, dst, False, me + 1).wait_recv()

    @pl.when(me > 0)
    def _():
        for k, (src, dst) in enumerate(pairs):
            rim_copy(k, src, dst, False, me - 1).wait_send()
            rim_copy(k, src, dst, True, me - 1).wait_recv()

    fbuf[...] = 0.05 * fbuf[...]

    def make_step(lo, hi):
        span = hi - lo

        def one_step(counter, carry):
            dif = dbuf[lo:hi]
            keep = keep_ref[lo:hi] > 0.5
            for slot in range(2):
                u = buf[2 * slot, lo:hi]
                v = buf[2 * slot + 1, lo:hi]
                new = []
                for comp, c in enumerate((u, v)):
                    next_row = pltpu.roll(c, span - 1, 0)
                    prev_row = pltpu.roll(c, 1, 0)
                    next_col = pltpu.roll(c, cols - 1, 1)
                    prev_col = pltpu.roll(c, 1, 1)
                    value = (
                        c
                        + dif * (next_row + prev_row + next_col + prev_col - 4.0 * c)
                        - 0.05 * (u * (next_row - prev_row) + v * (next_col - prev_col))
                        + fbuf[comp, lo:hi]
                    )
                    new.append(jnp.where(keep, value, 0.0))
                buf[2 * slot, lo:hi] = new[0]
                buf[2 * slot + 1, lo:hi] = new[1]
            return carry

        return one_step

    half = M // 2
    lax.fori_loop(0, half, make_step(0, rows), 0)
    lax.fori_loop(0, M - half, make_step(half, rows - half), 0)
    anchor = (lax.axis_index("tz") == 0) & (lax.axis_index("tq") == 0)
    comps = n_state // 2
    blocks = own // 8
    for comp in range(comps):
        d0, d1 = cd_ref[comp], cd_ref[comps + comp]
        c0, c1 = st_ref[comp], st_ref[comps + comp]
        plain0 = buf[comp, HALO:HALO + own] - d0 * c0
        sh1 = buf[comps + comp, HALO:HALO + own] - d1 * c1
        sh0 = jnp.where(anchor, d0 * c0 + plain0, plain0)
        shift_ref[comp] = sh0
        shift_ref[comps + comp] = sh1
        comp_shift = d1 * sh0 + sh1
        for rb in range(blocks):
            for cb in range(cols // 128):
                p = (comp * blocks + rb) * (cols // 128) + cb
                rs, cs = slice(rb * 8, rb * 8 + 8), slice(cb * 128, cb * 128 + 128)
                c1 = tiles_ref.shape[1]
                tiles_ref[p // c1, p % c1, 1] = comp_shift[rs, cs]


def exchange_body(send_ref, out_ref, recv1, pa, pb, gsend, recv2, xg, back2, xs, back1, sems, first=True):
    nq = send_ref.shape[0]
    nz = gsend.shape[0]
    mz = lax.axis_index("tz")
    mq = lax.axis_index("tq")
    sp = lax.axis_index("space")
    mesh_id = pl.DeviceIdType.MESH

    def exchange(phase, src, dst, n, me, where):
        ssem, rsem = sems.at[2 * phase], sems.at[2 * phase + 1]

        def outgoing(d):
            return pltpu.make_async_remote_copy(
                src_ref=src.at[d], dst_ref=dst.at[me], send_sem=ssem.at[d], recv_sem=rsem.at[me],
                device_id=where(d), device_id_type=mesh_id,
            )

        def incoming(e):
            return pltpu.make_async_remote_copy(
                src_ref=src.at[e], dst_ref=dst.at[e], send_sem=ssem.at[e], recv_sem=rsem.at[e],
                device_id=where(e), device_id_type=mesh_id,
            )

        def start(k, carry):
            outgoing(lax.rem(me + k, n)).start()
            return carry

        lax.fori_loop(1, n, start, 0)
        dst[me] = src[me]

        def wait(k, carry):
            d = lax.rem(me + k, n)
            outgoing(d).wait_send()
            incoming(d).wait_recv()
            return carry

        lax.fori_loop(1, n, wait, 0)

    in_plane = lambda d: (mz, d, sp)
    across = lambda d: (d, mq, sp)
    if first:
        exchange(0, send_ref, recv1, nq, mq, in_plane)

    def group_step(s, carry):
        ga, gb = carry
        pa[s] = ga
        pb[s] = gb
        a = recv1[s, :, 0]
        return a * ga, a * gb + recv1[s, :, 1]

    ones = jnp.ones(pa.shape[1:], jnp.float32)
    ga, gb = lax.fori_loop(0, nq, group_step, (ones, jnp.zeros_like(ones)))
    c2 = gsend.shape[1]
    for z in range(nz):
        gsend[z, :, 0] = ga[z * c2:(z + 1) * c2]
        gsend[z, :, 1] = gb[z * c2:(z + 1) * c2]
    exchange(1, gsend, recv2, nz, mz, across)

    def entry_step(s, x):
        xg[s] = x
        return recv2[s, :, 0] * x + recv2[s, :, 1]

    lax.fori_loop(0, nz, entry_step, jnp.zeros(xg.shape[1:], jnp.float32))
    exchange(2, xg, back2, nz, mz, across)
    group_in = back2[...].reshape(pa.shape[1:])

    def spread_step(s, carry):
        xs[s] = pa[s] * group_in + pb[s]
        return carry

    lax.fori_loop(0, nq, spread_step, 0)
    exchange(3, xs, back1, nq, mq, in_plane)
    out_ref[...] = back1[...]


def whole_kernel(st_ref, dif_ref, frc_ref, keep_ref, cd_ref, shift_ref, x_ref,
                 buf, dbuf, fbuf, fsems, send, recv1, pa, pb, gsend, recv2, xg, back2, xs, back1, xsems):
    n = lax.axis_size("space")
    me = lax.axis_index("space")
    mz = lax.axis_index("tz")
    mq = lax.axis_index("tq")
    nq = lax.axis_size("tq")
    nz = lax.axis_size("tz")
    mesh_id = pl.DeviceIdType.MESH
    barrier = pltpu.get_barrier_semaphore()

    @pl.when(me > 0)
    def _():
        pl.semaphore_signal(barrier, 1, device_id=(mz, mq, me - 1), device_id_type=mesh_id)

    @pl.when(me < n - 1)
    def _():
        pl.semaphore_signal(barrier, 1, device_id=(mz, mq, me + 1), device_id_type=mesh_id)

    for k in range(1, nq):
        pl.semaphore_signal(
            barrier, 1, device_id=(mz, lax.rem(mq + k, nq), me), device_id_type=mesh_id
        )
    for k in range(1, nz):
        pl.semaphore_signal(
            barrier, 1, device_id=(lax.rem(mz + k, nz), mq, me), device_id_type=mesh_id
        )
    peers = nq + nz - 2

    @pl.when((me > 0) & (me < n - 1))
    def _():
        pl.semaphore_wait(barrier, peers + 2)

    @pl.when((me == 0) | (me == n - 1))
    def _():
        pl.semaphore_wait(barrier, peers + 1)

    def half_copy(h, d_src, d_dst, peer):
        return pltpu.make_async_remote_copy(
            src_ref=send.at[d_src, :, h], dst_ref=recv1.at[d_dst, :, h],
            send_sem=xsems.at[8 + 2 * h, d_src], recv_sem=xsems.at[9 + 2 * h, d_dst],
            device_id=(mz, peer, me), device_id_type=mesh_id,
        )

    def start_half(h):
        def start(k, carry):
            d = lax.rem(mq + k, nq)
            half_copy(h, d, mq, d).start()
            return carry

        lax.fori_loop(1, nq, start, 0)
        recv1[mq, :, h] = send[mq, :, h]

    def wait_half(h):
        def wait(k, carry):
            d = lax.rem(mq + k, nq)
            half_copy(h, d, mq, d).wait_send()
            half_copy(h, d, d, d).wait_recv()
            return carry

        lax.fori_loop(1, nq, wait, 0)

    anchor = (mz == 0) & (mq == 0)
    n_state, own, cols = cd_ref.shape
    comps = n_state // 2
    blocks = own // 8
    c1 = send.shape[1]

    def early():
        for comp in range(comps):
            s0 = jnp.where(anchor, 0.0, cd_ref[comp])
            comp_scale = cd_ref[comps + comp] * s0
            for rb in range(blocks):
                for cb in range(cols // 128):
                    p = (comp * blocks + rb) * (cols // 128) + cb
                    rs, cs = slice(rb * 8, rb * 8 + 8), slice(cb * 128, cb * 128 + 128)
                    send[p // c1, p % c1, 0] = comp_scale[rs, cs]
        start_half(0)

    fine_body(st_ref, dif_ref, frc_ref, keep_ref, cd_ref, send, shift_ref, buf, dbuf, fbuf, fsems,
              early=early)
    start_half(1)
    wait_half(0)
    wait_half(1)
    exchange_body(send, x_ref, recv1, pa, pb, gsend, recv2, xg, back2, xs, back1, xsems, first=False)


def from_tiles(tiles, shape):
    rows, cols = shape[0] * shape[1], shape[2]
    grid = tiles.reshape(rows // 8, cols // 128, 8, 128)
    return grid.transpose(0, 2, 1, 3).reshape(shape)


def per_device_body(coarse_points, coarse_decay, diffusion, forcing):
    slots, comps, row_count, col_count = coarse_points.shape
    space_count = lax.axis_size("space")
    me = lax.axis_index("space")


    state = coarse_points.reshape(slots * comps, row_count, col_count)
    ext_rows = row_count + 2 * HALO
    global_row = me * row_count - HALO + lax.broadcasted_iota(jnp.int32, (ext_rows, 1), 0)
    keep = ((global_row >= 0) & (global_row < space_count * row_count)).astype(jnp.float32)

    vmem = pl.BlockSpec(memory_space=pltpu.VMEM)
    tiles = slots * comps * row_count * col_count // (2 * 8 * 128)
    q_count = lax.axis_size("tq")
    z_count = lax.axis_size("tz")
    c1 = tiles // q_count
    c2 = c1 // z_count
    x1 = (q_count, c1, 8, 128)
    x2 = (z_count, c2, 8, 128)
    send_shape = (q_count, c1, 2, 8, 128)
    shifts, back = pl.pallas_call(
        whole_kernel,
        out_shape=(
            jax.ShapeDtypeStruct((slots * comps, row_count, col_count), jnp.float32),
            jax.ShapeDtypeStruct(x1, jnp.float32),
        ),
        in_specs=[vmem] * 5,
        out_specs=(vmem, vmem),
        scratch_shapes=[
            pltpu.VMEM((slots * comps, ext_rows, col_count), jnp.float32),
            pltpu.VMEM((ext_rows, col_count), jnp.float32),
            pltpu.VMEM((comps, ext_rows, col_count), jnp.float32),
            pltpu.SemaphoreType.DMA((12,)),
            pltpu.VMEM(send_shape, jnp.float32),
            pltpu.VMEM(send_shape, jnp.float32),
            pltpu.VMEM(x1, jnp.float32),
            pltpu.VMEM(x1, jnp.float32),
            pltpu.VMEM((z_count, c2, 2, 8, 128), jnp.float32),
            pltpu.VMEM((z_count, c2, 2, 8, 128), jnp.float32),
            pltpu.VMEM(x2, jnp.float32),
            pltpu.VMEM(x2, jnp.float32),
            pltpu.VMEM(x1, jnp.float32),
            pltpu.VMEM(x1, jnp.float32),
            pltpu.SemaphoreType.DMA((12, max(q_count, z_count))),
        ],
        compiler_params=pltpu.CompilerParams(collective_id=0, has_side_effects=True),
    )(state, diffusion, forcing, keep, coarse_decay.reshape(state.shape))
    scale = coarse_decay
    at_anchor = (lax.axis_index("tz") == 0) & (lax.axis_index("tq") == 0)
    scale0 = jnp.where(at_anchor, 0.0, coarse_decay[0])
    shifts = shifts.reshape(coarse_points.shape)
    shift0 = shifts[0]
    shift = shifts
    back = back.reshape(tiles, 8, 128)
    entering = from_tiles(back, (comps, row_count, col_count))

    first = scale0 * entering + shift0
    second = scale[1] * first + shift[1]
    return jnp.stack([first, second], axis=0)


def solution(mesh):
    tm_count = mesh.shape["tm"]
    q_count = 8 if tm_count >= 16 and tm_count % 8 == 0 else 2
    grid = mesh.devices.reshape(tm_count // q_count, q_count, mesh.shape["space"])
    mesh = jax.sharding.Mesh(grid, ("tz", "tq", "space"))
    time_axes = ("tz", "tq")
    placed = (
        P(time_axes, None, "space", None),
        P(time_axes, None, "space", None),
        P("space", None),
        P(None, "space", None),
    )
    return jax.shard_map(
        per_device_body,
        mesh=mesh,
        in_specs=placed,
        out_specs=P(time_axes, None, "space", None),
        check_vma=False,
    )
```

```python
import jax
import jax.numpy as jnp
from jax import lax
from jax.experimental import pallas as pl
from jax.experimental.pallas import tpu as pltpu
from jax.sharding import PartitionSpec as P

M = 16
HALO = M


def fine_body(st_ref, dif_ref, frc_ref, keep_ref, cd_ref, tiles_ref, shift_ref, buf, dbuf, fbuf, sems):
    n_state = st_ref.shape[0]
    own = st_ref.shape[1]
    cols = st_ref.shape[2]
    rows = own + 2 * HALO
    n = lax.axis_size("space")
    me = lax.axis_index("space")
    place = (lax.axis_index("tz"), lax.axis_index("tq"))
    mesh_id = pl.DeviceIdType.MESH
    pairs = ((st_ref, buf), (dif_ref, dbuf), (frc_ref, fbuf))

    def rim_copy(k, src, dst, down, target):
        if down:
            s_rows, d_rows = pl.ds(own - HALO, HALO), pl.ds(0, HALO)
        else:
            s_rows, d_rows = pl.ds(0, HALO), pl.ds(HALO + own, HALO)
        if src.ndim == 3:
            src_v, dst_v = src.at[:, s_rows], dst.at[:, d_rows]
        else:
            src_v, dst_v = src.at[s_rows], dst.at[d_rows]
        slot = k + (0 if down else 3)
        return pltpu.make_async_remote_copy(
            src_ref=src_v, dst_ref=dst_v, send_sem=sems.at[slot], recv_sem=sems.at[6 + slot],
            device_id=place + (target,), device_id_type=mesh_id,
        )

    @pl.when(me < n - 1)
    def _():
        for k, (src, dst) in enumerate(pairs):
            rim_copy(k, src, dst, True, me + 1).start()

    @pl.when(me > 0)
    def _():
        for k, (src, dst) in enumerate(pairs):
            rim_copy(k, src, dst, False, me - 1).start()

    buf[:, HALO:HALO + own] = st_ref[...]
    dbuf[HALO:HALO + own] = dif_ref[...]
    fbuf[:, HALO:HALO + own] = frc_ref[...]

    @pl.when(me == 0)
    def _():
        buf[:, :HALO] = jnp.zeros((n_state, HALO, cols), jnp.float32)
        dbuf[:HALO] = jnp.zeros((HALO, cols), jnp.float32)
        fbuf[:, :HALO] = jnp.zeros((fbuf.shape[0], HALO, cols), jnp.float32)

    @pl.when(me == n - 1)
    def _():
        buf[:, HALO + own:] = jnp.zeros((n_state, HALO, cols), jnp.float32)
        dbuf[HALO + own:] = jnp.zeros((HALO, cols), jnp.float32)
        fbuf[:, HALO + own:] = jnp.zeros((fbuf.shape[0], HALO, cols), jnp.float32)

    @pl.when(me < n - 1)
    def _():
        for k, (src, dst) in enumerate(pairs):
            rim_copy(k, src, dst, True, me + 1).wait_send()
            rim_copy(k, src, dst, False, me + 1).wait_recv()

    @pl.when(me > 0)
    def _():
        for k, (src, dst) in enumerate(pairs):
            rim_copy(k, src, dst, False, me - 1).wait_send()
            rim_copy(k, src, dst, True, me - 1).wait_recv()

    def make_step(lo, hi):
        span = hi - lo

        def one_step(counter, carry):
            dif = dbuf[lo:hi]
            keep = keep_ref[lo:hi] > 0.5
            for slot in range(2):
                u = buf[2 * slot, lo:hi]
                v = buf[2 * slot + 1, lo:hi]
                new = []
                for comp, c in enumerate((u, v)):
                    next_row = pltpu.roll(c, span - 1, 0)
                    prev_row = pltpu.roll(c, 1, 0)
                    next_col = pltpu.roll(c, cols - 1, 1)
                    prev_col = pltpu.roll(c, 1, 1)
                    value = (
                        c
                        + dif * (next_row + prev_row + next_col + prev_col - 4.0 * c)
                        - 0.05 * (u * (next_row - prev_row) + v * (next_col - prev_col))
                        + 0.05 * fbuf[comp, lo:hi]
                    )
                    new.append(jnp.where(keep, value, 0.0))
                buf[2 * slot, lo:hi] = new[0]
                buf[2 * slot + 1, lo:hi] = new[1]
            return carry

        return one_step

    half = M // 2
    lax.fori_loop(0, half, make_step(0, rows), 0)
    lax.fori_loop(0, M - half, make_step(half, rows - half), 0)
    anchor = (lax.axis_index("tz") == 0) & (lax.axis_index("tq") == 0)
    comps = n_state // 2
    blocks = own // 8
    for comp in range(comps):
        d0, d1 = cd_ref[comp], cd_ref[comps + comp]
        c0, c1 = st_ref[comp], st_ref[comps + comp]
        plain0 = buf[comp, HALO:HALO + own] - d0 * c0
        sh1 = buf[comps + comp, HALO:HALO + own] - d1 * c1
        sh0 = jnp.where(anchor, d0 * c0 + plain0, plain0)
        shift_ref[comp] = sh0
        shift_ref[comps + comp] = sh1
        comp_shift = d1 * sh0 + sh1
        for rb in range(blocks):
            for cb in range(cols // 128):
                p = (comp * blocks + rb) * (cols // 128) + cb
                rs, cs = slice(rb * 8, rb * 8 + 8), slice(cb * 128, cb * 128 + 128)
                c1 = tiles_ref.shape[1]
                tiles_ref[p // c1, p % c1, 1] = comp_shift[rs, cs]


def exchange_body(send_ref, out_ref, recv1, pa, pb, gsend, recv2, xg, back2, xs, back1, sems, first=True):
    nq = send_ref.shape[0]
    nz = gsend.shape[0]
    mz = lax.axis_index("tz")
    mq = lax.axis_index("tq")
    sp = lax.axis_index("space")
    mesh_id = pl.DeviceIdType.MESH

    def exchange(phase, src, dst, n, me, where):
        ssem, rsem = sems.at[2 * phase], sems.at[2 * phase + 1]

        def outgoing(d):
            return pltpu.make_async_remote_copy(
                src_ref=src.at[d], dst_ref=dst.at[me], send_sem=ssem.at[d], recv_sem=rsem.at[me],
                device_id=where(d), device_id_type=mesh_id,
            )

        def incoming(e):
            return pltpu.make_async_remote_copy(
                src_ref=src.at[e], dst_ref=dst.at[e], send_sem=ssem.at[e], recv_sem=rsem.at[e],
                device_id=where(e), device_id_type=mesh_id,
            )

        def start(k, carry):
            outgoing(lax.rem(me + k, n)).start()
            return carry

        lax.fori_loop(1, n, start, 0)
        dst[me] = src[me]

        def wait(k, carry):
            d = lax.rem(me + k, n)
            outgoing(d).wait_send()
            incoming(d).wait_recv()
            return carry

        lax.fori_loop(1, n, wait, 0)

    in_plane = lambda d: (mz, d, sp)
    across = lambda d: (d, mq, sp)
    if first:
        exchange(0, send_ref, recv1, nq, mq, in_plane)

    def group_step(s, carry):
        ga, gb = carry
        pa[s] = ga
        pb[s] = gb
        a = recv1[s, :, 0]
        return a * ga, a * gb + recv1[s, :, 1]

    ones = jnp.ones(pa.shape[1:], jnp.float32)
    ga, gb = lax.fori_loop(0, nq, group_step, (ones, jnp.zeros_like(ones)))
    c2 = gsend.shape[1]
    for z in range(nz):
        gsend[z, :, 0] = ga[z * c2:(z + 1) * c2]
        gsend[z, :, 1] = gb[z * c2:(z + 1) * c2]
    exchange(1, gsend, recv2, nz, mz, across)

    def entry_step(s, x):
        xg[s] = x
        return recv2[s, :, 0] * x + recv2[s, :, 1]

    lax.fori_loop(0, nz, entry_step, jnp.zeros(xg.shape[1:], jnp.float32))
    exchange(2, xg, back2, nz, mz, across)
    group_in = back2[...].reshape(pa.shape[1:])

    ssem, rsem = sems.at[6], sems.at[7]

    def back_copy(d, at):
        return pltpu.make_async_remote_copy(
            src_ref=xs.at[d], dst_ref=back1.at[at], send_sem=ssem.at[d], recv_sem=rsem.at[at],
            device_id=in_plane(d), device_id_type=mesh_id,
        )

    xs[mq] = pa[mq] * group_in + pb[mq]
    back1[mq] = xs[mq]

    def spread_step(k, carry):
        d = lax.rem(mq + k, nq)
        xs[d] = pa[d] * group_in + pb[d]
        back_copy(d, mq).start()
        return carry

    lax.fori_loop(1, nq, spread_step, 0)

    def spread_wait(k, carry):
        d = lax.rem(mq + k, nq)
        back_copy(d, mq).wait_send()
        back_copy(d, d).wait_recv()
        return carry

    lax.fori_loop(1, nq, spread_wait, 0)
    out_ref[...] = back1[...]


def whole_kernel(st_ref, dif_ref, frc_ref, keep_ref, cd_ref, shift_ref, x_ref,
                 buf, dbuf, fbuf, fsems, send, recv1, pa, pb, gsend, recv2, xg, back2, xs, back1, xsems):
    n = lax.axis_size("space")
    me = lax.axis_index("space")
    mz = lax.axis_index("tz")
    mq = lax.axis_index("tq")
    nq = lax.axis_size("tq")
    nz = lax.axis_size("tz")
    mesh_id = pl.DeviceIdType.MESH
    barrier = pltpu.get_barrier_semaphore()

    @pl.when(me > 0)
    def _():
        pl.semaphore_signal(barrier, 1, device_id=(mz, mq, me - 1), device_id_type=mesh_id)

    @pl.when(me < n - 1)
    def _():
        pl.semaphore_signal(barrier, 1, device_id=(mz, mq, me + 1), device_id_type=mesh_id)

    for k in range(1, nq):
        pl.semaphore_signal(
            barrier, 1, device_id=(mz, lax.rem(mq + k, nq), me), device_id_type=mesh_id
        )
    for k in range(1, nz):
        pl.semaphore_signal(
            barrier, 1, device_id=(lax.rem(mz + k, nz), mq, me), device_id_type=mesh_id
        )
    peers = nq + nz - 2

    @pl.when((me > 0) & (me < n - 1))
    def _():
        pl.semaphore_wait(barrier, peers + 2)

    @pl.when((me == 0) | (me == n - 1))
    def _():
        pl.semaphore_wait(barrier, peers + 1)

    def half_copy(h, d_src, d_dst, peer):
        return pltpu.make_async_remote_copy(
            src_ref=send.at[d_src, :, h], dst_ref=recv1.at[d_dst, :, h],
            send_sem=xsems.at[8 + 2 * h, d_src], recv_sem=xsems.at[9 + 2 * h, d_dst],
            device_id=(mz, peer, me), device_id_type=mesh_id,
        )

    def start_half(h):
        def start(k, carry):
            d = lax.rem(mq + k, nq)
            half_copy(h, d, mq, d).start()
            return carry

        lax.fori_loop(1, nq, start, 0)
        recv1[mq, :, h] = send[mq, :, h]

    def wait_half(h):
        def wait(k, carry):
            d = lax.rem(mq + k, nq)
            half_copy(h, d, mq, d).wait_send()
            half_copy(h, d, d, d).wait_recv()
            return carry

        lax.fori_loop(1, nq, wait, 0)

    anchor = (mz == 0) & (mq == 0)
    n_state, own, cols = cd_ref.shape
    comps = n_state // 2
    blocks = own // 8
    c1 = send.shape[1]
    for comp in range(comps):
        s0 = jnp.where(anchor, 0.0, cd_ref[comp])
        comp_scale = cd_ref[comps + comp] * s0
        for rb in range(blocks):
            for cb in range(cols // 128):
                p = (comp * blocks + rb) * (cols // 128) + cb
                rs, cs = slice(rb * 8, rb * 8 + 8), slice(cb * 128, cb * 128 + 128)
                send[p // c1, p % c1, 0] = comp_scale[rs, cs]
    start_half(0)
    fine_body(st_ref, dif_ref, frc_ref, keep_ref, cd_ref, send, shift_ref, buf, dbuf, fbuf, fsems)
    start_half(1)
    wait_half(0)
    wait_half(1)
    exchange_body(send, x_ref, recv1, pa, pb, gsend, recv2, xg, back2, xs, back1, xsems, first=False)


def from_tiles(tiles, shape):
    rows, cols = shape[0] * shape[1], shape[2]
    grid = tiles.reshape(rows // 8, cols // 128, 8, 128)
    return grid.transpose(0, 2, 1, 3).reshape(shape)


def per_device_body(coarse_points, coarse_decay, diffusion, forcing):
    slots, comps, row_count, col_count = coarse_points.shape
    space_count = lax.axis_size("space")
    me = lax.axis_index("space")


    state = coarse_points.reshape(slots * comps, row_count, col_count)
    ext_rows = row_count + 2 * HALO
    global_row = me * row_count - HALO + lax.broadcasted_iota(jnp.int32, (ext_rows, 1), 0)
    keep = ((global_row >= 0) & (global_row < space_count * row_count)).astype(jnp.float32)

    vmem = pl.BlockSpec(memory_space=pltpu.VMEM)
    tiles = slots * comps * row_count * col_count // (2 * 8 * 128)
    q_count = lax.axis_size("tq")
    z_count = lax.axis_size("tz")
    c1 = tiles // q_count
    c2 = c1 // z_count
    x1 = (q_count, c1, 8, 128)
    x2 = (z_count, c2, 8, 128)
    send_shape = (q_count, c1, 2, 8, 128)
    shifts, back = pl.pallas_call(
        whole_kernel,
        out_shape=(
            jax.ShapeDtypeStruct((slots * comps, row_count, col_count), jnp.float32),
            jax.ShapeDtypeStruct(x1, jnp.float32),
        ),
        in_specs=[vmem] * 5,
        out_specs=(vmem, vmem),
        scratch_shapes=[
            pltpu.VMEM((slots * comps, ext_rows, col_count), jnp.float32),
            pltpu.VMEM((ext_rows, col_count), jnp.float32),
            pltpu.VMEM((comps, ext_rows, col_count), jnp.float32),
            pltpu.SemaphoreType.DMA((12,)),
            pltpu.VMEM(send_shape, jnp.float32),
            pltpu.VMEM(send_shape, jnp.float32),
            pltpu.VMEM(x1, jnp.float32),
            pltpu.VMEM(x1, jnp.float32),
            pltpu.VMEM((z_count, c2, 2, 8, 128), jnp.float32),
            pltpu.VMEM((z_count, c2, 2, 8, 128), jnp.float32),
            pltpu.VMEM(x2, jnp.float32),
            pltpu.VMEM(x2, jnp.float32),
            pltpu.VMEM(x1, jnp.float32),
            pltpu.VMEM(x1, jnp.float32),
            pltpu.SemaphoreType.DMA((12, max(q_count, z_count))),
        ],
        compiler_params=pltpu.CompilerParams(collective_id=0, has_side_effects=True),
    )(state, diffusion, forcing, keep, coarse_decay.reshape(state.shape))
    scale = coarse_decay
    at_anchor = (lax.axis_index("tz") == 0) & (lax.axis_index("tq") == 0)
    scale0 = jnp.where(at_anchor, 0.0, coarse_decay[0])
    shifts = shifts.reshape(coarse_points.shape)
    shift0 = shifts[0]
    shift = shifts
    back = back.reshape(tiles, 8, 128)
    entering = from_tiles(back, (comps, row_count, col_count))

    first = scale0 * entering + shift0
    second = scale[1] * first + shift[1]
    return jnp.stack([first, second], axis=0)


def solution(mesh):
    tm_count = mesh.shape["tm"]
    q_count = 8 if tm_count >= 16 and tm_count % 8 == 0 else 2
    grid = mesh.devices.reshape(tm_count // q_count, q_count, mesh.shape["space"])
    mesh = jax.sharding.Mesh(grid, ("tz", "tq", "space"))
    time_axes = ("tz", "tq")
    placed = (
        P(time_axes, None, "space", None),
        P(time_axes, None, "space", None),
        P("space", None),
        P(None, "space", None),
    )
    return jax.shard_map(
        per_device_body,
        mesh=mesh,
        in_specs=placed,
        out_specs=P(time_axes, None, "space", None),
        check_vma=False,
    )
```

```python
import jax
import jax.numpy as jnp
from jax import lax
from jax.experimental import pallas as pl
from jax.experimental.pallas import tpu as pltpu
from jax.sharding import PartitionSpec as P

M = 16
HALO = M


def fine_body(st_ref, dif_ref, frc_ref, keep_ref, cd_ref, tiles_ref, shift_ref, buf, dbuf, fbuf, sems):
    n_state = st_ref.shape[0]
    own = st_ref.shape[1]
    cols = st_ref.shape[2]
    rows = own + 2 * HALO
    n = lax.axis_size("space")
    me = lax.axis_index("space")
    place = (lax.axis_index("tz"), lax.axis_index("tq"))
    mesh_id = pl.DeviceIdType.MESH
    pairs = ((st_ref, buf), (dif_ref, dbuf), (frc_ref, fbuf))

    def rim_copy(k, src, dst, down, target):
        if down:
            s_rows, d_rows = pl.ds(own - HALO, HALO), pl.ds(0, HALO)
        else:
            s_rows, d_rows = pl.ds(0, HALO), pl.ds(HALO + own, HALO)
        if src.ndim == 3:
            src_v, dst_v = src.at[:, s_rows], dst.at[:, d_rows]
        else:
            src_v, dst_v = src.at[s_rows], dst.at[d_rows]
        slot = k + (0 if down else 3)
        return pltpu.make_async_remote_copy(
            src_ref=src_v, dst_ref=dst_v, send_sem=sems.at[slot], recv_sem=sems.at[6 + slot],
            device_id=place + (target,), device_id_type=mesh_id,
        )

    @pl.when(me < n - 1)
    def _():
        for k, (src, dst) in enumerate(pairs):
            rim_copy(k, src, dst, True, me + 1).start()

    @pl.when(me > 0)
    def _():
        for k, (src, dst) in enumerate(pairs):
            rim_copy(k, src, dst, False, me - 1).start()

    global_row = me * own - HALO + lax.broadcasted_iota(jnp.int32, keep_ref.shape, 0)
    keep_ref[...] = jnp.where((global_row >= 0) & (global_row < n * own), 1.0, 0.0)
    buf[:, HALO:HALO + own] = st_ref[...]
    dbuf[HALO:HALO + own] = dif_ref[...]
    fbuf[:, HALO:HALO + own] = frc_ref[...]

    @pl.when(me == 0)
    def _():
        buf[:, :HALO] = jnp.zeros((n_state, HALO, cols), jnp.float32)
        dbuf[:HALO] = jnp.zeros((HALO, cols), jnp.float32)
        fbuf[:, :HALO] = jnp.zeros((fbuf.shape[0], HALO, cols), jnp.float32)

    @pl.when(me == n - 1)
    def _():
        buf[:, HALO + own:] = jnp.zeros((n_state, HALO, cols), jnp.float32)
        dbuf[HALO + own:] = jnp.zeros((HALO, cols), jnp.float32)
        fbuf[:, HALO + own:] = jnp.zeros((fbuf.shape[0], HALO, cols), jnp.float32)

    @pl.when(me < n - 1)
    def _():
        for k, (src, dst) in enumerate(pairs):
            rim_copy(k, src, dst, True, me + 1).wait_send()
            rim_copy(k, src, dst, False, me + 1).wait_recv()

    @pl.when(me > 0)
    def _():
        for k, (src, dst) in enumerate(pairs):
            rim_copy(k, src, dst, False, me - 1).wait_send()
            rim_copy(k, src, dst, True, me - 1).wait_recv()

    def make_step(lo, hi):
        span = hi - lo

        def one_step(counter, carry):
            dif = dbuf[lo:hi]
            keep = keep_ref[lo:hi, 0:1] > 0.5
            for slot in range(2):
                u = buf[2 * slot, lo:hi]
                v = buf[2 * slot + 1, lo:hi]
                new = []
                for comp, c in enumerate((u, v)):
                    next_row = pltpu.roll(c, span - 1, 0)
                    prev_row = pltpu.roll(c, 1, 0)
                    next_col = pltpu.roll(c, cols - 1, 1)
                    prev_col = pltpu.roll(c, 1, 1)
                    value = (
                        c
                        + dif * (next_row + prev_row + next_col + prev_col - 4.0 * c)
                        - 0.05 * (u * (next_row - prev_row) + v * (next_col - prev_col))
                        + 0.05 * fbuf[comp, lo:hi]
                    )
                    new.append(jnp.where(keep, value, 0.0))
                buf[2 * slot, lo:hi] = new[0]
                buf[2 * slot + 1, lo:hi] = new[1]
            return carry

        return one_step

    half = M // 2
    lax.fori_loop(0, half, make_step(0, rows), 0)
    lax.fori_loop(0, M - half, make_step(half, rows - half), 0)
    anchor = (lax.axis_index("tz") == 0) & (lax.axis_index("tq") == 0)
    comps = n_state // 2
    blocks = own // 8
    for comp in range(comps):
        d0, d1 = cd_ref[comp], cd_ref[comps + comp]
        c0, c1 = st_ref[comp], st_ref[comps + comp]
        plain0 = buf[comp, HALO:HALO + own] - d0 * c0
        sh1 = buf[comps + comp, HALO:HALO + own] - d1 * c1
        sh0 = jnp.where(anchor, d0 * c0 + plain0, plain0)
        shift_ref[comp] = sh0
        shift_ref[comps + comp] = sh1
        comp_shift = d1 * sh0 + sh1
        for rb in range(blocks):
            for cb in range(cols // 128):
                p = (comp * blocks + rb) * (cols // 128) + cb
                rs, cs = slice(rb * 8, rb * 8 + 8), slice(cb * 128, cb * 128 + 128)
                c1 = tiles_ref.shape[1]
                tiles_ref[p // c1, p % c1, 1] = comp_shift[rs, cs]


def exchange_body(send_ref, out_ref, recv1, pa, pb, gsend, recv2, xg, back2, xs, back1, sems, first=True):
    nq = send_ref.shape[0]
    nz = gsend.shape[0]
    mz = lax.axis_index("tz")
    mq = lax.axis_index("tq")
    sp = lax.axis_index("space")
    mesh_id = pl.DeviceIdType.MESH

    def exchange(phase, src, dst, n, me, where):
        ssem, rsem = sems.at[2 * phase], sems.at[2 * phase + 1]

        def outgoing(d):
            return pltpu.make_async_remote_copy(
                src_ref=src.at[d], dst_ref=dst.at[me], send_sem=ssem.at[d], recv_sem=rsem.at[me],
                device_id=where(d), device_id_type=mesh_id,
            )

        def incoming(e):
            return pltpu.make_async_remote_copy(
                src_ref=src.at[e], dst_ref=dst.at[e], send_sem=ssem.at[e], recv_sem=rsem.at[e],
                device_id=where(e), device_id_type=mesh_id,
            )

        def start(k, carry):
            outgoing(lax.rem(me + k, n)).start()
            return carry

        lax.fori_loop(1, n, start, 0)
        dst[me] = src[me]

        def wait(k, carry):
            d = lax.rem(me + k, n)
            outgoing(d).wait_send()
            incoming(d).wait_recv()
            return carry

        lax.fori_loop(1, n, wait, 0)

    in_plane = lambda d: (mz, d, sp)
    across = lambda d: (d, mq, sp)
    if first:
        exchange(0, send_ref, recv1, nq, mq, in_plane)

    def group_step(s, carry):
        ga, gb = carry
        pa[s] = ga
        pb[s] = gb
        a = recv1[s, :, 0]
        return a * ga, a * gb + recv1[s, :, 1]

    ones = jnp.ones(pa.shape[1:], jnp.float32)
    ga, gb = lax.fori_loop(0, nq, group_step, (ones, jnp.zeros_like(ones)))
    c2 = gsend.shape[1]
    for z in range(nz):
        gsend[z, :, 0] = ga[z * c2:(z + 1) * c2]
        gsend[z, :, 1] = gb[z * c2:(z + 1) * c2]
    exchange(1, gsend, recv2, nz, mz, across)

    def entry_step(s, x):
        xg[s] = x
        return recv2[s, :, 0] * x + recv2[s, :, 1]

    lax.fori_loop(0, nz, entry_step, jnp.zeros(xg.shape[1:], jnp.float32))
    exchange(2, xg, back2, nz, mz, across)
    group_in = back2[...].reshape(pa.shape[1:])

    def spread_step(s, carry):
        xs[s] = pa[s] * group_in + pb[s]
        return carry

    lax.fori_loop(0, nq, spread_step, 0)
    exchange(3, xs, back1, nq, mq, in_plane)
    out_ref[...] = back1[...]


def whole_kernel(st_ref, dif_ref, frc_ref, cd_ref, shift_ref, x_ref,
                 buf, dbuf, fbuf, fsems, keep_ref, send, recv1, pa, pb, gsend, recv2, xg, back2, xs, back1, xsems):
    n = lax.axis_size("space")
    me = lax.axis_index("space")
    mz = lax.axis_index("tz")
    mq = lax.axis_index("tq")
    nq = lax.axis_size("tq")
    nz = lax.axis_size("tz")
    mesh_id = pl.DeviceIdType.MESH
    barrier = pltpu.get_barrier_semaphore()

    @pl.when(me > 0)
    def _():
        pl.semaphore_signal(barrier, 1, device_id=(mz, mq, me - 1), device_id_type=mesh_id)

    @pl.when(me < n - 1)
    def _():
        pl.semaphore_signal(barrier, 1, device_id=(mz, mq, me + 1), device_id_type=mesh_id)

    for k in range(1, nq):
        pl.semaphore_signal(
            barrier, 1, device_id=(mz, lax.rem(mq + k, nq), me), device_id_type=mesh_id
        )
    for k in range(1, nz):
        pl.semaphore_signal(
            barrier, 1, device_id=(lax.rem(mz + k, nz), mq, me), device_id_type=mesh_id
        )
    peers = nq + nz - 2

    @pl.when((me > 0) & (me < n - 1))
    def _():
        pl.semaphore_wait(barrier, peers + 2)

    @pl.when((me == 0) | (me == n - 1))
    def _():
        pl.semaphore_wait(barrier, peers + 1)

    def half_copy(h, d_src, d_dst, peer):
        return pltpu.make_async_remote_copy(
            src_ref=send.at[d_src, :, h], dst_ref=recv1.at[d_dst, :, h],
            send_sem=xsems.at[8 + 2 * h, d_src], recv_sem=xsems.at[9 + 2 * h, d_dst],
            device_id=(mz, peer, me), device_id_type=mesh_id,
        )

    def start_half(h):
        def start(k, carry):
            d = lax.rem(mq + k, nq)
            half_copy(h, d, mq, d).start()
            return carry

        lax.fori_loop(1, nq, start, 0)
        recv1[mq, :, h] = send[mq, :, h]

    def wait_half(h):
        def wait(k, carry):
            d = lax.rem(mq + k, nq)
            half_copy(h, d, mq, d).wait_send()
            half_copy(h, d, d, d).wait_recv()
            return carry

        lax.fori_loop(1, nq, wait, 0)

    anchor = (mz == 0) & (mq == 0)
    n_state, own, cols = cd_ref.shape
    comps = n_state // 2
    blocks = own // 8
    c1 = send.shape[1]
    for comp in range(comps):
        s0 = jnp.where(anchor, 0.0, cd_ref[comp])
        comp_scale = cd_ref[comps + comp] * s0
        for rb in range(blocks):
            for cb in range(cols // 128):
                p = (comp * blocks + rb) * (cols // 128) + cb
                rs, cs = slice(rb * 8, rb * 8 + 8), slice(cb * 128, cb * 128 + 128)
                send[p // c1, p % c1, 0] = comp_scale[rs, cs]
    start_half(0)
    fine_body(st_ref, dif_ref, frc_ref, keep_ref, cd_ref, send, shift_ref, buf, dbuf, fbuf, fsems)
    start_half(1)
    wait_half(0)
    wait_half(1)
    exchange_body(send, x_ref, recv1, pa, pb, gsend, recv2, xg, back2, xs, back1, xsems, first=False)


def from_tiles(tiles, shape):
    rows, cols = shape[0] * shape[1], shape[2]
    grid = tiles.reshape(rows // 8, cols // 128, 8, 128)
    return grid.transpose(0, 2, 1, 3).reshape(shape)


def per_device_body(coarse_points, coarse_decay, diffusion, forcing):
    slots, comps, row_count, col_count = coarse_points.shape


    state = coarse_points.reshape(slots * comps, row_count, col_count)
    ext_rows = row_count + 2 * HALO

    vmem = pl.BlockSpec(memory_space=pltpu.VMEM)
    tiles = slots * comps * row_count * col_count // (2 * 8 * 128)
    q_count = lax.axis_size("tq")
    z_count = lax.axis_size("tz")
    c1 = tiles // q_count
    c2 = c1 // z_count
    x1 = (q_count, c1, 8, 128)
    x2 = (z_count, c2, 8, 128)
    send_shape = (q_count, c1, 2, 8, 128)
    shifts, back = pl.pallas_call(
        whole_kernel,
        out_shape=(
            jax.ShapeDtypeStruct((slots * comps, row_count, col_count), jnp.float32),
            jax.ShapeDtypeStruct(x1, jnp.float32),
        ),
        in_specs=[vmem] * 4,
        out_specs=(vmem, vmem),
        scratch_shapes=[
            pltpu.VMEM((slots * comps, ext_rows, col_count), jnp.float32),
            pltpu.VMEM((ext_rows, col_count), jnp.float32),
            pltpu.VMEM((comps, ext_rows, col_count), jnp.float32),
            pltpu.SemaphoreType.DMA((12,)),
            pltpu.VMEM((ext_rows, 128), jnp.float32),
            pltpu.VMEM(send_shape, jnp.float32),
            pltpu.VMEM(send_shape, jnp.float32),
            pltpu.VMEM(x1, jnp.float32),
            pltpu.VMEM(x1, jnp.float32),
            pltpu.VMEM((z_count, c2, 2, 8, 128), jnp.float32),
            pltpu.VMEM((z_count, c2, 2, 8, 128), jnp.float32),
            pltpu.VMEM(x2, jnp.float32),
            pltpu.VMEM(x2, jnp.float32),
            pltpu.VMEM(x1, jnp.float32),
            pltpu.VMEM(x1, jnp.float32),
            pltpu.SemaphoreType.DMA((12, max(q_count, z_count))),
        ],
        compiler_params=pltpu.CompilerParams(collective_id=0, has_side_effects=True),
    )(state, diffusion, forcing, coarse_decay.reshape(state.shape))
    scale = coarse_decay
    at_anchor = (lax.axis_index("tz") == 0) & (lax.axis_index("tq") == 0)
    scale0 = jnp.where(at_anchor, 0.0, coarse_decay[0])
    shifts = shifts.reshape(coarse_points.shape)
    shift0 = shifts[0]
    shift = shifts
    back = back.reshape(tiles, 8, 128)
    entering = from_tiles(back, (comps, row_count, col_count))

    first = scale0 * entering + shift0
    second = scale[1] * first + shift[1]
    return jnp.stack([first, second], axis=0)


def solution(mesh):
    tm_count = mesh.shape["tm"]
    q_count = 8 if tm_count >= 16 and tm_count % 8 == 0 else 2
    grid = mesh.devices.reshape(tm_count // q_count, q_count, mesh.shape["space"])
    mesh = jax.sharding.Mesh(grid, ("tz", "tq", "space"))
    time_axes = ("tz", "tq")
    placed = (
        P(time_axes, None, "space", None),
        P(time_axes, None, "space", None),
        P("space", None),
        P(None, "space", None),
    )
    return jax.shard_map(
        per_device_body,
        mesh=mesh,
        in_specs=placed,
        out_specs=P(time_axes, None, "space", None),
        check_vma=False,
    )
```

```python
import jax
import jax.numpy as jnp
from jax import lax
from jax.experimental import pallas as pl
from jax.experimental.pallas import tpu as pltpu
from jax.sharding import PartitionSpec as P

M = 16
HALO = M


def fine_body(st_ref, dif_ref, frc_ref, keep_ref, cd_ref, tiles_ref, shift_ref, buf, dbuf, fbuf, sems):
    n_state = st_ref.shape[0]
    own = st_ref.shape[1]
    cols = st_ref.shape[2]
    rows = own + 2 * HALO
    n = lax.axis_size("space")
    me = lax.axis_index("space")
    place = (lax.axis_index("tz"), lax.axis_index("tq"))
    mesh_id = pl.DeviceIdType.MESH
    pairs = ((st_ref, buf), (dif_ref, dbuf), (frc_ref, fbuf))

    def rim_copy(k, src, dst, down, target):
        if down:
            s_rows, d_rows = pl.ds(own - HALO, HALO), pl.ds(0, HALO)
        else:
            s_rows, d_rows = pl.ds(0, HALO), pl.ds(HALO + own, HALO)
        if src.ndim == 3:
            src_v, dst_v = src.at[:, s_rows], dst.at[:, d_rows]
        else:
            src_v, dst_v = src.at[s_rows], dst.at[d_rows]
        slot = k + (0 if down else 3)
        return pltpu.make_async_remote_copy(
            src_ref=src_v, dst_ref=dst_v, send_sem=sems.at[slot], recv_sem=sems.at[6 + slot],
            device_id=place + (target,), device_id_type=mesh_id,
        )

    @pl.when(me < n - 1)
    def _():
        for k, (src, dst) in enumerate(pairs):
            rim_copy(k, src, dst, True, me + 1).start()

    @pl.when(me > 0)
    def _():
        for k, (src, dst) in enumerate(pairs):
            rim_copy(k, src, dst, False, me - 1).start()

    global_row = me * own - HALO + lax.broadcasted_iota(jnp.int32, keep_ref.shape, 0)
    keep_ref[...] = jnp.where((global_row >= 0) & (global_row < n * own), 1.0, 0.0)
    buf[:, HALO:HALO + own] = st_ref[...]
    dbuf[HALO:HALO + own] = dif_ref[...]
    fbuf[:, HALO:HALO + own] = frc_ref[...]

    @pl.when(me == 0)
    def _():
        buf[:, :HALO] = jnp.zeros((n_state, HALO, cols), jnp.float32)
        dbuf[:HALO] = jnp.zeros((HALO, cols), jnp.float32)
        fbuf[:, :HALO] = jnp.zeros((fbuf.shape[0], HALO, cols), jnp.float32)

    @pl.when(me == n - 1)
    def _():
        buf[:, HALO + own:] = jnp.zeros((n_state, HALO, cols), jnp.float32)
        dbuf[HALO + own:] = jnp.zeros((HALO, cols), jnp.float32)
        fbuf[:, HALO + own:] = jnp.zeros((fbuf.shape[0], HALO, cols), jnp.float32)

    @pl.when(me < n - 1)
    def _():
        for k, (src, dst) in enumerate(pairs):
            rim_copy(k, src, dst, True, me + 1).wait_send()
            rim_copy(k, src, dst, False, me + 1).wait_recv()

    @pl.when(me > 0)
    def _():
        for k, (src, dst) in enumerate(pairs):
            rim_copy(k, src, dst, False, me - 1).wait_send()
            rim_copy(k, src, dst, True, me - 1).wait_recv()

    def make_step(lo, hi):
        span = hi - lo

        def one_step(counter, carry):
            dif = dbuf[lo:hi]
            keep = keep_ref[lo:hi, 0:1] > 0.5
            for slot in range(2):
                u = buf[2 * slot, lo:hi]
                v = buf[2 * slot + 1, lo:hi]
                new = []
                for comp, c in enumerate((u, v)):
                    next_row = pltpu.roll(c, span - 1, 0)
                    prev_row = pltpu.roll(c, 1, 0)
                    next_col = pltpu.roll(c, cols - 1, 1)
                    prev_col = pltpu.roll(c, 1, 1)
                    value = (
                        c
                        + dif * (next_row + prev_row + next_col + prev_col - 4.0 * c)
                        - 0.05 * (u * (next_row - prev_row) + v * (next_col - prev_col))
                        + 0.05 * fbuf[comp, lo:hi]
                    )
                    new.append(jnp.where(keep, value, 0.0))
                buf[2 * slot, lo:hi] = new[0]
                buf[2 * slot + 1, lo:hi] = new[1]
            return carry

        return one_step

    half = M // 2
    lax.fori_loop(0, half, make_step(0, rows), 0)
    lax.fori_loop(0, M - half, make_step(half, rows - half), 0)
    anchor = (lax.axis_index("tz") == 0) & (lax.axis_index("tq") == 0)
    comps = n_state // 2
    blocks = own // 8
    for comp in range(comps):
        d0, d1 = cd_ref[comp], cd_ref[comps + comp]
        c0, c1 = st_ref[comp], st_ref[comps + comp]
        plain0 = buf[comp, HALO:HALO + own] - d0 * c0
        sh1 = buf[comps + comp, HALO:HALO + own] - d1 * c1
        sh0 = jnp.where(anchor, d0 * c0 + plain0, plain0)
        shift_ref[comp] = sh0
        shift_ref[comps + comp] = sh1
        comp_shift = d1 * sh0 + sh1
        for rb in range(blocks):
            for cb in range(cols // 128):
                p = (comp * blocks + rb) * (cols // 128) + cb
                rs, cs = slice(rb * 8, rb * 8 + 8), slice(cb * 128, cb * 128 + 128)
                c1 = tiles_ref.shape[1]
                tiles_ref[p // c1, p % c1, 1] = comp_shift[rs, cs]


def exchange_body(send_ref, out_ref, recv1, pa, pb, gsend, recv2, xg, back2, xs, back1, sems, first=True):
    nq = send_ref.shape[0]
    nz = gsend.shape[0]
    mz = lax.axis_index("tz")
    mq = lax.axis_index("tq")
    sp = lax.axis_index("space")
    mesh_id = pl.DeviceIdType.MESH

    def exchange(phase, src, dst, n, me, where):
        ssem, rsem = sems.at[2 * phase], sems.at[2 * phase + 1]

        def outgoing(d):
            return pltpu.make_async_remote_copy(
                src_ref=src.at[d], dst_ref=dst.at[me], send_sem=ssem.at[d], recv_sem=rsem.at[me],
                device_id=where(d), device_id_type=mesh_id,
            )

        def incoming(e):
            return pltpu.make_async_remote_copy(
                src_ref=src.at[e], dst_ref=dst.at[e], send_sem=ssem.at[e], recv_sem=rsem.at[e],
                device_id=where(e), device_id_type=mesh_id,
            )

        def start(k, carry):
            outgoing(lax.rem(me + k, n)).start()
            return carry

        lax.fori_loop(1, n, start, 0)
        dst[me] = src[me]

        def wait(k, carry):
            d = lax.rem(me + k, n)
            outgoing(d).wait_send()
            incoming(d).wait_recv()
            return carry

        lax.fori_loop(1, n, wait, 0)

    in_plane = lambda d: (mz, d, sp)
    across = lambda d: (d, mq, sp)
    if first:
        exchange(0, send_ref, recv1, nq, mq, in_plane)

    def group_step(s, carry):
        ga, gb = carry
        pa[s] = ga
        pb[s] = gb
        a = recv1[s, :, 0]
        return a * ga, a * gb + recv1[s, :, 1]

    ones = jnp.ones(pa.shape[1:], jnp.float32)
    ga, gb = lax.fori_loop(0, nq, group_step, (ones, jnp.zeros_like(ones)))
    c2 = gsend.shape[1]
    for z in range(nz):
        gsend[z, :, 0] = ga[z * c2:(z + 1) * c2]
        gsend[z, :, 1] = gb[z * c2:(z + 1) * c2]
    exchange(1, gsend, recv2, nz, mz, across)

    def entry_step(s, x):
        xg[s] = x
        return recv2[s, :, 0] * x + recv2[s, :, 1]

    lax.fori_loop(0, nz, entry_step, jnp.zeros(xg.shape[1:], jnp.float32))
    exchange(2, xg, back2, nz, mz, across)
    group_in = back2[...].reshape(pa.shape[1:])

    def spread_step(s, carry):
        xs[s] = pa[s] * group_in + pb[s]
        return carry

    lax.fori_loop(0, nq, spread_step, 0)
    exchange(3, xs, back1, nq, mq, in_plane)
    n_comp, own, cols = out_ref.shape
    blocks = own // 8
    c1 = back1.shape[1]
    for comp in range(n_comp):
        for rb in range(blocks):
            for cb in range(cols // 128):
                p = (comp * blocks + rb) * (cols // 128) + cb
                out_ref[comp, rb * 8:rb * 8 + 8, cb * 128:cb * 128 + 128] = back1[p // c1, p % c1]


def whole_kernel(st_ref, dif_ref, frc_ref, cd_ref, shift_ref, x_ref,
                 buf, dbuf, fbuf, fsems, keep_ref, send, recv1, pa, pb, gsend, recv2, xg, back2, xs, back1, xsems):
    n = lax.axis_size("space")
    me = lax.axis_index("space")
    mz = lax.axis_index("tz")
    mq = lax.axis_index("tq")
    nq = lax.axis_size("tq")
    nz = lax.axis_size("tz")
    mesh_id = pl.DeviceIdType.MESH
    barrier = pltpu.get_barrier_semaphore()

    @pl.when(me > 0)
    def _():
        pl.semaphore_signal(barrier, 1, device_id=(mz, mq, me - 1), device_id_type=mesh_id)

    @pl.when(me < n - 1)
    def _():
        pl.semaphore_signal(barrier, 1, device_id=(mz, mq, me + 1), device_id_type=mesh_id)

    for k in range(1, nq):
        pl.semaphore_signal(
            barrier, 1, device_id=(mz, lax.rem(mq + k, nq), me), device_id_type=mesh_id
        )
    for k in range(1, nz):
        pl.semaphore_signal(
            barrier, 1, device_id=(lax.rem(mz + k, nz), mq, me), device_id_type=mesh_id
        )
    peers = nq + nz - 2

    @pl.when((me > 0) & (me < n - 1))
    def _():
        pl.semaphore_wait(barrier, peers + 2)

    @pl.when((me == 0) | (me == n - 1))
    def _():
        pl.semaphore_wait(barrier, peers + 1)

    def half_copy(h, d_src, d_dst, peer):
        return pltpu.make_async_remote_copy(
            src_ref=send.at[d_src, :, h], dst_ref=recv1.at[d_dst, :, h],
            send_sem=xsems.at[8 + 2 * h, d_src], recv_sem=xsems.at[9 + 2 * h, d_dst],
            device_id=(mz, peer, me), device_id_type=mesh_id,
        )

    def start_half(h):
        def start(k, carry):
            d = lax.rem(mq + k, nq)
            half_copy(h, d, mq, d).start()
            return carry

        lax.fori_loop(1, nq, start, 0)
        recv1[mq, :, h] = send[mq, :, h]

    def wait_half(h):
        def wait(k, carry):
            d = lax.rem(mq + k, nq)
            half_copy(h, d, mq, d).wait_send()
            half_copy(h, d, d, d).wait_recv()
            return carry

        lax.fori_loop(1, nq, wait, 0)

    anchor = (mz == 0) & (mq == 0)
    n_state, own, cols = cd_ref.shape
    comps = n_state // 2
    blocks = own // 8
    c1 = send.shape[1]
    for comp in range(comps):
        s0 = jnp.where(anchor, 0.0, cd_ref[comp])
        comp_scale = cd_ref[comps + comp] * s0
        for rb in range(blocks):
            for cb in range(cols // 128):
                p = (comp * blocks + rb) * (cols // 128) + cb
                rs, cs = slice(rb * 8, rb * 8 + 8), slice(cb * 128, cb * 128 + 128)
                send[p // c1, p % c1, 0] = comp_scale[rs, cs]
    start_half(0)
    fine_body(st_ref, dif_ref, frc_ref, keep_ref, cd_ref, send, shift_ref, buf, dbuf, fbuf, fsems)
    start_half(1)
    wait_half(0)
    wait_half(1)
    exchange_body(send, x_ref, recv1, pa, pb, gsend, recv2, xg, back2, xs, back1, xsems, first=False)


def per_device_body(coarse_points, coarse_decay, diffusion, forcing):
    slots, comps, row_count, col_count = coarse_points.shape


    state = coarse_points.reshape(slots * comps, row_count, col_count)
    ext_rows = row_count + 2 * HALO

    vmem = pl.BlockSpec(memory_space=pltpu.VMEM)
    tiles = slots * comps * row_count * col_count // (2 * 8 * 128)
    q_count = lax.axis_size("tq")
    z_count = lax.axis_size("tz")
    c1 = tiles // q_count
    c2 = c1 // z_count
    x1 = (q_count, c1, 8, 128)
    x2 = (z_count, c2, 8, 128)
    send_shape = (q_count, c1, 2, 8, 128)
    shifts, back = pl.pallas_call(
        whole_kernel,
        out_shape=(
            jax.ShapeDtypeStruct((slots * comps, row_count, col_count), jnp.float32),
            jax.ShapeDtypeStruct((comps, row_count, col_count), jnp.float32),
        ),
        in_specs=[vmem] * 4,
        out_specs=(vmem, vmem),
        scratch_shapes=[
            pltpu.VMEM((slots * comps, ext_rows, col_count), jnp.float32),
            pltpu.VMEM((ext_rows, col_count), jnp.float32),
            pltpu.VMEM((comps, ext_rows, col_count), jnp.float32),
            pltpu.SemaphoreType.DMA((12,)),
            pltpu.VMEM((ext_rows, 128), jnp.float32),
            pltpu.VMEM(send_shape, jnp.float32),
            pltpu.VMEM(send_shape, jnp.float32),
            pltpu.VMEM(x1, jnp.float32),
            pltpu.VMEM(x1, jnp.float32),
            pltpu.VMEM((z_count, c2, 2, 8, 128), jnp.float32),
            pltpu.VMEM((z_count, c2, 2, 8, 128), jnp.float32),
            pltpu.VMEM(x2, jnp.float32),
            pltpu.VMEM(x2, jnp.float32),
            pltpu.VMEM(x1, jnp.float32),
            pltpu.VMEM(x1, jnp.float32),
            pltpu.SemaphoreType.DMA((12, max(q_count, z_count))),
        ],
        compiler_params=pltpu.CompilerParams(collective_id=0, has_side_effects=True),
    )(state, diffusion, forcing, coarse_decay.reshape(state.shape))
    scale = coarse_decay
    at_anchor = (lax.axis_index("tz") == 0) & (lax.axis_index("tq") == 0)
    scale0 = jnp.where(at_anchor, 0.0, coarse_decay[0])
    shifts = shifts.reshape(coarse_points.shape)
    shift0 = shifts[0]
    shift = shifts
    entering = back

    first = scale0 * entering + shift0
    second = scale[1] * first + shift[1]
    return jnp.stack([first, second], axis=0)


def solution(mesh):
    tm_count = mesh.shape["tm"]
    q_count = 8 if tm_count >= 16 and tm_count % 8 == 0 else 2
    grid = mesh.devices.reshape(tm_count // q_count, q_count, mesh.shape["space"])
    mesh = jax.sharding.Mesh(grid, ("tz", "tq", "space"))
    time_axes = ("tz", "tq")
    placed = (
        P(time_axes, None, "space", None),
        P(time_axes, None, "space", None),
        P("space", None),
        P(None, "space", None),
    )
    return jax.shard_map(
        per_device_body,
        mesh=mesh,
        in_specs=placed,
        out_specs=P(time_axes, None, "space", None),
        check_vma=False,
    )
```
